32 devices in a mesh: tm: 4 (over x, core), fibre: 8 (over z, y).
Axes of the slice: x: 2, y: 2, z: 4, core: 2. Of those that a mesh axis runs over, the one named last changes fastest.
Arguments:
- signal: float32 [64, 64, 1024], P(None, 'fibre', 'tm'), may hold values from -6 to 6
- first_kernel_weight: float32 [3, 3, 128, 64], replicated, may hold values from -0.25 to 0.25
- first_layer_bias: float32 [128], replicated, may hold values from -1 to 1
- first_residual_matrix: float32 [64, 64], replicated, may hold values from -0.75 to 0.75
- second_kernel_weight: float32 [3, 3, 128, 64], replicated, may hold values from -0.25 to 0.25
- second_layer_bias: float32 [128], replicated, may hold values from -1 to 1
- second_residual_matrix: float32 [64, 64], replicated, may hold values from -0.75 to 0.75
Outputs:
- features: float32 [64, 64, 1024], P(None, 'fibre', 'tm')
The draws below stay inside these ranges and needn't reach their ends.
All inputs are finite; a program needn't handle non-finite values.
Results may differ from the reference program's by a relative error of at most 0.0001.
Values sent between devices are 32-bit elements; how exact they have to be, the bound alone decides.
A program may use at most 64 MiB of HBM per device.

```python
import jax
import jax.numpy as jnp
from jax import lax

CH = 64
DILATION_ONE = 128
DILATION_TWO = 256
FIB_DEV = 8
FIBRES = 64
TIME = 1024


def level_of(stream_key, dims, cuts, least, top_value):
    level = 1.0
    for position, shards_of in cuts:
        heights = jax.random.uniform(jax.random.fold_in(jax.random.fold_in(stream_key, 6), position), (shards_of,), jnp.float32, least / len(cuts), top_value / len(cuts))
        level = level * jnp.repeat(jnp.exp(heights), dims[position] // shards_of).reshape((-1,) + (1,) * (len(dims) - 1 - position))
    return level


def bell_draw(key, dims, scale, most, split=(), kind=jnp.bfloat16):
    values = jax.random.normal(key, dims, jnp.float32) * scale
    if len(split) > 0:
        values = level_of(key, dims, split, -0.22, 0.18) * values
    return jnp.clip(values, min=-most, max=most).astype(kind)


def setup_inputs(seed: int = 0) -> dict:
    arg_keys = jax.random.split(jax.random.key(seed), 8)
    return {
        "signal": bell_draw(arg_keys[0], (CH, FIBRES, TIME), 1.0, 6.0, ((1, 8), (2, 4)), jnp.float32),
        "first_kernel_weight": bell_draw(arg_keys[1], (3, 3, 2 * CH, CH), (9 * CH) ** -0.5, 0.25, (), jnp.float32),
        "first_layer_bias": jnp.clip(jax.random.uniform(arg_keys[2], (2 * CH,), jnp.float32, -1.0, 1.0), -1.0, 1.0),
        "first_residual_matrix": bell_draw(arg_keys[3], (CH, CH), CH ** -0.5, 0.75, (), jnp.float32),
        "second_kernel_weight": bell_draw(arg_keys[4], (3, 3, 2 * CH, CH), (9 * CH) ** -0.5, 0.25, (), jnp.float32),
        "second_layer_bias": jnp.clip(jax.random.uniform(arg_keys[5], (2 * CH,), jnp.float32, -1.0, 1.0), -1.0, 1.0),
        "second_residual_matrix": bell_draw(arg_keys[6], (CH, CH), CH ** -0.5, 0.75, (), jnp.float32),
    }


def apply_gated_layer(widened_input, weight, bias, mixing, dilation):
    fibre_out = widened_input.shape[1] - 2
    time_out = widened_input.shape[2] - 2 * dilation
    preact = jnp.zeros((weight.shape[2], fibre_out, time_out), jnp.float32) + bias[:, None, None]
    for across in range(3):
        for along in range(3):
            offset = 2 * dilation - along * dilation
            window = widened_input[:, across:across + fibre_out, offset:offset + time_out]
            preact = preact + jnp.einsum("oc,cft->oft", weight[across, along], window, precision=lax.Precision.HIGHEST)
    channels = mixing.shape[0]
    gated = jnp.tanh(preact[:channels]) * jax.nn.sigmoid(preact[channels:])
    return widened_input[:, 1:-1, 2 * dilation:] + jnp.einsum("oc,cft->oft", mixing, gated, precision=lax.Precision.HIGHEST)


def complete_layer_output(field, weight, bias, mixing, dilation):
    padded = jnp.pad(field, ((0, 0), (1, 1), (2 * dilation, 0)))
    block_count = field.shape[1] // FIB_DEV

    def one_block(block_index):
        widened_input = lax.dynamic_slice_in_dim(padded, block_index * FIB_DEV, FIB_DEV + 2, 1)
        return apply_gated_layer(widened_input, weight, bias, mixing, dilation)

    blocks = lax.map(one_block, jnp.arange(block_count, dtype=jnp.int32))
    return jnp.transpose(blocks, (1, 0, 2, 3)).reshape(field.shape)


def reference(signal, first_kernel_weight, first_layer_bias, first_residual_matrix, second_kernel_weight, second_layer_bias, second_residual_matrix):
    between_layers = complete_layer_output(signal, first_kernel_weight, first_layer_bias, first_residual_matrix, DILATION_ONE)
    return complete_layer_output(between_layers, second_kernel_weight, second_layer_bias, second_residual_matrix, DILATION_TWO)
```

```python
import jax
import jax.numpy as jnp
from jax import lax
from jax.experimental import pallas as pl
from jax.experimental.pallas import tpu as pltpu
from jax.sharding import PartitionSpec as P

DILATION_ONE = 128
DILATION_TWO = 256
BF = jnp.bfloat16
F32 = jnp.float32


def split(value):
    hi = value.astype(BF)
    return hi, (value - hi.astype(F32)).astype(BF)


def thirds(value):
    hi, lo = split(value)
    return [hi, lo, hi]


def pick(i, values):
    out = jnp.int32(values[-1])
    for n in range(len(values) - 2, -1, -1):
        out = jnp.where(i == n, jnp.int32(values[n]), out)
    return out


def kernel(
    nt, nf, fib,
    x_hbm, w1_hbm, b1_hbm, r1_hbm, w2_hbm, b2_hbm, r2_hbm, out_ref,
    s, m, xv, w1, b1, r1, w2, b2, r2, l1, l2, q1, q2, c1, c2, acc, acc2,
    in_sem, w_sem, h0s, h0r, h2s, h2r, xs, xr, ps, pr, ts, tr, ms, mr, es, er,
):
    T = lax.axis_index("tm")
    F = lax.axis_index("fibre")
    odd = lax.rem(T, 2)
    even = odd == 0
    isodd = odd == 1
    late = T >= 2
    partner = T + 1 - 2 * odd
    ch, length = s.shape[2], s.shape[3] // 2
    own = fib // 2
    wide = own + 2
    mid = own + 1
    out_ch = 2 * ch
    far = nt > 4
    up, down = F + 1 < nf, F > 0
    arrive = [1, own] + list(range(2, own))
    order = arrive + [0, own + 1]
    order2 = list(range(1, own)) + [0, own]

    def dev(t, f):
        return {"tm": t, "fibre": f}

    load = pltpu.make_async_copy(x_hbm, xv, in_sem.at[0])
    load.start()
    weights = [
        pltpu.make_async_copy(a, b, w_sem.at[i])
        for i, (a, b) in enumerate(
            [(w1_hbm, w1), (b1_hbm, b1), (r1_hbm, r1), (w2_hbm, w2), (b2_hbm, b2), (r2_hbm, r2)]
        )
    ]
    for c in weights:
        c.start()

    barrier = pltpu.get_barrier_semaphore()
    friends = [(partner, F, None), (T, F + 1, up), (T, F - 1, down), (T + 2, F, T + 2 < nt), (T - 2, F, late)]
    if far:
        send3 = isodd & (T + 3 < nt)
        recv3 = even & (T >= 4)
        for e, ok in ((0, None), (1, up), (-1, down)):
            for d, okt in ((3, send3), (-3, recv3)):
                friends.append((T + d, F + e, okt if ok is None else okt & ok))
    count = jnp.int32(0)
    for t, f, ok in friends:
        if ok is None:
            pl.semaphore_signal(barrier, inc=1, device_id=dev(t, f), device_id_type=pl.DeviceIdType.MESH)
            count = count + 1
        else:
            @pl.when(ok)
            def _(t=t, f=f):
                pl.semaphore_signal(barrier, inc=1, device_id=dev(t, f), device_id_type=pl.DeviceIdType.MESH)
            count = count + ok.astype(jnp.int32)

    load.wait()
    for f in range(fib):
        for c in range(0, length, 128):
            s[0, 1 + f // 2, :, pl.ds((f % 2) * length + c, 128)] = xv[pl.ds(c // 128 * fib + f, ch, stride=fib * length // 128), :]
    pl.semaphore_wait(barrier, count)

    def remote(src, dst, ssem, rsem, t, f):
        return pltpu.make_async_remote_copy(
            src_ref=src, dst_ref=dst, send_sem=ssem, recv_sem=rsem,
            device_id=dev(t, f), device_id_type=pl.DeviceIdType.MESH,
        )

    def halo_up(j, ss, rr):
        return remote(s.at[j, own], s.at[j, 0], ss.at[0], rr.at[0], T, F + 1)

    def halo_down(j, ss, rr):
        return remote(s.at[j, 1], s.at[j, own + 1], ss.at[1], rr.at[1], T, F - 1)

    def cross(q):
        return remote(s.at[0, q], s.at[2, q], xs.at[q], xr.at[q], T + 2, F)

    @pl.when(up)
    def _():
        halo_up(0, h0s, h0r).start()

    @pl.when(down)
    def _():
        halo_down(0, h0s, h0r).start()

    @pl.when(T + 2 < nt)
    def _():
        for q in arrive:
            cross(q).start()

    def part(src, q):
        return remote(s.at[src, q], s.at[1, q], ps.at[q], pr.at[q], partner, F)

    def part3(q):
        return remote(s.at[2, q], s.at[3, q], ts.at[q], tr.at[q], partner, F)

    def share(src, r):
        return remote(m.at[src, r], m.at[1, r], ms.at[r], mr.at[r], partner, F)

    @pl.when(even)
    def _():
        for q in arrive:
            part(0, q).start()

    if far:
        def third(i, e):
            if e == 0:
                src, dst = s.at[0, pl.ds(1, own)], s.at[3, pl.ds(1, own)]
            elif e == 1:
                src, dst = s.at[0, own], s.at[3, 0]
            else:
                src, dst = s.at[0, 1], s.at[3, own + 1]
            return remote(src, dst, es.at[i], er.at[i], T + 3, F + e)

        thirds_list = [(0, 0, None, None), (1, 1, up, down), (2, -1, down, up)]
        for i, e, ok, _ok in thirds_list:
            @pl.when(send3 if ok is None else send3 & ok)
            def _(i=i, e=e):
                third(i, e).start()

    zero = jnp.zeros(s.shape[2:], F32)

    def zero_halo(j):
        @pl.when(jnp.logical_not(down))
        def _():
            s[j, 0] = zero

        @pl.when(jnp.logical_not(up))
        def _():
            s[j, own + 1] = zero

    zero_halo(0)


    @pl.when(T == 0)
    def _():
        s[1] = jnp.zeros(s.shape[1:], F32)
        m[1] = jnp.zeros(m.shape[1:], F32)

    @pl.when(T < 2)
    def _():
        m[2] = jnp.zeros(m.shape[1:], F32)

    @pl.when(T == 2)
    def _():
        s[3] = jnp.zeros(s.shape[1:], F32)

    @pl.when(late)
    def _():
        zero_halo(2)

    if far:
        @pl.when(recv3)
        def _():
            zero_halo(3)

    for c in weights:
        c.wait()

    def prepare(w, left, r, mix, bias, tall):
        for a in range(3):
            for k in range(3):
                hi, lo = split(w[a, k].T)
                for i, piece in enumerate((hi, hi, lo)):
                    left[pl.ds(a * out_ch, out_ch), pl.ds((3 * k + i) * ch, ch)] = piece
        hi, lo = split(r[...])
        for i, piece in enumerate((hi, hi, lo)):
            mix[:, pl.ds(i * ch, ch)] = piece
        tall[...] = jnp.broadcast_to(bias[...], (out_ch, out_ch)).T

    prepare(w1, l1, r1, q1, b1, c1)
    acc[...] = jnp.zeros_like(acc)
    acc2[...] = jnp.zeros_like(acc2)

    @pl.when(down)
    def _():
        halo_up(0, h0s, h0r).wait_recv()

    @pl.when(up)
    def _():
        halo_down(0, h0s, h0r).wait_recv()

    @pl.when(even)
    def _():
        part(0, 0).start()
        part(0, own + 1).start()

    prepare(w2, l2, r2, q2, b2, c2)

    def push(low, high, left, pieces):
        p = jnp.dot(left[...], jnp.concatenate(pieces, axis=0), preferred_element_type=F32)
        p0, p1, p2 = p[:out_ch], p[out_ch:2 * out_ch], p[2 * out_ch:]
        n = length
        low[...] = low[...] + jnp.concatenate([p0[:, :n] + p1[:, n:], p0[:, n:]], axis=1)
        high[...] = high[...] + jnp.concatenate([p2[:, :n], p1[:, :n] + p2[:, n:]], axis=1)

    def gate(total, mix, tall, base):
        bias = tall[...]
        bias = jnp.concatenate([bias] * (total.shape[1] // bias.shape[1]), axis=1)
        pre = total + bias
        g = jnp.tanh(pre[:ch]) * (0.5 * jnp.tanh(0.5 * pre[ch:]) + 0.5)
        return base + jnp.dot(mix[...], jnp.concatenate(thirds(g), axis=0), preferred_element_type=F32)

    def straddle(ref, j, r):
        return jnp.concatenate([ref[j, r, :, length:], ref[j, r + 1, :, :length]], axis=1)

    def ready(i):
        return jnp.where(i < own, i - 1, jnp.where(i == own, 0, own))

    def twice(i):
        return i == own - 1

    def emit(slot, cur, r, dst):
        value = gate(acc[slot, r + 1], q1, c1, straddle(s, cur, r))
        row = F * fib + 2 * r - 1
        lo = jnp.where((row >= 0) & (row < nf * fib), value[:, :length], 0.0)
        hi = jnp.where((row + 1 >= 0) & (row + 1 < nf * fib), value[:, length:], 0.0)
        m[dst, r] = jnp.concatenate([lo, hi], axis=1)

    def first(slot, i, q, cur, prev, dst):
        chi, clo = split(s[cur, q])
        phi, plo = split(s[prev, q])
        d, n = DILATION_ONE, length

        def shift(p, c):
            return jnp.concatenate([p[:, d:n], c[:, :d], p[:, n + d:], c[:, n:n + d]], axis=1)

        shi, slo = shift(phi, chi), shift(plo, clo)
        push(acc.at[slot, q + 1], acc.at[slot, q], l1, [chi, clo, chi, shi, slo, shi, phi, plo, phi])

        @pl.when(i >= 2)
        def _():
            emit(slot, cur, ready(i), dst)

        @pl.when(twice(i))
        def _():
            emit(slot, cur, own - 1, dst)

    def out_emit(p):
        value = gate(acc2[p + 1], q2, c2, straddle(m, 0, p))
        for e in range(2):
            for c in range(0, length, 128):
                out_ref[pl.ds(c // 128 * fib + 2 * p + e, ch, stride=fib * length // 128), :] = value[:, e * length + c:e * length + c + 128]

    def last(i):
        r = pick(i, order2)

        @pl.when(T >= 1)
        def _():
            share(0, r).wait_recv()
        pieces = []
        for k in range(3):
            pieces += thirds(m[k, r])
        push(acc2.at[r + 1], acc2.at[r], l2, pieces)

        @pl.when(i >= 1)
        def _():
            out_emit(jnp.where(i < own - 1, i, jnp.where(i == own - 1, 0, own - 1)))

    def send_mid(i):
        def one(r):
            @pl.when(even)
            def _():
                share(0, r).start()

            @pl.when(isodd & late)
            def _():
                share(2, r).start()

        one(ready(i))

        @pl.when(twice(i))
        def _():
            one(own - 1)

    def forward(q):
        @pl.when(even)
        def _():
            part3(q).start()

        @pl.when(isodd)
        def _():
            part(2, q).start()

    def early(i, carry):
        q = pick(i, order)

        @pl.when(T >= 1)
        def _():
            part(0, q).wait_recv()

        first(0, i, q, 0, 1, 0)

        @pl.when((T == 0) & (i >= 2))
        def _():
            send_mid(i)

        return carry

    @pl.when(isodd | (T == 0))
    def _():
        lax.fori_loop(0, wide, early, 0)

    def stream(i, carry):
        q = pick(i, order)

        @pl.when(i >= own)
        def _():
            last(i - own)

        inner = i < own

        @pl.when(inner)
        def _():
            cross(q).wait_recv()

        @pl.when((q == 1) & down)
        def _():
            halo_down(2, h2s, h2r).start()

        @pl.when((q == own) & up)
        def _():
            halo_up(2, h2s, h2r).start()

        @pl.when((q == 0) & down)
        def _():
            halo_up(2, h2s, h2r).wait_recv()

        @pl.when((q == own + 1) & up)
        def _():
            halo_down(2, h2s, h2r).wait_recv()
        forward(q)

        @pl.when(isodd)
        def _():
            part3(q).wait_recv()
        first(1, i, q, 2, 3, 2)

        @pl.when(even)
        def _():
            part(0, q).wait_recv()
            first(0, i, q, 0, 1, 0)

        @pl.when(i >= 2)
        def _():
            send_mid(i)
        return carry

    @pl.when(late)
    def _():
        if far:
            for i, e, _ok, ok in thirds_list:
                @pl.when(recv3 if ok is None else recv3 & ok)
                def _(i=i, e=e):
                    third(i, e).wait_recv()
        lax.fori_loop(0, wide, stream, 0)

    def final(i, carry):
        last(i)
        return carry

    lax.fori_loop(jnp.where(late, 2, 0), mid, final, 0)
    @pl.when(T + 2 < nt)
    def _():
        for q in arrive:
            cross(q).wait_send()

    @pl.when(up)
    def _():
        halo_up(0, h0s, h0r).wait_send()

    @pl.when(down)
    def _():
        halo_down(0, h0s, h0r).wait_send()

    @pl.when(late & up)
    def _():
        halo_up(2, h2s, h2r).wait_send()

    @pl.when(late & down)
    def _():
        halo_down(2, h2s, h2r).wait_send()

    for q in range(wide):
        @pl.when(even | late)
        def _(q=q):
            part(0, q).wait_send()

        @pl.when(even & late)
        def _(q=q):
            part3(q).wait_send()

    @pl.when(even | late)
    def _():
        for r in range(mid):
            share(0, r).wait_send()

    if far:
        for i, e, ok, _ok in thirds_list:
            @pl.when(send3 if ok is None else send3 & ok)
            def _(i=i, e=e):
                third(i, e).wait_send()


def solution(mesh):
    nt, nf = mesh.shape["tm"], mesh.shape["fibre"]
    placed = (P(None, "fibre", "tm"), P(), P(), P(), P(), P(), P())

    def body(signal, w1, b1, r1, w2, b2, r2):
        ch, fib, length = signal.shape
        assert length == DILATION_TWO == 2 * DILATION_ONE and nt % 2 == 0 and fib % 2 == 0 and fib >= 8
        x = signal.reshape(ch, fib, length // 128, 128).transpose(0, 2, 1, 3).reshape(-1, 128)
        out_ch = w1.shape[2]
        own = fib // 2
        w1, w2 = jnp.transpose(w1, (0, 1, 3, 2)), jnp.transpose(w2, (0, 1, 3, 2))
        b1 = b1.reshape(1, out_ch)
        b2 = b2.reshape(1, out_ch)
        dma = lambda n: pltpu.SemaphoreType.DMA((n,))
        out = pl.pallas_call(
            lambda *refs: kernel(nt, nf, fib, *refs),
            name="gated_layers",
            out_shape=pltpu.VMEM(x.shape, F32),
            in_specs=[pl.BlockSpec(memory_space=pl.ANY)] * 7,
            out_specs=pl.BlockSpec(memory_space=pltpu.VMEM),
            scratch_shapes=[
                pltpu.VMEM((4, own + 2, ch, 2 * length), F32),
                pltpu.VMEM((3, own + 1, ch, 2 * length), F32),
                pltpu.VMEM(x.shape, F32),
                pltpu.VMEM(w1.shape, F32), pltpu.VMEM(b1.shape, F32), pltpu.VMEM(r1.shape, F32),
                pltpu.VMEM(w2.shape, F32), pltpu.VMEM(b2.shape, F32), pltpu.VMEM(r2.shape, F32),
                pltpu.VMEM((3 * out_ch, 9 * ch), BF), pltpu.VMEM((3 * out_ch, 9 * ch), BF),
                pltpu.VMEM((ch, 3 * ch), BF), pltpu.VMEM((ch, 3 * ch), BF),
                pltpu.VMEM((out_ch, out_ch), F32), pltpu.VMEM((out_ch, out_ch), F32),
                pltpu.VMEM((2, own + 3, out_ch, 2 * length), F32),
                pltpu.VMEM((own + 2, out_ch, 2 * length), F32),
                dma(1), dma(6), dma(2), dma(2), dma(2), dma(2), dma(own + 2), dma(own + 2),
                dma(own + 2), dma(own + 2), dma(own + 2), dma(own + 2),
                dma(own + 1), dma(own + 1), dma(3), dma(3),
            ],
            compiler_params=pltpu.CompilerParams(collective_id=0, has_side_effects=True),
        )(x, w1, b1, r1, w2, b2, r2)
        out = out.reshape(ch, length // 128, fib, 128).transpose(0, 2, 1, 3)
        return out.reshape(ch, fib, length)

    return jax.shard_map(body, mesh=mesh, in_specs=placed, out_specs=P(None, "fibre", "tm"), check_vma=False)
```

```python
import jax
import jax.numpy as jnp
from jax import lax
from jax.experimental import pallas as pl
from jax.experimental.pallas import tpu as pltpu
from jax.sharding import PartitionSpec as P

DILATION_ONE = 128
DILATION_TWO = 256
FIB_DEV = 8
BF = jnp.bfloat16
F32 = jnp.float32


def split(value):
    hi = value.astype(BF)
    return hi, (value - hi.astype(F32)).astype(BF)


def pick(i, values):
    out = jnp.int32(values[-1])
    for n in range(len(values) - 2, -1, -1):
        out = jnp.where(i == n, jnp.int32(values[n]), out)
    return out


def kernel(
    nt, nf, fib,
    x_hbm, w1_hbm, b1_hbm, r1_hbm, w2_hbm, b2_hbm, r2_hbm, out_ref,
    af, ab, xv, w1, b1, r1, w2, b2, r2, taps, mix, tall,
    in_sem, w_sem, h0s, h0r, h2s, h2r, xs, xr, ps, pr, ts, tr, ms, mr, es, er, go,
):
    s, m = af.at[0], af.at[1]
    T = lax.axis_index("tm")
    F = lax.axis_index("fibre")
    odd = lax.rem(T, 2)
    even = odd == 0
    isodd = odd == 1
    late = T >= 2
    partner = T + 1 - 2 * odd
    ch, length = af.shape[3], af.shape[4] // 2
    own = fib // 2
    wide = own + 2
    mid = own + 1
    out_ch = 2 * ch
    step = DILATION_ONE
    far = nt > 4
    up, down = F + 1 < nf, F > 0
    onward = T + 2 < nt
    inner = list(range(1, own + 1))
    arrive = [1, own] + list(range(2, own))
    edges = [0, own + 1]

    def dev(t, f):
        return {"tm": t, "fibre": f}

    load = pltpu.make_async_copy(x_hbm, xv, in_sem.at[0])
    load.start()
    weights = [
        pltpu.make_async_copy(a, b, w_sem.at[i])
        for i, (a, b) in enumerate(
            [(w1_hbm, w1), (b1_hbm, b1), (r1_hbm, r1), (w2_hbm, w2), (b2_hbm, b2), (r2_hbm, r2)]
        )
    ]
    for c in weights:
        c.start()

    barrier = pltpu.get_barrier_semaphore()
    friends = [(partner, F, None), (T, F + 1, up), (T, F - 1, down), (T + 2, F, onward), (T - 2, F, late)]
    if far:
        send3 = isodd & (T + 3 < nt)
        recv3 = even & (T >= 4)
        for e, ok in ((0, None), (1, up), (-1, down)):
            for d, okt in ((3, send3), (-3, recv3)):
                friends.append((T + d, F + e, okt if ok is None else okt & ok))
    count = jnp.int32(0)
    for t, f, ok in friends:
        if ok is None:
            pl.semaphore_signal(barrier, inc=1, device_id=dev(t, f), device_id_type=pl.DeviceIdType.MESH)
            count = count + 1
        else:
            @pl.when(ok)
            def _(t=t, f=f):
                pl.semaphore_signal(barrier, inc=1, device_id=dev(t, f), device_id_type=pl.DeviceIdType.MESH)
            count = count + ok.astype(jnp.int32)

    load.wait()
    for f in range(fib):
        for h in range(2):
            value = xv[pl.ds(h * fib + f, ch, stride=fib * 2), :]
            lanes = pl.ds((f % 2) * step, step)
            af[0, 0, 1 + f // 2, :, pl.ds((2 * h + f % 2) * step, step)] = value
            hi, lo = split(value)
            ab[0, 1 + f // 2, 6 + h, 0, :, lanes] = hi
            ab[0, 1 + f // 2, 6 + h, 1, :, lanes] = lo
    pl.semaphore_wait(barrier, count)

    def remote(src, dst, ssem, rsem, t, f):
        return pltpu.make_async_remote_copy(
            src_ref=src, dst_ref=dst, send_sem=ssem, recv_sem=rsem,
            device_id=dev(t, f), device_id_type=pl.DeviceIdType.MESH,
        )

    def halo_up(j, ss, rr):
        return remote(s.at[j, own], s.at[j, 0], ss.at[0], rr.at[0], T, F + 1)

    def halo_down(j, ss, rr):
        return remote(s.at[j, 1], s.at[j, own + 1], ss.at[1], rr.at[1], T, F - 1)

    def cross(q):
        return remote(s.at[0, q], s.at[2, q], xs.at[q], xr.at[q], T + 2, F)

    def part(src, q):
        return remote(s.at[src, q], s.at[1, q], ps.at[q], pr.at[q], partner, F)

    def part3(q):
        return remote(s.at[2, q], s.at[3, q], ts.at[q], tr.at[q], partner, F)

    def share(src, r):
        return remote(m.at[src, r], m.at[1, r], ms.at[r], mr.at[r], partner, F)

    @pl.when(onward & even)
    def _():
        for q in arrive:
            cross(q).start()

    @pl.when(up)
    def _():
        halo_up(0, h0s, h0r).start()

    @pl.when(down)
    def _():
        halo_down(0, h0s, h0r).start()

    @pl.when(even)
    def _():
        for q in arrive:
            part(0, q).start()

    if far:
        def third(i, e):
            if e == 0:
                src, dst = s.at[0, pl.ds(1, own)], s.at[3, pl.ds(1, own)]
            elif e == 1:
                src, dst = s.at[0, own], s.at[3, 0]
            else:
                src, dst = s.at[0, 1], s.at[3, own + 1]
            return remote(src, dst, es.at[i], er.at[i], T + 3, F + e)

        thirds_list = [(0, 0, None, None), (1, 1, up, down), (2, -1, down, up)]
        for i, e, ok, _ok in thirds_list:
            @pl.when(send3 if ok is None else send3 & ok)
            def _(i=i, e=e):
                third(i, e).start()

    zero = jnp.zeros(af.shape[3:], F32)

    def zero_halo(j):
        @pl.when(jnp.logical_not(down))
        def _():
            af[0, j, 0] = zero

        @pl.when(jnp.logical_not(up))
        def _():
            af[0, j, own + 1] = zero

    zero_halo(0)

    def no_chunks(layer, first, n):
        for q in range(wide if layer == 0 else mid):
            ab[layer, q, pl.ds(first, n)] = jnp.zeros((n,) + ab.shape[3:], BF)

    @pl.when(T == 0)
    def _():
        no_chunks(0, 4, 2)
        no_chunks(1, 4, 2)

    @pl.when(T < 2)
    def _():
        no_chunks(1, 2, 2)

    @pl.when(T == 2)
    def _():
        no_chunks(0, 0, 2)

    @pl.when(late)
    def _():
        zero_halo(2)

    if far:
        @pl.when(recv3)
        def _():
            zero_halo(3)

    for c in weights:
        c.wait()

    def prepare(layer, w, r, bias):
        for a in range(3):
            for k in range(3):
                hi, lo = split(w[a, k].T)
                for i, piece in enumerate((hi, hi, lo)):
                    taps[layer, :, pl.ds((9 * a + 3 * k + i) * ch, ch)] = piece
        hi, lo = split(r[...])
        for i, piece in enumerate((hi, hi, lo)):
            mix[layer, :, pl.ds(i * ch, ch)] = piece
        tall[layer] = jnp.broadcast_to(bias[...], (out_ch, out_ch)).T

    prepare(0, w1, r1, b1)
    prepare(1, w2, r2, b2)

    def ingest(layer, j, q):
        hi, lo = split(af[layer, j, q])
        for h in range(2):
            ab[layer, q, 2 * (3 - j) + h, 0] = hi[:, h * 2 * step:(h + 1) * 2 * step]
            ab[layer, q, 2 * (3 - j) + h, 1] = lo[:, h * 2 * step:(h + 1) * 2 * step]

    @pl.when(onward & even)
    def _():
        for q in arrive[:-1]:
            cross(q).wait_send()
        pl.semaphore_signal(go, inc=1, device_id=dev(partner, F), device_id_type=pl.DeviceIdType.MESH)

    @pl.when(onward & isodd)
    def _():
        pl.semaphore_wait(go, 1)
        for q in arrive:
            cross(q).start()

    if far:
        @pl.when(recv3)
        def _():
            for i, e, _ok, ok in thirds_list:
                if ok is None:
                    third(i, e).wait_recv()
                else:
                    @pl.when(ok)
                    def _(i=i, e=e):
                        third(i, e).wait_recv()

            def old(q, carry):
                ingest(0, 3, q)
                return carry

            lax.fori_loop(0, wide, old, 0)

    late_even, late_odd = late & even, late & isodd

    def halos_in(j, ss, rr):
        @pl.when(down)
        def _():
            halo_up(j, ss, rr).wait_recv()

        @pl.when(up)
        def _():
            halo_down(j, ss, rr).wait_recv()

    def crossed(q):
        cross(q).wait_recv()

        @pl.when(even)
        def _():
            part3(q).start()

        @pl.when(isodd)
        def _():
            part(2, q).start()

        if q == 1:
            @pl.when(down)
            def _():
                halo_down(2, h2s, h2r).start()

        if q == own:
            @pl.when(up)
            def _():
                halo_up(2, h2s, h2r).start()

    def event(i):
        if i == 0:
            @pl.when(late_even)
            def _():
                for q in arrive:
                    crossed(q)

            @pl.when(isodd)
            def _():
                for q in arrive:
                    part(0, q).wait_recv()
        if i == 1:
            @pl.when(late_odd)
            def _():
                crossed(arrive[0])

            halos_in(0, h0s, h0r)

            @pl.when(even)
            def _():
                for q in edges:
                    part(0, q).start()

            @pl.when(isodd)
            def _():
                for q in edges:
                    part(0, q).wait_recv()

            @pl.when(late_even)
            def _():
                halos_in(2, h2s, h2r)
                for q in edges:
                    part3(q).start()
        if i in (2, 3):
            now = arrive[:-1] if i == 2 else arrive[-1:]

            @pl.when(late_even)
            def _():
                for q in now:
                    part(0, q).wait_recv()

            @pl.when(late_odd)
            def _():
                for q in now:
                    if q != arrive[0]:
                        crossed(q)
                for q in now:
                    part3(q).wait_recv()
        if i == 4:
            @pl.when(late_even)
            def _():
                for q in edges:
                    part(0, q).wait_recv()

            @pl.when(late_odd)
            def _():
                halos_in(2, h2s, h2r)
                for q in edges:
                    part(2, q).start()
                for q in edges:
                    part3(q).wait_recv()
        if i == 5:
            @pl.when(T >= 1)
            def _():
                for r in range(1, own):
                    share(0, r).wait_recv()
        if i == 6:
            @pl.when(T >= 1)
            def _():
                for r in (0, own):
                    share(0, r).wait_recv()

    rows = [
        (("A", 1), ("A", 2)), (("A", 3), ("A", 0)), (("A", own), ("B", 1)), (("B", 2), ("B", 3)), (("B", 0), ("B", own)),
        (("C", 1), ("C", 2)), (("C", 0), ("C", own - 1)),
    ]
    steps = len(rows)
    first_of_two = steps - 2
    ja = jnp.where(late_even, 2, 0)
    jb = jnp.where(even, 0, 2)
    start = [1, 0, 1, 3, 0, 1, 0]
    number = [own, 2, 2, own - 2, 2, own - 1, 2]
    stride = [1, own + 1, 1, 1, own + 1, 1, own]
    le = [(2,), (0, 2), (1,), (1,), (1,), (1,), (1,)]
    lo_ = [(1,), (0, 1), (2, 3), (2, 3), (2, 3), (1,), (1,)]
    ee = [(), (0,), (), (), (), (), ()]
    eo = [(1,), (0, 1), (), (), (), (1,), (1,)]

    def by_class(i, of):
        table = [pick(i, [of(entry) for entry in c]) for c in (le, lo_, ee, eo)]
        return jnp.where(late, jnp.where(even, table[0], table[1]), jnp.where(even, table[2], table[3]))

    def operand(layer, r, b, d):
        pieces = []
        for a in range(3):
            for k in range(3):
                both = []
                for part_ in range(2):
                    cols = []
                    for h in range(2):
                        c = 2 * b + h - k * d
                        if a == 0:
                            cols.append(ab[layer, r, c, part_])
                        elif a == 2:
                            cols.append(ab[layer, r + 1, c, part_])
                        else:
                            cols += [ab[layer, r, c, part_, :, step:], ab[layer, r + 1, c, part_, :, :step]]
                    both.append(jnp.concatenate(cols, axis=1))
                pieces += [both[0], both[1], both[0]]
        return jnp.concatenate(pieces, axis=0)

    def straddle(layer, j, r):
        cols = []
        for h in range(2):
            cols += [af[layer, j, r, :, (2 * h + 1) * step:(2 * h + 2) * step], af[layer, j, r + 1, :, 2 * h * step:(2 * h + 1) * step]]
        return jnp.concatenate(cols, axis=1)

    def compute(layer, d, units):
        right = jnp.concatenate([operand(layer, r, 3 - j, d) for r, j in units], axis=1)
        total = jnp.dot(taps[layer], right, preferred_element_type=F32)
        pre = total + jnp.concatenate([tall[layer]] * (total.shape[1] // out_ch), axis=1)
        g = jnp.tanh(pre[:ch]) * (0.5 * jnp.tanh(0.5 * pre[ch:]) + 0.5)
        hi, lo = split(g)
        base = jnp.concatenate([straddle(layer, j, r) for r, j in units], axis=1)
        return base + jnp.dot(mix[layer], jnp.concatenate([hi, lo, hi], axis=0), preferred_element_type=F32)

    def body(i, carry):
        for n in range(steps):
            @pl.when(i == n)
            def _(n=n):
                event(n)

        first, each, pace = pick(i, start), pick(i, number), pick(i, stride)
        j0 = by_class(i, lambda e: e[0] if e else 0)
        j1 = by_class(i, lambda e: e[1] if len(e) > 1 else 0)
        blocks = by_class(i, len)
        layer = (i >= first_of_two).astype(jnp.int32)

        def take(n, carry):
            second = n >= each
            q = first + pace * jnp.where(second, n - each, n)
            ingest(layer, jnp.where(second, j1, j0), q)
            return carry

        lax.fori_loop(0, each * blocks, take, 0)

        units = []
        for lane in range(2):
            r = pick(i, [pair[lane][1] for pair in rows])
            kind = pick(i, ["ABC".index(pair[lane][0]) for pair in rows])
            if any(pair[lane][0] == "B" and pair[0][0] == "A" for pair in rows):
                r = jnp.where((kind == 1) & jnp.logical_not(late), own, r)
            j = jnp.where(kind == 0, ja, jnp.where(kind == 1, jnp.where(late, jb, 0), 0))
            units.append((r, j, kind))

        @pl.when(late | (i < 3) | (i >= first_of_two))
        def _():
            value = compute(layer, layer + 1, [(r, j) for r, j, _ in units])

            @pl.when(layer == 0)
            def _():
                for n, (r, j, kind) in enumerate(units):
                    v = value[:, n * 2 * length:(n + 1) * 2 * length]
                    row = F * fib + 2 * r - 1
                    ok = [(row >= 0) & (row < nf * fib), (row + 1 >= 0) & (row + 1 < nf * fib)]
                    v = jnp.concatenate([jnp.where(ok[p % 2], v[:, p * step:(p + 1) * step], 0.0) for p in range(4)], axis=1)
                    af[1, j, r] = v
                    hi, lo = split(v)
                    for h in range(2):
                        ab[1, r, 2 * (3 - j) + h, 0] = hi[:, h * 2 * step:(h + 1) * 2 * step]
                        ab[1, r, 2 * (3 - j) + h, 1] = lo[:, h * 2 * step:(h + 1) * 2 * step]

                for r, j, kind in units:
                    @pl.when((late & (kind == 1)) | ((T == 0) & (kind == 0)))
                    def _(r=r, j=j):
                        share(j, r).start()

            @pl.when(layer == 1)
            def _():
                for n, (r, j, kind) in enumerate(units):
                    for p in range(4):
                        h, e = p // 2, p % 2
                        at = n * 2 * length + p * step
                        out_ref[pl.ds(h * fib + 2 * r + e, ch, stride=fib * 2), :] = value[:, at:at + step]
        return carry

    lax.fori_loop(0, steps, body, 0)

    @pl.when(onward & even)
    def _():
        cross(arrive[-1]).wait_send()

    @pl.when(onward & isodd)
    def _():
        for q in arrive:
            cross(q).wait_send()

    for j, ss, rr, ok in ((0, h0s, h0r, None), (2, h2s, h2r, late)):
        @pl.when(up if ok is None else up & ok)
        def _(j=j, ss=ss, rr=rr):
            halo_up(j, ss, rr).wait_send()

        @pl.when(down if ok is None else down & ok)
        def _(j=j, ss=ss, rr=rr):
            halo_down(j, ss, rr).wait_send()

    for q in range(wide):
        @pl.when(even | late)
        def _(q=q):
            part(0, q).wait_send()

        @pl.when(late_even)
        def _(q=q):
            part3(q).wait_send()

    @pl.when(even | late)
    def _():
        for r in range(mid):
            share(0, r).wait_send()

    if far:
        for i, e, ok, _ok in thirds_list:
            @pl.when(send3 if ok is None else send3 & ok)
            def _(i=i, e=e):
                third(i, e).wait_send()


def solution(mesh):
    nt, nf = mesh.shape["tm"], mesh.shape["fibre"]
    placed = (P(None, "fibre", "tm"), P(), P(), P(), P(), P(), P())

    def body(signal, w1, b1, r1, w2, b2, r2):
        ch, fib, length = signal.shape
        assert length == DILATION_TWO == 2 * DILATION_ONE and nt % 2 == 0 and fib == FIB_DEV
        x = signal.reshape(ch, fib, length // 128, 128).transpose(0, 2, 1, 3).reshape(-1, 128)
        out_ch = w1.shape[2]
        own = fib // 2
        w1, w2 = jnp.transpose(w1, (0, 1, 3, 2)), jnp.transpose(w2, (0, 1, 3, 2))
        b1 = b1.reshape(1, out_ch)
        b2 = b2.reshape(1, out_ch)
        dma = lambda n: pltpu.SemaphoreType.DMA((n,))
        out = pl.pallas_call(
            lambda *refs: kernel(nt, nf, fib, *refs),
            name="gated_layers",
            out_shape=pltpu.VMEM(x.shape, F32),
            in_specs=[pl.BlockSpec(memory_space=pl.ANY)] * 7,
            out_specs=pl.BlockSpec(memory_space=pltpu.VMEM),
            scratch_shapes=[
                pltpu.VMEM((2, 4, own + 2, ch, 2 * length), F32),
                pltpu.VMEM((2, own + 2, 4 * length // DILATION_ONE, 2, ch, 2 * DILATION_ONE), BF),
                pltpu.VMEM(x.shape, F32),
                pltpu.VMEM(w1.shape, F32), pltpu.VMEM(b1.shape, F32), pltpu.VMEM(r1.shape, F32),
                pltpu.VMEM(w2.shape, F32), pltpu.VMEM(b2.shape, F32), pltpu.VMEM(r2.shape, F32),
                pltpu.VMEM((2, out_ch, 27 * ch), BF), pltpu.VMEM((2, ch, 3 * ch), BF),
                pltpu.VMEM((2, out_ch, out_ch), F32),
                dma(1), dma(6), dma(2), dma(2), dma(2), dma(2), dma(own + 2), dma(own + 2),
                dma(own + 2), dma(own + 2), dma(own + 2), dma(own + 2),
                dma(own + 1), dma(own + 1), dma(3), dma(3),
                pltpu.SemaphoreType.REGULAR,
            ],
            compiler_params=pltpu.CompilerParams(
                collective_id=0, has_side_effects=True, vmem_limit_bytes=60 * 1024 * 1024
            ),
        )(x, w1, b1, r1, w2, b2, r2)
        out = out.reshape(ch, length // 128, fib, 128).transpose(0, 2, 1, 3)
        return out.reshape(ch, fib, length)

    return jax.shard_map(body, mesh=mesh, in_specs=placed, out_specs=P(None, "fibre", "tm"), check_vma=False)
```

```python
import jax
import jax.numpy as jnp
from jax import lax
from jax.experimental import pallas as pl
from jax.experimental.pallas import tpu as pltpu
from jax.sharding import PartitionSpec as P

DILATION_ONE = 128
DILATION_TWO = 256
FIB_DEV = 8
BF = jnp.bfloat16
F32 = jnp.float32


def split(value):
    hi = value.astype(BF)
    return hi, (value - hi.astype(F32)).astype(BF)


def pick(i, values):
    out = jnp.int32(values[-1])
    for n in range(len(values) - 2, -1, -1):
        out = jnp.where(i == n, jnp.int32(values[n]), out)
    return out


def kernel(
    nt, nf, fib,
    x_hbm, w1_hbm, b1_hbm, r1_hbm, w2_hbm, b2_hbm, r2_hbm, out_ref,
    af, ab, xv, w1, b1, r1, w2, b2, r2, taps, mix, tall,
    in_sem, w_sem, h0s, h0r, h2s, h2r, xs, xr, ps, pr, ts, tr, ms, mr, es, er, go,
):
    s, m = af.at[0], af.at[1]
    T = lax.axis_index("tm")
    F = lax.axis_index("fibre")
    odd = lax.rem(T, 2)
    even = odd == 0
    isodd = odd == 1
    late = T >= 2
    partner = T + 1 - 2 * odd
    ch, length = af.shape[3], af.shape[4] // 2
    own = fib // 2
    wide = own + 2
    mid = own + 1
    out_ch = 2 * ch
    step = DILATION_ONE
    far = nt > 4
    up, down = F + 1 < nf, F > 0
    onward = T + 2 < nt
    inner = list(range(1, own + 1))
    arrive = [1, own] + list(range(2, own))
    edges = [0, own + 1]

    def dev(t, f):
        return {"tm": t, "fibre": f}

    load = pltpu.make_async_copy(x_hbm, xv, in_sem.at[0])
    load.start()
    weights = [
        pltpu.make_async_copy(a, b, w_sem.at[i])
        for i, (a, b) in enumerate(
            [(w1_hbm, w1), (b1_hbm, b1), (r1_hbm, r1), (w2_hbm, w2), (b2_hbm, b2), (r2_hbm, r2)]
        )
    ]
    for c in weights:
        c.start()

    barrier = pltpu.get_barrier_semaphore()
    friends = [(partner, F, None), (T, F + 1, up), (T, F - 1, down), (T + 2, F, onward), (T - 2, F, late)]
    if far:
        send3 = isodd & (T + 3 < nt)
        recv3 = even & (T >= 4)
        for e, ok in ((0, None), (1, up), (-1, down)):
            for d, okt in ((3, send3), (-3, recv3)):
                friends.append((T + d, F + e, okt if ok is None else okt & ok))
    count = jnp.int32(0)
    for t, f, ok in friends:
        if ok is None:
            pl.semaphore_signal(barrier, inc=1, device_id=dev(t, f), device_id_type=pl.DeviceIdType.MESH)
            count = count + 1
        else:
            @pl.when(ok)
            def _(t=t, f=f):
                pl.semaphore_signal(barrier, inc=1, device_id=dev(t, f), device_id_type=pl.DeviceIdType.MESH)
            count = count + ok.astype(jnp.int32)

    load.wait()
    for f in range(fib):
        for h in range(2):
            value = xv[pl.ds(h * fib + f, ch, stride=fib * 2), :]
            lanes = pl.ds((f % 2) * step, step)
            af[0, 0, 1 + f // 2, :, pl.ds((2 * h + f % 2) * step, step)] = value
            hi, lo = split(value)
            ab[0, 1 + f // 2, 6 + h, 0, :, lanes] = hi
            ab[0, 1 + f // 2, 6 + h, 1, :, lanes] = lo
    pl.semaphore_wait(barrier, count)

    def remote(src, dst, ssem, rsem, t, f):
        return pltpu.make_async_remote_copy(
            src_ref=src, dst_ref=dst, send_sem=ssem, recv_sem=rsem,
            device_id=dev(t, f), device_id_type=pl.DeviceIdType.MESH,
        )

    def halo_up(j, ss, rr):
        return remote(s.at[j, own], s.at[j, 0], ss.at[0], rr.at[0], T, F + 1)

    def halo_down(j, ss, rr):
        return remote(s.at[j, 1], s.at[j, own + 1], ss.at[1], rr.at[1], T, F - 1)

    def cross(q):
        return remote(s.at[0, q], s.at[2, q], xs.at[q], xr.at[q], T + 2, F)

    def part(src, q):
        return remote(s.at[src, q], s.at[1, q], ps.at[q], pr.at[q], partner, F)

    def part3(q):
        return remote(s.at[2, q], s.at[3, q], ts.at[q], tr.at[q], partner, F)

    def share(src, r):
        return remote(m.at[src, r], m.at[1, r], ms.at[r], mr.at[r], partner, F)

    @pl.when(onward & even)
    def _():
        for q in arrive:
            cross(q).start()

    @pl.when(up)
    def _():
        halo_up(0, h0s, h0r).start()

    @pl.when(down)
    def _():
        halo_down(0, h0s, h0r).start()

    @pl.when(even)
    def _():
        for q in arrive:
            part(0, q).start()

    if far:
        def third(i, e):
            if e == 0:
                src, dst = s.at[0, pl.ds(1, own)], s.at[3, pl.ds(1, own)]
            elif e == 1:
                src, dst = s.at[0, own], s.at[3, 0]
            else:
                src, dst = s.at[0, 1], s.at[3, own + 1]
            return remote(src, dst, es.at[i], er.at[i], T + 3, F + e)

        thirds_list = [(0, 0, None, None), (1, 1, up, down), (2, -1, down, up)]
        for i, e, ok, _ok in thirds_list:
            @pl.when(send3 if ok is None else send3 & ok)
            def _(i=i, e=e):
                third(i, e).start()

    zero = jnp.zeros(af.shape[3:], F32)

    def zero_halo(j):
        @pl.when(jnp.logical_not(down))
        def _():
            af[0, j, 0] = zero

        @pl.when(jnp.logical_not(up))
        def _():
            af[0, j, own + 1] = zero

    zero_halo(0)

    def no_chunks(layer, first, n):
        for q in range(wide if layer == 0 else mid):
            ab[layer, q, pl.ds(first, n)] = jnp.zeros((n,) + ab.shape[3:], BF)

    @pl.when(T == 0)
    def _():
        no_chunks(0, 4, 2)
        no_chunks(1, 4, 2)

    @pl.when(T < 2)
    def _():
        no_chunks(1, 2, 2)

    @pl.when(T == 2)
    def _():
        no_chunks(0, 0, 2)

    @pl.when(late)
    def _():
        zero_halo(2)

    if far:
        @pl.when(recv3)
        def _():
            zero_halo(3)

    for c in weights:
        c.wait()

    def prepare(layer, w, r, bias):
        for a in range(3):
            for k in range(3):
                hi, lo = split(w[a, k].T)
                for i, piece in enumerate((hi, hi, lo)):
                    taps[layer, :, pl.ds((9 * a + 3 * k + i) * ch, ch)] = piece
        hi, lo = split(r[...])
        for i, piece in enumerate((hi, hi, lo)):
            mix[layer, :, pl.ds(i * ch, ch)] = piece
        tall[layer] = jnp.broadcast_to(bias[...], (out_ch, out_ch)).T

    prepare(0, w1, r1, b1)
    prepare(1, w2, r2, b2)

    def ingest(layer, j, q):
        hi, lo = split(af[layer, j, q])
        for h in range(2):
            ab[layer, q, 2 * (3 - j) + h, 0] = hi[:, h * 2 * step:(h + 1) * 2 * step]
            ab[layer, q, 2 * (3 - j) + h, 1] = lo[:, h * 2 * step:(h + 1) * 2 * step]

    @pl.when(onward & even)
    def _():
        for q in arrive[:-1]:
            cross(q).wait_send()
        pl.semaphore_signal(go, inc=1, device_id=dev(partner, F), device_id_type=pl.DeviceIdType.MESH)

    @pl.when(onward & isodd)
    def _():
        pl.semaphore_wait(go, 1)
        for q in arrive:
            cross(q).start()

    if far:
        @pl.when(recv3)
        def _():
            for i, e, _ok, ok in thirds_list:
                if ok is None:
                    third(i, e).wait_recv()
                else:
                    @pl.when(ok)
                    def _(i=i, e=e):
                        third(i, e).wait_recv()

            def old(q, carry):
                ingest(0, 3, q)
                return carry

            lax.fori_loop(0, wide, old, 0)

    late_even, late_odd = late & even, late & isodd

    def halos_in(j, ss, rr):
        @pl.when(down)
        def _():
            halo_up(j, ss, rr).wait_recv()

        @pl.when(up)
        def _():
            halo_down(j, ss, rr).wait_recv()

    def crossed(q):
        cross(q).wait_recv()

        @pl.when(even)
        def _():
            part3(q).start()

        @pl.when(isodd)
        def _():
            part(2, q).start()

        if q == 1:
            @pl.when(down)
            def _():
                halo_down(2, h2s, h2r).start()

        if q == own:
            @pl.when(up)
            def _():
                halo_up(2, h2s, h2r).start()

    def event(i):
        if i == 0:
            @pl.when(late_even)
            def _():
                for q in arrive:
                    crossed(q)

            @pl.when(isodd)
            def _():
                for q in arrive:
                    part(0, q).wait_recv()
        if i == 1:
            @pl.when(late_odd)
            def _():
                crossed(arrive[0])

            halos_in(0, h0s, h0r)

            @pl.when(even)
            def _():
                for q in edges:
                    part(0, q).start()

            @pl.when(isodd)
            def _():
                for q in edges:
                    part(0, q).wait_recv()

            @pl.when(late_even)
            def _():
                halos_in(2, h2s, h2r)
                for q in edges:
                    part3(q).start()
        if i in (2, 3):
            now = arrive[:-1] if i == 2 else arrive[-1:]

            @pl.when(late_even)
            def _():
                for q in now:
                    part(0, q).wait_recv()

            @pl.when(late_odd)
            def _():
                for q in now:
                    if q != arrive[0]:
                        crossed(q)
                for q in now:
                    part3(q).wait_recv()
        if i == 4:
            @pl.when(late_even)
            def _():
                for q in edges:
                    part(0, q).wait_recv()

            @pl.when(late_odd)
            def _():
                halos_in(2, h2s, h2r)
                for q in edges:
                    part(2, q).start()
                for q in edges:
                    part3(q).wait_recv()
        if i == 5:
            @pl.when(T >= 1)
            def _():
                for r in range(1, own):
                    share(0, r).wait_recv()
        if i == 6:
            @pl.when(T >= 1)
            def _():
                for r in (0, own):
                    share(0, r).wait_recv()

    rows = [
        (("A", 1), ("A", 2)), (("A", 3), ("A", 0)), (("A", own), ("B", 1)), (("B", 2), ("B", 3)), (("B", 0), ("B", own)),
        (("C", 1), ("C", 2)), (("C", 0), ("C", own - 1)),
    ]
    steps = len(rows)
    first_of_two = steps - 2
    ja = jnp.where(late_even, 2, 0)
    jb = jnp.where(even, 0, 2)
    start = [1, 0, 1, 3, 0, 1, 0]
    number = [own, 2, 2, own - 2, 2, own - 1, 2]
    stride = [1, own + 1, 1, 1, own + 1, 1, own]
    le = [(2,), (0, 2), (1,), (1,), (1,), (1,), (1,)]
    lo_ = [(1,), (0, 1), (2, 3), (2, 3), (2, 3), (1,), (1,)]
    ee = [(), (0,), (), (), (), (), ()]
    eo = [(1,), (0, 1), (), (), (), (1,), (1,)]

    def by_class(i, of):
        table = [pick(i, [of(entry) for entry in c]) for c in (le, lo_, ee, eo)]
        return jnp.where(late, jnp.where(even, table[0], table[1]), jnp.where(even, table[2], table[3]))

    def operand(layer, r, b, d):
        pieces = []
        for a in range(3):
            for k in range(3):
                both = []
                for part_ in range(2):
                    cols = []
                    for h in range(2):
                        c = 2 * b + h - k * d
                        if a == 0:
                            cols.append(ab[layer, r, c, part_])
                        elif a == 2:
                            cols.append(ab[layer, r + 1, c, part_])
                        else:
                            cols += [ab[layer, r, c, part_, :, step:], ab[layer, r + 1, c, part_, :, :step]]
                    both.append(jnp.concatenate(cols, axis=1))
                pieces += [both[0], both[1], both[0]]
        return jnp.concatenate(pieces, axis=0)

    def straddle(layer, j, r):
        cols = []
        for h in range(2):
            cols += [af[layer, j, r, :, (2 * h + 1) * step:(2 * h + 2) * step], af[layer, j, r + 1, :, 2 * h * step:(2 * h + 1) * step]]
        return jnp.concatenate(cols, axis=1)

    def compute(layer, d, units):
        right = jnp.concatenate([operand(layer, r, 3 - j, d) for r, j in units], axis=1)
        total = jnp.dot(taps[layer], right, preferred_element_type=F32)
        pre = total + jnp.concatenate([tall[layer]] * (total.shape[1] // out_ch), axis=1)
        g = jnp.tanh(pre[:ch]) * (0.5 * jnp.tanh(0.5 * pre[ch:]) + 0.5)
        hi, lo = split(g)
        base = jnp.concatenate([straddle(layer, j, r) for r, j in units], axis=1)
        return base + jnp.dot(mix[layer], jnp.concatenate([hi, lo, hi], axis=0), preferred_element_type=F32)

    def body(i, carry):
        for n in range(steps):
            @pl.when(i == n)
            def _(n=n):
                event(n)

        first, each, pace = pick(i, start), pick(i, number), pick(i, stride)
        j0 = by_class(i, lambda e: e[0] if e else 0)
        j1 = by_class(i, lambda e: e[1] if len(e) > 1 else 0)
        blocks = by_class(i, len)
        layer = (i >= first_of_two).astype(jnp.int32)

        def take(n, carry):
            second = n >= each
            q = first + pace * jnp.where(second, n - each, n)
            ingest(layer, jnp.where(second, j1, j0), q)
            return carry

        lax.fori_loop(0, each * blocks, take, 0)

        units = []
        for lane in range(2):
            r = pick(i, [pair[lane][1] for pair in rows])
            kind = pick(i, ["ABC".index(pair[lane][0]) for pair in rows])
            if any(pair[lane][0] == "B" and pair[0][0] == "A" for pair in rows):
                r = jnp.where((kind == 1) & jnp.logical_not(late), own, r)
            j = jnp.where(kind == 0, ja, jnp.where(kind == 1, jnp.where(late, jb, 0), 0))
            units.append((r, j, kind))

        @pl.when(late | (i < 3) | (i >= first_of_two))
        def _():
            value = compute(layer, layer + 1, [(r, j) for r, j, _ in units])

            @pl.when(layer == 0)
            def _():
                for n, (r, j, kind) in enumerate(units):
                    v = value[:, n * 2 * length:(n + 1) * 2 * length]
                    row = F * fib + 2 * r - 1
                    ok = [(row >= 0) & (row < nf * fib), (row + 1 >= 0) & (row + 1 < nf * fib)]
                    v = jnp.concatenate([jnp.where(ok[p % 2], v[:, p * step:(p + 1) * step], 0.0) for p in range(4)], axis=1)
                    af[1, j, r] = v
                    hi, lo = split(v)
                    for h in range(2):
                        ab[1, r, 2 * (3 - j) + h, 0] = hi[:, h * 2 * step:(h + 1) * 2 * step]
                        ab[1, r, 2 * (3 - j) + h, 1] = lo[:, h * 2 * step:(h + 1) * 2 * step]

                for r, j, kind in units:
                    @pl.when((late & (kind == 1)) | ((T == 0) & (kind == 0)))
                    def _(r=r, j=j):
                        share(j, r).start()

            @pl.when(layer == 1)
            def _():
                for n, (r, j, kind) in enumerate(units):
                    for p in range(4):
                        h, e = p // 2, p % 2
                        at = n * 2 * length + p * step
                        out_ref[pl.ds(h * fib + 2 * r + e, ch, stride=fib * 2), :] = value[:, at:at + step]
        return carry

    lax.fori_loop(0, steps, body, 0)

    @pl.when(onward & even)
    def _():
        cross(arrive[-1]).wait_send()

    @pl.when(onward & isodd)
    def _():
        for q in arrive:
            cross(q).wait_send()

    for j, ss, rr, ok in ((0, h0s, h0r, None), (2, h2s, h2r, late)):
        @pl.when(up if ok is None else up & ok)
        def _(j=j, ss=ss, rr=rr):
            halo_up(j, ss, rr).wait_send()

        @pl.when(down if ok is None else down & ok)
        def _(j=j, ss=ss, rr=rr):
            halo_down(j, ss, rr).wait_send()

    for q in range(wide):
        @pl.when(even | late)
        def _(q=q):
            part(0, q).wait_send()

        @pl.when(late_even)
        def _(q=q):
            part3(q).wait_send()

    @pl.when(even | late)
    def _():
        for r in range(mid):
            share(0, r).wait_send()

    if far:
        for i, e, ok, _ok in thirds_list:
            @pl.when(send3 if ok is None else send3 & ok)
            def _(i=i, e=e):
                third(i, e).wait_send()


def spread_kernel(
    nt, nf, fib,
    x_hbm, w1_hbm, b1_hbm, r1_hbm, w2_hbm, b2_hbm, r2_hbm, out_ref,
    xv, w1, b1, r1, w2, b2, r2, taps, mix, tall, pk, af, sf, ab, mf, mb, fs, fr,
    in_sem, w_sem, xs, xr, hs, hr, gs, gr,
):
    T = lax.axis_index("tm")
    F = lax.axis_index("fibre")
    odd = lax.rem(T, 2)
    partner = T + 1 - 2 * odd
    peers = [partner, lax.rem(T + 2, nt), lax.rem(partner + 2, nt)]
    chip = T - odd
    other = lax.rem(chip + 2, nt)
    ch = pk.shape[2]
    own = fib // 2
    out_ch = 2 * ch
    step = DILATION_ONE
    group = step // nt
    up, down = F + 1 < nf, F > 0
    inner = list(range(2, own))
    lane = lax.broadcasted_iota(jnp.int32, (ch, step), 1)
    early_half = lane < 2 * group
    first_fibre = lax.rem(lane, 2 * group) < group

    def dev(t, f):
        return {"tm": t, "fibre": f}

    load = pltpu.make_async_copy(x_hbm, xv, in_sem.at[0])
    load.start()
    weights = [
        pltpu.make_async_copy(a, b, w_sem.at[i])
        for i, (a, b) in enumerate(
            [(w1_hbm, w1), (b1_hbm, b1), (r1_hbm, r1), (w2_hbm, w2), (b2_hbm, b2), (r2_hbm, r2)]
        )
    ]
    for c in weights:
        c.start()

    barrier = pltpu.get_barrier_semaphore()
    for p in peers:
        pl.semaphore_signal(barrier, inc=1, device_id=dev(p, F), device_id_type=pl.DeviceIdType.MESH)
    count = jnp.int32(len(peers))
    for e, ok in ((1, up), (-1, down)):
        @pl.when(ok)
        def _(e=e):
            pl.semaphore_signal(barrier, inc=1, device_id=dev(T, F + e), device_id_type=pl.DeviceIdType.MESH)
        count = count + ok.astype(jnp.int32)

    def swap(parts):
        a, b, c, d = parts
        half = 2 * group
        a, c = jnp.where(early_half, a, pltpu.roll(c, half, 1)), jnp.where(early_half, pltpu.roll(a, half, 1), c)
        b, d = jnp.where(early_half, b, pltpu.roll(d, half, 1)), jnp.where(early_half, pltpu.roll(b, half, 1), d)
        back = step - group
        a, b = jnp.where(first_fibre, a, pltpu.roll(b, group, 1)), jnp.where(first_fibre, pltpu.roll(a, back, 1), b)
        c, d = jnp.where(first_fibre, c, pltpu.roll(d, group, 1)), jnp.where(first_fibre, pltpu.roll(c, back, 1), d)
        return a, b, c, d

    load.wait()

    def pack(q, carry):
        parts = [xv[pl.ds(h * fib + 2 * q + e, ch, stride=fib * 2), :] for h in range(2) for e in range(2)]
        for t, value in enumerate(swap(parts)):
            pk[t, q] = value

            @pl.when(T == t)
            def _(value=value):
                af[q + 1, t] = value
        return carry

    lax.fori_loop(0, own, pack, 0)
    pl.semaphore_wait(barrier, count)

    def remote(src, dst, ssem, rsem, t, f):
        return pltpu.make_async_remote_copy(
            src_ref=src, dst_ref=dst, send_sem=ssem, recv_sem=rsem,
            device_id=dev(t, f), device_id_type=pl.DeviceIdType.MESH,
        )

    def signal_out(k, q):
        n = k * own + q - 1
        return remote(pk.at[peers[k], q - 1], af.at[q, T], xs.at[n], xr.at[n], peers[k], F)

    def signal_in(k, q):
        n = k * own + q - 1
        return remote(pk.at[peers[k], q - 1], af.at[q, peers[k]], xs.at[n], xr.at[n], peers[k], F)

    def halo_up(n):
        blocks = pl.ds((chip, other)[n], 2)
        return remote(af.at[own, blocks], af.at[0, blocks], hs.at[2 * n], hr.at[2 * n], T, F + 1)

    def halo_down(n):
        blocks = pl.ds((chip, other)[n], 2)
        return remote(af.at[1, blocks], af.at[own + 1, blocks], hs.at[2 * n + 1], hr.at[2 * n + 1], T, F - 1)

    def feature_out(k, p):
        n = k * own + p
        return remote(fs.at[p, peers[k]], fr.at[p, T], gs.at[n], gr.at[n], peers[k], F)

    def feature_in(k, p):
        n = k * own + p
        return remote(fs.at[p, peers[k]], fr.at[p, peers[k]], gs.at[n], gr.at[n], peers[k], F)

    for q in (1, own):
        signal_out(1, q).start()
        signal_out(2, q).start()
    for q in [1, own] + inner:
        signal_out(0, q).start()
    for q in inner:
        signal_out(1, q).start()
        signal_out(2, q).start()

    no_rows = jnp.zeros((nt, ch, step), F32)

    @pl.when(jnp.logical_not(down))
    def _():
        af[0] = no_rows

    @pl.when(jnp.logical_not(up))
    def _():
        af[own + 1] = no_rows

    for q in range(own + 2):
        for kind in range(2):
            ab[kind, 0, q, :, :, :step] = jnp.zeros((2, ch, step), BF)
            if q <= own:
                mb[kind, q, :, :, :2 * step] = jnp.zeros((2, ch, 2 * step), BF)

    def pass_on(n):
        @pl.when(up)
        def _():
            halo_up(n).start()

        @pl.when(down)
        def _():
            halo_down(n).start()

    for q in (1, own):
        signal_in(0, q).wait_recv()
    pass_on(0)

    for c in weights:
        c.wait()

    def prepare(layer, w, r, bias):
        for a in range(3):
            for k in range(3):
                hi, lo = split(w[a, k].T)
                for i, piece in enumerate((hi, hi, lo)):
                    taps[layer, :, pl.ds((9 * a + 3 * k + i) * ch, ch)] = piece
        hi, lo = split(r[...])
        for i, piece in enumerate((hi, hi, lo)):
            mix[layer, :, pl.ds(i * ch, ch)] = piece
        tall[layer] = jnp.broadcast_to(bias[...], (out_ch, out_ch)).T

    prepare(0, w1, r1, b1)

    for k in (1, 2):
        for q in (1, own):
            signal_in(k, q).wait_recv()
    pass_on(1)

    def keep(ref, kind, q, values, lead, shifted):
        later = None
        for t, value in enumerate(values):
            at = pl.ds((t + lead) * step, step)
            hi, lo = split(value)
            if shifted:
                turned = pltpu.roll(value, 2 * group, 1)
                before = jnp.where(early_half, jnp.zeros_like(turned) if later is None else later, turned)
                later = turned
                ref[kind, 0, q, 0, :, at], ref[kind, 0, q, 1, :, at] = hi, lo
                hi, lo = split(before)
                ref[kind, 1, q, 0, :, at], ref[kind, 1, q, 1, :, at] = hi, lo
            else:
                ref[kind, q, 0, :, at], ref[kind, q, 1, :, at] = hi, lo

    def pair(q):
        keep(ab, 0, q, [af[q, t] for t in range(nt)], 1, True)

    def between(left, right):
        return jnp.where(first_fibre, pltpu.roll(left, step - group, 1), pltpu.roll(right, group, 1))

    def across(r):
        values = [between(af[r, t], af[r + 1, t]) for t in range(nt)]
        for t in range(nt):
            sf[r, :, pl.ds(t * step, step)] = values[t]
        keep(ab, 1, r, values, 1, True)

    def each(values, do):
        def go(i, carry):
            do(pick(i, values))
            return carry

        lax.fori_loop(0, len(values), go, 0)

    def first_operand(r):
        pieces = []
        n = nt * step
        for kind, q in ((0, r), (1, r), (0, r + 1)):
            for early, lanes in ((0, slice(step, step + n)), (1, slice(step, step + n)), (0, slice(0, n))):
                hi, lo = ab[kind, early, q, 0, :, lanes], ab[kind, early, q, 1, :, lanes]
                pieces += [hi, lo, hi]
        return jnp.concatenate(pieces, axis=0)

    def second_operand(p):
        pieces = []
        n = nt * step
        for kind, q in ((0, p), (1, p), (0, p + 1)):
            for k in range(3):
                lanes = slice((2 - k) * step, (2 - k) * step + n)
                hi, lo = mb[kind, q, 0, :, lanes], mb[kind, q, 1, :, lanes]
                pieces += [hi, lo, hi]
        return jnp.concatenate(pieces, axis=0)

    def layer_of(layer, right, base):
        total = jnp.dot(taps[layer], right, preferred_element_type=F32)
        pre = total + jnp.concatenate([tall[layer]] * (total.shape[1] // out_ch), axis=1)
        g = jnp.tanh(pre[:ch]) * (0.5 * jnp.tanh(0.5 * pre[ch:]) + 0.5)
        hi, lo = split(g)
        return base + jnp.dot(mix[layer], jnp.concatenate([hi, lo, hi], axis=0), preferred_element_type=F32)

    def middle(rows):
        value = layer_of(
            0, jnp.concatenate([first_operand(r) for r in rows], axis=1), jnp.concatenate([sf[r] for r in rows], axis=1)
        )
        for i, r in enumerate(rows):
            parts = [value[:, (i * nt + t) * step:(i * nt + t + 1) * step] for t in range(nt)]
            if r in (0, own):
                ok = down if r == 0 else up
                outside = first_fibre if r == 0 else jnp.logical_not(first_fibre)
                parts = [jnp.where(outside & jnp.logical_not(ok), 0.0, v) for v in parts]
            for t in range(nt):
                mf[r, t] = parts[t]
            keep(mb, 0, r, parts, 2, False)

    def features(ps):
        bases = []
        for p in ps:
            values = [between(mf[p, t], mf[p + 1, t]) for t in range(nt)]
            keep(mb, 1, p, values, 2, False)
            bases += values
        value = layer_of(1, jnp.concatenate([second_operand(p) for p in ps], axis=1), jnp.concatenate(bases, axis=1))
        for i, p in enumerate(ps):
            for t in range(nt):
                v = value[:, (i * nt + t) * step:(i * nt + t + 1) * step]
                fs[p, t] = v

                @pl.when(T == t)
                def _(v=v, p=p, t=t):
                    fr[p, t] = v
        for k in (1, 2, 0):
            for p in ps:
                feature_out(k, p).start()

    prepare(1, w2, r2, b2)
    each([1, own], pair)
    for q in inner:
        for k in range(3):
            signal_in(k, q).wait_recv()
    each(inner, pair)
    each(list(range(1, own)), across)
    middle(list(range(1, own)))
    features(list(range(1, own - 1)))

    for n in range(2):
        @pl.when(down)
        def _(n=n):
            halo_up(n).wait_recv()

        @pl.when(up)
        def _(n=n):
            halo_down(n).wait_recv()
    each([0, own + 1], pair)
    each([0, own], across)
    middle([0, own])
    features([0, own - 1])

    def finish(i, carry):
        p = pick(i, list(range(1, own - 1)) + [0, own - 1])
        for k in range(3):
            feature_in(k, p).wait_recv()
        for n, value in enumerate(swap([fr[p, t] for t in range(nt)])):
            out_ref[pl.ds(n // 2 * fib + 2 * p + n % 2, ch, stride=fib * 2), :] = value
        return carry

    lax.fori_loop(0, own, finish, 0)

    for k in range(3):
        for q in range(1, own + 1):
            signal_out(k, q).wait_send()
            feature_out(k, q - 1).wait_send()
    for n in range(2):
        @pl.when(up)
        def _(n=n):
            halo_up(n).wait_send()

        @pl.when(down)
        def _(n=n):
            halo_down(n).wait_send()


def solution(mesh):
    nt, nf = mesh.shape["tm"], mesh.shape["fibre"]
    placed = (P(None, "fibre", "tm"), P(), P(), P(), P(), P(), P())

    def body(signal, w1, b1, r1, w2, b2, r2):
        ch, fib, length = signal.shape
        assert length == DILATION_TWO == 2 * DILATION_ONE and nt % 2 == 0 and fib == FIB_DEV
        x = signal.reshape(ch, fib, length // 128, 128).transpose(0, 2, 1, 3).reshape(-1, 128)
        out_ch = w1.shape[2]
        own = fib // 2
        w1, w2 = jnp.transpose(w1, (0, 1, 3, 2)), jnp.transpose(w2, (0, 1, 3, 2))
        b1 = b1.reshape(1, out_ch)
        b2 = b2.reshape(1, out_ch)
        dma = lambda n: pltpu.SemaphoreType.DMA((n,))
        inputs = [
            pltpu.VMEM(x.shape, F32),
            pltpu.VMEM(w1.shape, F32), pltpu.VMEM(b1.shape, F32), pltpu.VMEM(r1.shape, F32),
            pltpu.VMEM(w2.shape, F32), pltpu.VMEM(b2.shape, F32), pltpu.VMEM(r2.shape, F32),
            pltpu.VMEM((2, out_ch, 27 * ch), BF), pltpu.VMEM((2, ch, 3 * ch), BF),
            pltpu.VMEM((2, out_ch, out_ch), F32),
        ]
        step = DILATION_ONE
        if nt == 4:
            form = spread_kernel
            scratch = inputs + [
                pltpu.VMEM((nt, own, ch, step), F32), pltpu.VMEM((own + 2, nt, ch, step), F32),
                pltpu.VMEM((own + 1, ch, nt * step), F32),
                pltpu.VMEM((2, 2, own + 2, 2, ch, (nt + 1) * step), BF),
                pltpu.VMEM((own + 1, nt, ch, step), F32),
                pltpu.VMEM((2, own + 1, 2, ch, (nt + 2) * step), BF),
                pltpu.VMEM((own, nt, ch, step), F32), pltpu.VMEM((own, nt, ch, step), F32),
                dma(1), dma(6), dma(3 * own), dma(3 * own), dma(4), dma(4), dma(3 * own), dma(3 * own),
            ]
        else:
            form = kernel
            scratch = [
                pltpu.VMEM((2, 4, own + 2, ch, 2 * length), F32),
                pltpu.VMEM((2, own + 2, 4 * length // step, 2, ch, 2 * step), BF),
            ] + inputs + [
                dma(1), dma(6), dma(2), dma(2), dma(2), dma(2), dma(own + 2), dma(own + 2),
                dma(own + 2), dma(own + 2), dma(own + 2), dma(own + 2),
                dma(own + 1), dma(own + 1), dma(3), dma(3),
                pltpu.SemaphoreType.REGULAR,
            ]
        out = pl.pallas_call(
            lambda *refs: form(nt, nf, fib, *refs),
            name="gated_layers",
            out_shape=pltpu.VMEM(x.shape, F32),
            in_specs=[pl.BlockSpec(memory_space=pl.ANY)] * 7,
            out_specs=pl.BlockSpec(memory_space=pltpu.VMEM),
            scratch_shapes=scratch,
            compiler_params=pltpu.CompilerParams(
                collective_id=0, has_side_effects=True, vmem_limit_bytes=60 * 1024 * 1024
            ),
        )(x, w1, b1, r1, w2, b2, r2)
        out = out.reshape(ch, length // 128, fib, 128).transpose(0, 2, 1, 3)
        return out.reshape(ch, fib, length)

    return jax.shard_map(body, mesh=mesh, in_specs=placed, out_specs=P(None, "fibre", "tm"), check_vma=False)
```

```python
import jax
import jax.numpy as jnp
from jax import lax
from jax.experimental import pallas as pl
from jax.experimental.pallas import tpu as pltpu
from jax.sharding import PartitionSpec as P

DILATION_ONE = 128
DILATION_TWO = 256
FIB_DEV = 8
BF = jnp.bfloat16
F32 = jnp.float32


def split(value):
    hi = value.astype(BF)
    return hi, (value - hi.astype(F32)).astype(BF)


def pick(i, values):
    out = jnp.int32(values[-1])
    for n in range(len(values) - 2, -1, -1):
        out = jnp.where(i == n, jnp.int32(values[n]), out)
    return out


def kernel(
    nt, nf, fib,
    x_hbm, w1_hbm, b1_hbm, r1_hbm, w2_hbm, b2_hbm, r2_hbm, out_ref,
    af, ab, xv, w1, b1, r1, w2, b2, r2, taps, mix, tall,
    in_sem, w_sem, h0s, h0r, h2s, h2r, xs, xr, ps, pr, ts, tr, ms, mr, es, er, go,
):
    s, m = af.at[0], af.at[1]
    T = lax.axis_index("tm")
    F = lax.axis_index("fibre")
    odd = lax.rem(T, 2)
    even = odd == 0
    isodd = odd == 1
    late = T >= 2
    partner = T + 1 - 2 * odd
    ch, length = af.shape[3], af.shape[4] // 2
    own = fib // 2
    wide = own + 2
    mid = own + 1
    out_ch = 2 * ch
    step = DILATION_ONE
    far = nt > 4
    up, down = F + 1 < nf, F > 0
    onward = T + 2 < nt
    inner = list(range(1, own + 1))
    arrive = [1, own] + list(range(2, own))
    edges = [0, own + 1]

    def dev(t, f):
        return {"tm": t, "fibre": f}

    load = pltpu.make_async_copy(x_hbm, xv, in_sem.at[0])
    load.start()
    weights = [
        pltpu.make_async_copy(a, b, w_sem.at[i])
        for i, (a, b) in enumerate(
            [(w1_hbm, w1), (b1_hbm, b1), (r1_hbm, r1), (w2_hbm, w2), (b2_hbm, b2), (r2_hbm, r2)]
        )
    ]
    for c in weights:
        c.start()

    barrier = pltpu.get_barrier_semaphore()
    friends = [(partner, F, None), (T, F + 1, up), (T, F - 1, down), (T + 2, F, onward), (T - 2, F, late)]
    if far:
        send3 = isodd & (T + 3 < nt)
        recv3 = even & (T >= 4)
        for e, ok in ((0, None), (1, up), (-1, down)):
            for d, okt in ((3, send3), (-3, recv3)):
                friends.append((T + d, F + e, okt if ok is None else okt & ok))
    count = jnp.int32(0)
    for t, f, ok in friends:
        if ok is None:
            pl.semaphore_signal(barrier, inc=1, device_id=dev(t, f), device_id_type=pl.DeviceIdType.MESH)
            count = count + 1
        else:
            @pl.when(ok)
            def _(t=t, f=f):
                pl.semaphore_signal(barrier, inc=1, device_id=dev(t, f), device_id_type=pl.DeviceIdType.MESH)
            count = count + ok.astype(jnp.int32)

    load.wait()
    for f in range(fib):
        for h in range(2):
            value = xv[pl.ds(h * fib + f, ch, stride=fib * 2), :]
            lanes = pl.ds((f % 2) * step, step)
            af[0, 0, 1 + f // 2, :, pl.ds((2 * h + f % 2) * step, step)] = value
            hi, lo = split(value)
            ab[0, 1 + f // 2, 6 + h, 0, :, lanes] = hi
            ab[0, 1 + f // 2, 6 + h, 1, :, lanes] = lo
    pl.semaphore_wait(barrier, count)

    def remote(src, dst, ssem, rsem, t, f):
        return pltpu.make_async_remote_copy(
            src_ref=src, dst_ref=dst, send_sem=ssem, recv_sem=rsem,
            device_id=dev(t, f), device_id_type=pl.DeviceIdType.MESH,
        )

    def halo_up(j, ss, rr):
        return remote(s.at[j, own], s.at[j, 0], ss.at[0], rr.at[0], T, F + 1)

    def halo_down(j, ss, rr):
        return remote(s.at[j, 1], s.at[j, own + 1], ss.at[1], rr.at[1], T, F - 1)

    def cross(q):
        return remote(s.at[0, q], s.at[2, q], xs.at[q], xr.at[q], T + 2, F)

    def part(src, q):
        return remote(s.at[src, q], s.at[1, q], ps.at[q], pr.at[q], partner, F)

    def part3(q):
        return remote(s.at[2, q], s.at[3, q], ts.at[q], tr.at[q], partner, F)

    def share(src, r):
        return remote(m.at[src, r], m.at[1, r], ms.at[r], mr.at[r], partner, F)

    @pl.when(onward & even)
    def _():
        for q in arrive:
            cross(q).start()

    @pl.when(up)
    def _():
        halo_up(0, h0s, h0r).start()

    @pl.when(down)
    def _():
        halo_down(0, h0s, h0r).start()

    @pl.when(even)
    def _():
        for q in arrive:
            part(0, q).start()

    if far:
        def third(i, e):
            if e == 0:
                src, dst = s.at[0, pl.ds(1, own)], s.at[3, pl.ds(1, own)]
            elif e == 1:
                src, dst = s.at[0, own], s.at[3, 0]
            else:
                src, dst = s.at[0, 1], s.at[3, own + 1]
            return remote(src, dst, es.at[i], er.at[i], T + 3, F + e)

        thirds_list = [(0, 0, None, None), (1, 1, up, down), (2, -1, down, up)]
        for i, e, ok, _ok in thirds_list:
            @pl.when(send3 if ok is None else send3 & ok)
            def _(i=i, e=e):
                third(i, e).start()

    zero = jnp.zeros(af.shape[3:], F32)

    def zero_halo(j):
        @pl.when(jnp.logical_not(down))
        def _():
            af[0, j, 0] = zero

        @pl.when(jnp.logical_not(up))
        def _():
            af[0, j, own + 1] = zero

    zero_halo(0)

    def no_chunks(layer, first, n):
        for q in range(wide if layer == 0 else mid):
            ab[layer, q, pl.ds(first, n)] = jnp.zeros((n,) + ab.shape[3:], BF)

    @pl.when(T == 0)
    def _():
        no_chunks(0, 4, 2)
        no_chunks(1, 4, 2)

    @pl.when(T < 2)
    def _():
        no_chunks(1, 2, 2)

    @pl.when(T == 2)
    def _():
        no_chunks(0, 0, 2)

    @pl.when(late)
    def _():
        zero_halo(2)

    if far:
        @pl.when(recv3)
        def _():
            zero_halo(3)

    for c in weights:
        c.wait()

    def prepare(layer, w, r, bias):
        for a in range(3):
            for k in range(3):
                hi, lo = split(w[a, k].T)
                for i, piece in enumerate((hi, hi, lo)):
                    taps[layer, :, pl.ds((9 * a + 3 * k + i) * ch, ch)] = piece
        hi, lo = split(r[...])
        for i, piece in enumerate((hi, hi, lo)):
            mix[layer, :, pl.ds(i * ch, ch)] = piece
        tall[layer] = jnp.broadcast_to(bias[...], (out_ch, out_ch)).T

    prepare(0, w1, r1, b1)
    prepare(1, w2, r2, b2)

    def ingest(layer, j, q):
        hi, lo = split(af[layer, j, q])
        for h in range(2):
            ab[layer, q, 2 * (3 - j) + h, 0] = hi[:, h * 2 * step:(h + 1) * 2 * step]
            ab[layer, q, 2 * (3 - j) + h, 1] = lo[:, h * 2 * step:(h + 1) * 2 * step]

    @pl.when(onward & even)
    def _():
        for q in arrive[:-1]:
            cross(q).wait_send()
        pl.semaphore_signal(go, inc=1, device_id=dev(partner, F), device_id_type=pl.DeviceIdType.MESH)

    @pl.when(onward & isodd)
    def _():
        pl.semaphore_wait(go, 1)
        for q in arrive:
            cross(q).start()

    if far:
        @pl.when(recv3)
        def _():
            for i, e, _ok, ok in thirds_list:
                if ok is None:
                    third(i, e).wait_recv()
                else:
                    @pl.when(ok)
                    def _(i=i, e=e):
                        third(i, e).wait_recv()

            def old(q, carry):
                ingest(0, 3, q)
                return carry

            lax.fori_loop(0, wide, old, 0)

    late_even, late_odd = late & even, late & isodd

    def halos_in(j, ss, rr):
        @pl.when(down)
        def _():
            halo_up(j, ss, rr).wait_recv()

        @pl.when(up)
        def _():
            halo_down(j, ss, rr).wait_recv()

    def crossed(q):
        cross(q).wait_recv()

        @pl.when(even)
        def _():
            part3(q).start()

        @pl.when(isodd)
        def _():
            part(2, q).start()

        if q == 1:
            @pl.when(down)
            def _():
                halo_down(2, h2s, h2r).start()

        if q == own:
            @pl.when(up)
            def _():
                halo_up(2, h2s, h2r).start()

    def event(i):
        if i == 0:
            @pl.when(late_even)
            def _():
                for q in arrive:
                    crossed(q)

            @pl.when(isodd)
            def _():
                for q in arrive:
                    part(0, q).wait_recv()
        if i == 1:
            @pl.when(late_odd)
            def _():
                crossed(arrive[0])

            halos_in(0, h0s, h0r)

            @pl.when(even)
            def _():
                for q in edges:
                    part(0, q).start()

            @pl.when(isodd)
            def _():
                for q in edges:
                    part(0, q).wait_recv()

            @pl.when(late_even)
            def _():
                halos_in(2, h2s, h2r)
                for q in edges:
                    part3(q).start()
        if i in (2, 3):
            now = arrive[:-1] if i == 2 else arrive[-1:]

            @pl.when(late_even)
            def _():
                for q in now:
                    part(0, q).wait_recv()

            @pl.when(late_odd)
            def _():
                for q in now:
                    if q != arrive[0]:
                        crossed(q)
                for q in now:
                    part3(q).wait_recv()
        if i == 4:
            @pl.when(late_even)
            def _():
                for q in edges:
                    part(0, q).wait_recv()

            @pl.when(late_odd)
            def _():
                halos_in(2, h2s, h2r)
                for q in edges:
                    part(2, q).start()
                for q in edges:
                    part3(q).wait_recv()
        if i == 5:
            @pl.when(T >= 1)
            def _():
                for r in range(1, own):
                    share(0, r).wait_recv()
        if i == 6:
            @pl.when(T >= 1)
            def _():
                for r in (0, own):
                    share(0, r).wait_recv()

    rows = [
        (("A", 1), ("A", 2)), (("A", 3), ("A", 0)), (("A", own), ("B", 1)), (("B", 2), ("B", 3)), (("B", 0), ("B", own)),
        (("C", 1), ("C", 2)), (("C", 0), ("C", own - 1)),
    ]
    steps = len(rows)
    first_of_two = steps - 2
    ja = jnp.where(late_even, 2, 0)
    jb = jnp.where(even, 0, 2)
    start = [1, 0, 1, 3, 0, 1, 0]
    number = [own, 2, 2, own - 2, 2, own - 1, 2]
    stride = [1, own + 1, 1, 1, own + 1, 1, own]
    le = [(2,), (0, 2), (1,), (1,), (1,), (1,), (1,)]
    lo_ = [(1,), (0, 1), (2, 3), (2, 3), (2, 3), (1,), (1,)]
    ee = [(), (0,), (), (), (), (), ()]
    eo = [(1,), (0, 1), (), (), (), (1,), (1,)]

    def by_class(i, of):
        table = [pick(i, [of(entry) for entry in c]) for c in (le, lo_, ee, eo)]
        return jnp.where(late, jnp.where(even, table[0], table[1]), jnp.where(even, table[2], table[3]))

    def operand(layer, r, b, d):
        pieces = []
        for a in range(3):
            for k in range(3):
                both = []
                for part_ in range(2):
                    cols = []
                    for h in range(2):
                        c = 2 * b + h - k * d
                        if a == 0:
                            cols.append(ab[layer, r, c, part_])
                        elif a == 2:
                            cols.append(ab[layer, r + 1, c, part_])
                        else:
                            cols += [ab[layer, r, c, part_, :, step:], ab[layer, r + 1, c, part_, :, :step]]
                    both.append(jnp.concatenate(cols, axis=1))
                pieces += [both[0], both[1], both[0]]
        return jnp.concatenate(pieces, axis=0)

    def straddle(layer, j, r):
        cols = []
        for h in range(2):
            cols += [af[layer, j, r, :, (2 * h + 1) * step:(2 * h + 2) * step], af[layer, j, r + 1, :, 2 * h * step:(2 * h + 1) * step]]
        return jnp.concatenate(cols, axis=1)

    def compute(layer, d, units):
        right = jnp.concatenate([operand(layer, r, 3 - j, d) for r, j in units], axis=1)
        total = jnp.dot(taps[layer], right, preferred_element_type=F32)
        pre = total + jnp.concatenate([tall[layer]] * (total.shape[1] // out_ch), axis=1)
        g = jnp.tanh(pre[:ch]) * (0.5 * jnp.tanh(0.5 * pre[ch:]) + 0.5)
        hi, lo = split(g)
        base = jnp.concatenate([straddle(layer, j, r) for r, j in units], axis=1)
        return base + jnp.dot(mix[layer], jnp.concatenate([hi, lo, hi], axis=0), preferred_element_type=F32)

    def body(i, carry):
        for n in range(steps):
            @pl.when(i == n)
            def _(n=n):
                event(n)

        first, each, pace = pick(i, start), pick(i, number), pick(i, stride)
        j0 = by_class(i, lambda e: e[0] if e else 0)
        j1 = by_class(i, lambda e: e[1] if len(e) > 1 else 0)
        blocks = by_class(i, len)
        layer = (i >= first_of_two).astype(jnp.int32)

        def take(n, carry):
            second = n >= each
            q = first + pace * jnp.where(second, n - each, n)
            ingest(layer, jnp.where(second, j1, j0), q)
            return carry

        lax.fori_loop(0, each * blocks, take, 0)

        units = []
        for lane in range(2):
            r = pick(i, [pair[lane][1] for pair in rows])
            kind = pick(i, ["ABC".index(pair[lane][0]) for pair in rows])
            if any(pair[lane][0] == "B" and pair[0][0] == "A" for pair in rows):
                r = jnp.where((kind == 1) & jnp.logical_not(late), own, r)
            j = jnp.where(kind == 0, ja, jnp.where(kind == 1, jnp.where(late, jb, 0), 0))
            units.append((r, j, kind))

        @pl.when(late | (i < 3) | (i >= first_of_two))
        def _():
            value = compute(layer, layer + 1, [(r, j) for r, j, _ in units])

            @pl.when(layer == 0)
            def _():
                for n, (r, j, kind) in enumerate(units):
                    v = value[:, n * 2 * length:(n + 1) * 2 * length]
                    row = F * fib + 2 * r - 1
                    ok = [(row >= 0) & (row < nf * fib), (row + 1 >= 0) & (row + 1 < nf * fib)]
                    v = jnp.concatenate([jnp.where(ok[p % 2], v[:, p * step:(p + 1) * step], 0.0) for p in range(4)], axis=1)
                    af[1, j, r] = v
                    hi, lo = split(v)
                    for h in range(2):
                        ab[1, r, 2 * (3 - j) + h, 0] = hi[:, h * 2 * step:(h + 1) * 2 * step]
                        ab[1, r, 2 * (3 - j) + h, 1] = lo[:, h * 2 * step:(h + 1) * 2 * step]

                for r, j, kind in units:
                    @pl.when((late & (kind == 1)) | ((T == 0) & (kind == 0)))
                    def _(r=r, j=j):
                        share(j, r).start()

            @pl.when(layer == 1)
            def _():
                for n, (r, j, kind) in enumerate(units):
                    for p in range(4):
                        h, e = p // 2, p % 2
                        at = n * 2 * length + p * step
                        out_ref[pl.ds(h * fib + 2 * r + e, ch, stride=fib * 2), :] = value[:, at:at + step]
        return carry

    lax.fori_loop(0, steps, body, 0)

    @pl.when(onward & even)
    def _():
        cross(arrive[-1]).wait_send()

    @pl.when(onward & isodd)
    def _():
        for q in arrive:
            cross(q).wait_send()

    for j, ss, rr, ok in ((0, h0s, h0r, None), (2, h2s, h2r, late)):
        @pl.when(up if ok is None else up & ok)
        def _(j=j, ss=ss, rr=rr):
            halo_up(j, ss, rr).wait_send()

        @pl.when(down if ok is None else down & ok)
        def _(j=j, ss=ss, rr=rr):
            halo_down(j, ss, rr).wait_send()

    for q in range(wide):
        @pl.when(even | late)
        def _(q=q):
            part(0, q).wait_send()

        @pl.when(late_even)
        def _(q=q):
            part3(q).wait_send()

    @pl.when(even | late)
    def _():
        for r in range(mid):
            share(0, r).wait_send()

    if far:
        for i, e, ok, _ok in thirds_list:
            @pl.when(send3 if ok is None else send3 & ok)
            def _(i=i, e=e):
                third(i, e).wait_send()


def spread_kernel(
    nt, nf, fib,
    x_hbm, w1_hbm, b1_hbm, r1_hbm, w2_hbm, b2_hbm, r2_hbm, out_ref,
    xv, w1, b1, r1, w2, b2, r2, taps, mix, tall, pk, af, sf, ab, mf, mb, fs, fr,
    in_sem, w_sem, xs, xr, hs, hr, gs, gr,
):
    T = lax.axis_index("tm")
    F = lax.axis_index("fibre")
    odd = lax.rem(T, 2)
    partner = T + 1 - 2 * odd
    peers = [partner, lax.rem(T + 2, nt), lax.rem(partner + 2, nt)]
    chip = T - odd
    other = lax.rem(chip + 2, nt)
    ch = pk.shape[2]
    own = fib // 2
    out_ch = 2 * ch
    step = DILATION_ONE
    group = step // nt
    up, down = F + 1 < nf, F > 0
    inner = list(range(2, own))
    lane = lax.broadcasted_iota(jnp.int32, (ch, step), 1)
    early_half = lane < 2 * group
    first_fibre = lax.rem(lane, 2 * group) < group

    def dev(t, f):
        return {"tm": t, "fibre": f}

    load = pltpu.make_async_copy(x_hbm, xv, in_sem.at[0])
    load.start()
    weights = [
        pltpu.make_async_copy(a, b, w_sem.at[i])
        for i, (a, b) in enumerate(
            [(w1_hbm, w1), (b1_hbm, b1), (r1_hbm, r1), (w2_hbm, w2), (b2_hbm, b2), (r2_hbm, r2)]
        )
    ]
    for c in weights:
        c.start()

    barrier = pltpu.get_barrier_semaphore()
    for p in peers:
        pl.semaphore_signal(barrier, inc=1, device_id=dev(p, F), device_id_type=pl.DeviceIdType.MESH)
    count = jnp.int32(len(peers))
    for e, ok in ((1, up), (-1, down)):
        @pl.when(ok)
        def _(e=e):
            pl.semaphore_signal(barrier, inc=1, device_id=dev(T, F + e), device_id_type=pl.DeviceIdType.MESH)
        count = count + ok.astype(jnp.int32)

    def swap(parts):
        a, b, c, d = parts
        half = 2 * group
        a, c = jnp.where(early_half, a, pltpu.roll(c, half, 1)), jnp.where(early_half, pltpu.roll(a, half, 1), c)
        b, d = jnp.where(early_half, b, pltpu.roll(d, half, 1)), jnp.where(early_half, pltpu.roll(b, half, 1), d)
        back = step - group
        a, b = jnp.where(first_fibre, a, pltpu.roll(b, group, 1)), jnp.where(first_fibre, pltpu.roll(a, back, 1), b)
        c, d = jnp.where(first_fibre, c, pltpu.roll(d, group, 1)), jnp.where(first_fibre, pltpu.roll(c, back, 1), d)
        return a, b, c, d

    load.wait()

    def pack(q, carry):
        parts = [xv[pl.ds(h * fib + 2 * q + e, ch, stride=fib * 2), :] for h in range(2) for e in range(2)]
        for t, value in enumerate(swap(parts)):
            pk[t, q] = value

            @pl.when(T == t)
            def _(value=value):
                af[q + 1, t] = value
        return carry

    lax.fori_loop(0, own, pack, 0)
    pl.semaphore_wait(barrier, count)

    def remote(src, dst, ssem, rsem, t, f):
        return pltpu.make_async_remote_copy(
            src_ref=src, dst_ref=dst, send_sem=ssem, recv_sem=rsem,
            device_id=dev(t, f), device_id_type=pl.DeviceIdType.MESH,
        )

    def signal_out(k, q):
        n = k * own + q - 1
        return remote(pk.at[peers[k], q - 1], af.at[q, T], xs.at[n], xr.at[n], peers[k], F)

    def signal_in(k, q):
        n = k * own + q - 1
        return remote(pk.at[peers[k], q - 1], af.at[q, peers[k]], xs.at[n], xr.at[n], peers[k], F)

    def halo_up(n):
        blocks = pl.ds((chip, other)[n], 2)
        return remote(af.at[own, blocks], af.at[0, blocks], hs.at[2 * n], hr.at[2 * n], T, F + 1)

    def halo_down(n):
        blocks = pl.ds((chip, other)[n], 2)
        return remote(af.at[1, blocks], af.at[own + 1, blocks], hs.at[2 * n + 1], hr.at[2 * n + 1], T, F - 1)

    def feature_out(k, p):
        n = k * own + p
        return remote(fs.at[p, peers[k]], fr.at[p, T], gs.at[n], gr.at[n], peers[k], F)

    def feature_in(k, p):
        n = k * own + p
        return remote(fs.at[p, peers[k]], fr.at[p, peers[k]], gs.at[n], gr.at[n], peers[k], F)

    for q in range(1, own + 1):
        signal_out(1, q).start()
        signal_out(2, q).start()
        if q == 1:
            for near in [1, own] + inner:
                signal_out(0, near).start()

    no_rows = jnp.zeros((nt, ch, step), F32)

    @pl.when(jnp.logical_not(down))
    def _():
        af[0] = no_rows

    @pl.when(jnp.logical_not(up))
    def _():
        af[own + 1] = no_rows

    for q in range(own + 2):
        for kind in range(2):
            ab[kind, 0, q, :, :, :step] = jnp.zeros((2, ch, step), BF)
            if q <= own:
                mb[kind, q, :, :, :2 * step] = jnp.zeros((2, ch, 2 * step), BF)

    for q in (1, own):
        signal_in(0, q).wait_recv()

    @pl.when(up)
    def _():
        halo_up(0).start()

    @pl.when(down)
    def _():
        halo_down(0).start()

    for c in weights:
        c.wait()

    def prepare(layer, w, r, bias):
        for a in range(3):
            for k in range(3):
                hi, lo = split(w[a, k].T)
                for i, piece in enumerate((hi, hi, lo)):
                    taps[layer, :, pl.ds((9 * a + 3 * k + i) * ch, ch)] = piece
        hi, lo = split(r[...])
        for i, piece in enumerate((hi, hi, lo)):
            mix[layer, :, pl.ds(i * ch, ch)] = piece
        tall[layer] = jnp.broadcast_to(bias[...], (out_ch, out_ch)).T

    prepare(0, w1, r1, b1)
    prepare(1, w2, r2, b2)

    def keep(ref, kind, q, values, lead, shifted):
        later = None
        for t, value in enumerate(values):
            at = pl.ds((t + lead) * step, step)
            hi, lo = split(value)
            if shifted:
                turned = pltpu.roll(value, 2 * group, 1)
                before = jnp.where(early_half, jnp.zeros_like(turned) if later is None else later, turned)
                later = turned
                ref[kind, 0, q, 0, :, at], ref[kind, 0, q, 1, :, at] = hi, lo
                hi, lo = split(before)
                ref[kind, 1, q, 0, :, at], ref[kind, 1, q, 1, :, at] = hi, lo
            else:
                ref[kind, q, 0, :, at], ref[kind, q, 1, :, at] = hi, lo

    def pair(q):
        keep(ab, 0, q, [af[q, t] for t in range(nt)], 1, True)

    def between(left, right):
        return jnp.where(first_fibre, pltpu.roll(left, step - group, 1), pltpu.roll(right, group, 1))

    def across(r):
        values = [between(af[r, t], af[r + 1, t]) for t in range(nt)]
        for t in range(nt):
            sf[r, :, pl.ds(t * step, step)] = values[t]
        keep(ab, 1, r, values, 1, True)

    def first_operand(r):
        pieces = []
        n = nt * step
        for kind, q in ((0, r), (1, r), (0, r + 1)):
            for early, lanes in ((0, slice(step, step + n)), (1, slice(step, step + n)), (0, slice(0, n))):
                hi, lo = ab[kind, early, q, 0, :, lanes], ab[kind, early, q, 1, :, lanes]
                pieces += [hi, lo, hi]
        return jnp.concatenate(pieces, axis=0)

    def second_operand(p, first):
        pieces = []
        for kind, q in ((0, p), (1, p), (0, p + 1)):
            for k in range(3):
                lanes = pl.ds(pl.multiple_of((2 - k + first) * step, step), 2 * step)
                hi, lo = mb[kind, q, 0, :, lanes], mb[kind, q, 1, :, lanes]
                pieces += [hi, lo, hi]
        return jnp.concatenate(pieces, axis=0)

    def layer_of(layer, right, base):
        total = jnp.dot(taps[layer], right, preferred_element_type=F32)
        pre = total + jnp.concatenate([tall[layer]] * (total.shape[1] // out_ch), axis=1)
        g = jnp.tanh(pre[:ch]) * (0.5 * jnp.tanh(0.5 * pre[ch:]) + 0.5)
        hi, lo = split(g)
        return base + jnp.dot(mix[layer], jnp.concatenate([hi, lo, hi], axis=0), preferred_element_type=F32)

    def middle(r):
        value = layer_of(0, first_operand(r), sf[r])
        row = F * fib + 2 * r - 1
        ok = [((f >= 0) & (f < nf * fib)).astype(jnp.int32) for f in (row, row + 1)]
        inside = jnp.where(first_fibre, ok[0], ok[1]) == 1
        parts = [jnp.where(inside, value[:, t * step:(t + 1) * step], 0.0) for t in range(nt)]
        for t in range(nt):
            mf[r, t] = parts[t]
        keep(mb, 0, r, parts, 2, False)

    def two_blocks(p, first):
        return sf[p, :, pl.ds(pl.multiple_of(first * step, step), 2 * step)]

    def away(p):
        values = [between(mf[p, t], mf[p + 1, t]) for t in range(nt)]
        keep(mb, 1, p, values, 2, False)
        for t in range(nt):
            sf[p, :, pl.ds(t * step, step)] = values[t]
        value = layer_of(1, second_operand(p, other), two_blocks(p, other))
        for t in range(2):
            fs[p, other + t] = value[:, t * step:(t + 1) * step]
        for k in (1, 2):
            feature_out(k, p).start()

    def home(ps):
        value = layer_of(
            1,
            jnp.concatenate([second_operand(p, chip) for p in ps], axis=1),
            jnp.concatenate([two_blocks(p, chip) for p in ps], axis=1),
        )
        for i, p in enumerate(ps):
            parts = [value[:, (2 * i + t) * step:(2 * i + t + 1) * step] for t in range(2)]
            fs[p, partner] = jnp.where(odd == 1, parts[0], parts[1])
            fr[p, T] = jnp.where(odd == 1, parts[1], parts[0])
            feature_out(0, p).start()

    pairs = list(range(1, own + 2)) + [0]
    rows = [0] + list(range(1, own + 1)) + [0]
    outs = [0, 0] + list(range(1, own)) + [0]

    def body(i, carry):
        q, r, p = pick(i, pairs), pick(i, rows), pick(i, outs)

        @pl.when(i < own)
        def _():
            for k in range(3):
                @pl.when((k > 0) | ((q != 1) & (q != own)))
                def _(k=k):
                    signal_in(k, q).wait_recv()

        @pl.when((q == 1) & down)
        def _():
            halo_down(1).start()

        @pl.when((q == own) & up)
        def _():
            halo_up(1).start()

        @pl.when((q == own + 1) & up)
        def _():
            for n in range(2):
                halo_down(n).wait_recv()

        @pl.when((q == 0) & down)
        def _():
            for n in range(2):
                halo_up(n).wait_recv()

        pair(q)

        @pl.when(i >= 1)
        def _():
            across(r)
            middle(r)

        @pl.when(i >= 2)
        def _():
            away(p)
        return carry

    lax.fori_loop(0, own + 2, body, 0)
    home(list(range(own)))

    def finish(i, carry):
        p = lax.rem(i + 1, own)
        for k in range(3):
            feature_in(k, p).wait_recv()
        for n, value in enumerate(swap([fr[p, t] for t in range(nt)])):
            out_ref[pl.ds(n // 2 * fib + 2 * p + n % 2, ch, stride=fib * 2), :] = value
        return carry

    lax.fori_loop(0, own, finish, 0)

    for k in range(3):
        for q in range(1, own + 1):
            signal_out(k, q).wait_send()
            feature_out(k, q - 1).wait_send()
    for n in range(2):
        @pl.when(up)
        def _(n=n):
            halo_up(n).wait_send()

        @pl.when(down)
        def _(n=n):
            halo_down(n).wait_send()


def solution(mesh):
    nt, nf = mesh.shape["tm"], mesh.shape["fibre"]
    placed = (P(None, "fibre", "tm"), P(), P(), P(), P(), P(), P())

    def body(signal, w1, b1, r1, w2, b2, r2):
        ch, fib, length = signal.shape
        assert length == DILATION_TWO == 2 * DILATION_ONE and nt % 2 == 0 and fib == FIB_DEV
        x = signal.reshape(ch, fib, length // 128, 128).transpose(0, 2, 1, 3).reshape(-1, 128)
        out_ch = w1.shape[2]
        own = fib // 2
        w1, w2 = jnp.transpose(w1, (0, 1, 3, 2)), jnp.transpose(w2, (0, 1, 3, 2))
        b1 = b1.reshape(1, out_ch)
        b2 = b2.reshape(1, out_ch)
        dma = lambda n: pltpu.SemaphoreType.DMA((n,))
        inputs = [
            pltpu.VMEM(x.shape, F32),
            pltpu.VMEM(w1.shape, F32), pltpu.VMEM(b1.shape, F32), pltpu.VMEM(r1.shape, F32),
            pltpu.VMEM(w2.shape, F32), pltpu.VMEM(b2.shape, F32), pltpu.VMEM(r2.shape, F32),
            pltpu.VMEM((2, out_ch, 27 * ch), BF), pltpu.VMEM((2, ch, 3 * ch), BF),
            pltpu.VMEM((2, out_ch, out_ch), F32),
        ]
        step = DILATION_ONE
        if nt == 4:
            form = spread_kernel
            scratch = inputs + [
                pltpu.VMEM((nt, own, ch, step), F32), pltpu.VMEM((own + 2, nt, ch, step), F32),
                pltpu.VMEM((own + 1, ch, nt * step), F32),
                pltpu.VMEM((2, 2, own + 2, 2, ch, (nt + 1) * step), BF),
                pltpu.VMEM((own + 1, nt, ch, step), F32),
                pltpu.VMEM((2, own + 1, 2, ch, (nt + 2) * step), BF),
                pltpu.VMEM((own, nt, ch, step), F32), pltpu.VMEM((own, nt, ch, step), F32),
                dma(1), dma(6), dma(3 * own), dma(3 * own), dma(4), dma(4), dma(3 * own), dma(3 * own),
            ]
        else:
            form = kernel
            scratch = [
                pltpu.VMEM((2, 4, own + 2, ch, 2 * length), F32),
                pltpu.VMEM((2, own + 2, 4 * length // step, 2, ch, 2 * step), BF),
            ] + inputs + [
                dma(1), dma(6), dma(2), dma(2), dma(2), dma(2), dma(own + 2), dma(own + 2),
                dma(own + 2), dma(own + 2), dma(own + 2), dma(own + 2),
                dma(own + 1), dma(own + 1), dma(3), dma(3),
                pltpu.SemaphoreType.REGULAR,
            ]
        out = pl.pallas_call(
            lambda *refs: form(nt, nf, fib, *refs),
            name="gated_layers",
            out_shape=pltpu.VMEM(x.shape, F32),
            in_specs=[pl.BlockSpec(memory_space=pl.ANY)] * 7,
            out_specs=pl.BlockSpec(memory_space=pltpu.VMEM),
            scratch_shapes=scratch,
            compiler_params=pltpu.CompilerParams(
                collective_id=0, has_side_effects=True, vmem_limit_bytes=60 * 1024 * 1024
            ),
        )(x, w1, b1, r1, w2, b2, r2)
        out = out.reshape(ch, length // 128, fib, 128).transpose(0, 2, 1, 3)
        return out.reshape(ch, fib, length)

    return jax.shard_map(body, mesh=mesh, in_specs=placed, out_specs=P(None, "fibre", "tm"), check_vma=False)
```

```python
import jax
import jax.numpy as jnp
from jax import lax
from jax.experimental import pallas as pl
from jax.experimental.pallas import tpu as pltpu
from jax.sharding import PartitionSpec as P

DILATION_ONE = 128
DILATION_TWO = 256
FIB_DEV = 8
BF = jnp.bfloat16
F32 = jnp.float32


def split(value):
    hi = value.astype(BF)
    return hi, (value - hi.astype(F32)).astype(BF)


def pick(i, values):
    out = jnp.int32(values[-1])
    for n in range(len(values) - 2, -1, -1):
        out = jnp.where(i == n, jnp.int32(values[n]), out)
    return out


def kernel(
    nt, nf, fib,
    x_hbm, w1_hbm, b1_hbm, r1_hbm, w2_hbm, b2_hbm, r2_hbm, out_ref,
    af, ab, xv, w1, b1, r1, w2, b2, r2, taps, mix, tall,
    in_sem, w_sem, h0s, h0r, h2s, h2r, xs, xr, ps, pr, ts, tr, ms, mr, es, er, go,
):
    s, m = af.at[0], af.at[1]
    T = lax.axis_index("tm")
    F = lax.axis_index("fibre")
    odd = lax.rem(T, 2)
    even = odd == 0
    isodd = odd == 1
    late = T >= 2
    partner = T + 1 - 2 * odd
    ch, length = af.shape[3], af.shape[4] // 2
    own = fib // 2
    wide = own + 2
    mid = own + 1
    out_ch = 2 * ch
    step = DILATION_ONE
    far = nt > 4
    up, down = F + 1 < nf, F > 0
    onward = T + 2 < nt
    inner = list(range(1, own + 1))
    arrive = [1, own] + list(range(2, own))
    edges = [0, own + 1]

    def dev(t, f):
        return {"tm": t, "fibre": f}

    load = pltpu.make_async_copy(x_hbm, xv, in_sem.at[0])
    load.start()
    weights = [
        pltpu.make_async_copy(a, b, w_sem.at[i])
        for i, (a, b) in enumerate(
            [(w1_hbm, w1), (b1_hbm, b1), (r1_hbm, r1), (w2_hbm, w2), (b2_hbm, b2), (r2_hbm, r2)]
        )
    ]
    for c in weights:
        c.start()

    barrier = pltpu.get_barrier_semaphore()
    friends = [(partner, F, None), (T, F + 1, up), (T, F - 1, down), (T + 2, F, onward), (T - 2, F, late)]
    if far:
        send3 = isodd & (T + 3 < nt)
        recv3 = even & (T >= 4)
        for e, ok in ((0, None), (1, up), (-1, down)):
            for d, okt in ((3, send3), (-3, recv3)):
                friends.append((T + d, F + e, okt if ok is None else okt & ok))
    count = jnp.int32(0)
    for t, f, ok in friends:
        if ok is None:
            pl.semaphore_signal(barrier, inc=1, device_id=dev(t, f), device_id_type=pl.DeviceIdType.MESH)
            count = count + 1
        else:
            @pl.when(ok)
            def _(t=t, f=f):
                pl.semaphore_signal(barrier, inc=1, device_id=dev(t, f), device_id_type=pl.DeviceIdType.MESH)
            count = count + ok.astype(jnp.int32)

    load.wait()
    for f in range(fib):
        for h in range(2):
            value = xv[pl.ds(h * fib + f, ch, stride=fib * 2), :]
            lanes = pl.ds((f % 2) * step, step)
            af[0, 0, 1 + f // 2, :, pl.ds((2 * h + f % 2) * step, step)] = value
            hi, lo = split(value)
            ab[0, 1 + f // 2, 6 + h, 0, :, lanes] = hi
            ab[0, 1 + f // 2, 6 + h, 1, :, lanes] = lo
    pl.semaphore_wait(barrier, count)

    def remote(src, dst, ssem, rsem, t, f):
        return pltpu.make_async_remote_copy(
            src_ref=src, dst_ref=dst, send_sem=ssem, recv_sem=rsem,
            device_id=dev(t, f), device_id_type=pl.DeviceIdType.MESH,
        )

    def halo_up(j, ss, rr):
        return remote(s.at[j, own], s.at[j, 0], ss.at[0], rr.at[0], T, F + 1)

    def halo_down(j, ss, rr):
        return remote(s.at[j, 1], s.at[j, own + 1], ss.at[1], rr.at[1], T, F - 1)

    def cross(q):
        return remote(s.at[0, q], s.at[2, q], xs.at[q], xr.at[q], T + 2, F)

    def part(src, q):
        return remote(s.at[src, q], s.at[1, q], ps.at[q], pr.at[q], partner, F)

    def part3(q):
        return remote(s.at[2, q], s.at[3, q], ts.at[q], tr.at[q], partner, F)

    def share(src, r):
        return remote(m.at[src, r], m.at[1, r], ms.at[r], mr.at[r], partner, F)

    @pl.when(onward & even)
    def _():
        for q in arrive:
            cross(q).start()

    @pl.when(up)
    def _():
        halo_up(0, h0s, h0r).start()

    @pl.when(down)
    def _():
        halo_down(0, h0s, h0r).start()

    @pl.when(even)
    def _():
        for q in arrive:
            part(0, q).start()

    if far:
        def third(i, e):
            if e == 0:
                src, dst = s.at[0, pl.ds(1, own)], s.at[3, pl.ds(1, own)]
            elif e == 1:
                src, dst = s.at[0, own], s.at[3, 0]
            else:
                src, dst = s.at[0, 1], s.at[3, own + 1]
            return remote(src, dst, es.at[i], er.at[i], T + 3, F + e)

        thirds_list = [(0, 0, None, None), (1, 1, up, down), (2, -1, down, up)]
        for i, e, ok, _ok in thirds_list:
            @pl.when(send3 if ok is None else send3 & ok)
            def _(i=i, e=e):
                third(i, e).start()

    zero = jnp.zeros(af.shape[3:], F32)

    def zero_halo(j):
        @pl.when(jnp.logical_not(down))
        def _():
            af[0, j, 0] = zero

        @pl.when(jnp.logical_not(up))
        def _():
            af[0, j, own + 1] = zero

    zero_halo(0)

    def no_chunks(layer, first, n):
        for q in range(wide if layer == 0 else mid):
            ab[layer, q, pl.ds(first, n)] = jnp.zeros((n,) + ab.shape[3:], BF)

    @pl.when(T == 0)
    def _():
        no_chunks(0, 4, 2)
        no_chunks(1, 4, 2)

    @pl.when(T < 2)
    def _():
        no_chunks(1, 2, 2)

    @pl.when(T == 2)
    def _():
        no_chunks(0, 0, 2)

    @pl.when(late)
    def _():
        zero_halo(2)

    if far:
        @pl.when(recv3)
        def _():
            zero_halo(3)

    for c in weights:
        c.wait()

    def prepare(layer, w, r, bias):
        for a in range(3):
            for k in range(3):
                hi, lo = split(w[a, k].T)
                for i, piece in enumerate((hi, hi, lo)):
                    taps[layer, :, pl.ds((9 * a + 3 * k + i) * ch, ch)] = piece
        hi, lo = split(r[...])
        for i, piece in enumerate((hi, hi, lo)):
            mix[layer, :, pl.ds(i * ch, ch)] = piece
        tall[layer] = jnp.broadcast_to(bias[...], (out_ch, out_ch)).T

    prepare(0, w1, r1, b1)
    prepare(1, w2, r2, b2)

    def ingest(layer, j, q):
        hi, lo = split(af[layer, j, q])
        for h in range(2):
            ab[layer, q, 2 * (3 - j) + h, 0] = hi[:, h * 2 * step:(h + 1) * 2 * step]
            ab[layer, q, 2 * (3 - j) + h, 1] = lo[:, h * 2 * step:(h + 1) * 2 * step]

    @pl.when(onward & even)
    def _():
        for q in arrive[:-1]:
            cross(q).wait_send()
        pl.semaphore_signal(go, inc=1, device_id=dev(partner, F), device_id_type=pl.DeviceIdType.MESH)

    @pl.when(onward & isodd)
    def _():
        pl.semaphore_wait(go, 1)
        for q in arrive:
            cross(q).start()

    if far:
        @pl.when(recv3)
        def _():
            for i, e, _ok, ok in thirds_list:
                if ok is None:
                    third(i, e).wait_recv()
                else:
                    @pl.when(ok)
                    def _(i=i, e=e):
                        third(i, e).wait_recv()

            def old(q, carry):
                ingest(0, 3, q)
                return carry

            lax.fori_loop(0, wide, old, 0)

    late_even, late_odd = late & even, late & isodd

    def halos_in(j, ss, rr):
        @pl.when(down)
        def _():
            halo_up(j, ss, rr).wait_recv()

        @pl.when(up)
        def _():
            halo_down(j, ss, rr).wait_recv()

    def crossed(q):
        cross(q).wait_recv()

        @pl.when(even)
        def _():
            part3(q).start()

        @pl.when(isodd)
        def _():
            part(2, q).start()

        if q == 1:
            @pl.when(down)
            def _():
                halo_down(2, h2s, h2r).start()

        if q == own:
            @pl.when(up)
            def _():
                halo_up(2, h2s, h2r).start()

    def event(i):
        if i == 0:
            @pl.when(late_even)
            def _():
                for q in arrive:
                    crossed(q)

            @pl.when(isodd)
            def _():
                for q in arrive:
                    part(0, q).wait_recv()
        if i == 1:
            @pl.when(late_odd)
            def _():
                crossed(arrive[0])

            halos_in(0, h0s, h0r)

            @pl.when(even)
            def _():
                for q in edges:
                    part(0, q).start()

            @pl.when(isodd)
            def _():
                for q in edges:
                    part(0, q).wait_recv()

            @pl.when(late_even)
            def _():
                halos_in(2, h2s, h2r)
                for q in edges:
                    part3(q).start()
        if i in (2, 3):
            now = arrive[:-1] if i == 2 else arrive[-1:]

            @pl.when(late_even)
            def _():
                for q in now:
                    part(0, q).wait_recv()

            @pl.when(late_odd)
            def _():
                for q in now:
                    if q != arrive[0]:
                        crossed(q)
                for q in now:
                    part3(q).wait_recv()
        if i == 4:
            @pl.when(late_even)
            def _():
                for q in edges:
                    part(0, q).wait_recv()

            @pl.when(late_odd)
            def _():
                halos_in(2, h2s, h2r)
                for q in edges:
                    part(2, q).start()
                for q in edges:
                    part3(q).wait_recv()
        if i == 5:
            @pl.when(T >= 1)
            def _():
                for r in range(1, own):
                    share(0, r).wait_recv()
        if i == 6:
            @pl.when(T >= 1)
            def _():
                for r in (0, own):
                    share(0, r).wait_recv()

    rows = [
        (("A", 1), ("A", 2)), (("A", 3), ("A", 0)), (("A", own), ("B", 1)), (("B", 2), ("B", 3)), (("B", 0), ("B", own)),
        (("C", 1), ("C", 2)), (("C", 0), ("C", own - 1)),
    ]
    steps = len(rows)
    first_of_two = steps - 2
    ja = jnp.where(late_even, 2, 0)
    jb = jnp.where(even, 0, 2)
    start = [1, 0, 1, 3, 0, 1, 0]
    number = [own, 2, 2, own - 2, 2, own - 1, 2]
    stride = [1, own + 1, 1, 1, own + 1, 1, own]
    le = [(2,), (0, 2), (1,), (1,), (1,), (1,), (1,)]
    lo_ = [(1,), (0, 1), (2, 3), (2, 3), (2, 3), (1,), (1,)]
    ee = [(), (0,), (), (), (), (), ()]
    eo = [(1,), (0, 1), (), (), (), (1,), (1,)]

    def by_class(i, of):
        table = [pick(i, [of(entry) for entry in c]) for c in (le, lo_, ee, eo)]
        return jnp.where(late, jnp.where(even, table[0], table[1]), jnp.where(even, table[2], table[3]))

    def operand(layer, r, b, d):
        pieces = []
        for a in range(3):
            for k in range(3):
                both = []
                for part_ in range(2):
                    cols = []
                    for h in range(2):
                        c = 2 * b + h - k * d
                        if a == 0:
                            cols.append(ab[layer, r, c, part_])
                        elif a == 2:
                            cols.append(ab[layer, r + 1, c, part_])
                        else:
                            cols += [ab[layer, r, c, part_, :, step:], ab[layer, r + 1, c, part_, :, :step]]
                    both.append(jnp.concatenate(cols, axis=1))
                pieces += [both[0], both[1], both[0]]
        return jnp.concatenate(pieces, axis=0)

    def straddle(layer, j, r):
        cols = []
        for h in range(2):
            cols += [af[layer, j, r, :, (2 * h + 1) * step:(2 * h + 2) * step], af[layer, j, r + 1, :, 2 * h * step:(2 * h + 1) * step]]
        return jnp.concatenate(cols, axis=1)

    def compute(layer, d, units):
        right = jnp.concatenate([operand(layer, r, 3 - j, d) for r, j in units], axis=1)
        total = jnp.dot(taps[layer], right, preferred_element_type=F32)
        pre = total + jnp.concatenate([tall[layer]] * (total.shape[1] // out_ch), axis=1)
        g = jnp.tanh(pre[:ch]) * (0.5 * jnp.tanh(0.5 * pre[ch:]) + 0.5)
        hi, lo = split(g)
        base = jnp.concatenate([straddle(layer, j, r) for r, j in units], axis=1)
        return base + jnp.dot(mix[layer], jnp.concatenate([hi, lo, hi], axis=0), preferred_element_type=F32)

    def body(i, carry):
        for n in range(steps):
            @pl.when(i == n)
            def _(n=n):
                event(n)

        first, each, pace = pick(i, start), pick(i, number), pick(i, stride)
        j0 = by_class(i, lambda e: e[0] if e else 0)
        j1 = by_class(i, lambda e: e[1] if len(e) > 1 else 0)
        blocks = by_class(i, len)
        layer = (i >= first_of_two).astype(jnp.int32)

        def take(n, carry):
            second = n >= each
            q = first + pace * jnp.where(second, n - each, n)
            ingest(layer, jnp.where(second, j1, j0), q)
            return carry

        lax.fori_loop(0, each * blocks, take, 0)

        units = []
        for lane in range(2):
            r = pick(i, [pair[lane][1] for pair in rows])
            kind = pick(i, ["ABC".index(pair[lane][0]) for pair in rows])
            if any(pair[lane][0] == "B" and pair[0][0] == "A" for pair in rows):
                r = jnp.where((kind == 1) & jnp.logical_not(late), own, r)
            j = jnp.where(kind == 0, ja, jnp.where(kind == 1, jnp.where(late, jb, 0), 0))
            units.append((r, j, kind))

        @pl.when(late | (i < 3) | (i >= first_of_two))
        def _():
            value = compute(layer, layer + 1, [(r, j) for r, j, _ in units])

            @pl.when(layer == 0)
            def _():
                for n, (r, j, kind) in enumerate(units):
                    v = value[:, n * 2 * length:(n + 1) * 2 * length]
                    row = F * fib + 2 * r - 1
                    ok = [(row >= 0) & (row < nf * fib), (row + 1 >= 0) & (row + 1 < nf * fib)]
                    v = jnp.concatenate([jnp.where(ok[p % 2], v[:, p * step:(p + 1) * step], 0.0) for p in range(4)], axis=1)
                    af[1, j, r] = v
                    hi, lo = split(v)
                    for h in range(2):
                        ab[1, r, 2 * (3 - j) + h, 0] = hi[:, h * 2 * step:(h + 1) * 2 * step]
                        ab[1, r, 2 * (3 - j) + h, 1] = lo[:, h * 2 * step:(h + 1) * 2 * step]

                for r, j, kind in units:
                    @pl.when((late & (kind == 1)) | ((T == 0) & (kind == 0)))
                    def _(r=r, j=j):
                        share(j, r).start()

            @pl.when(layer == 1)
            def _():
                for n, (r, j, kind) in enumerate(units):
                    for p in range(4):
                        h, e = p // 2, p % 2
                        at = n * 2 * length + p * step
                        out_ref[pl.ds(h * fib + 2 * r + e, ch, stride=fib * 2), :] = value[:, at:at + step]
        return carry

    lax.fori_loop(0, steps, body, 0)

    @pl.when(onward & even)
    def _():
        cross(arrive[-1]).wait_send()

    @pl.when(onward & isodd)
    def _():
        for q in arrive:
            cross(q).wait_send()

    for j, ss, rr, ok in ((0, h0s, h0r, None), (2, h2s, h2r, late)):
        @pl.when(up if ok is None else up & ok)
        def _(j=j, ss=ss, rr=rr):
            halo_up(j, ss, rr).wait_send()

        @pl.when(down if ok is None else down & ok)
        def _(j=j, ss=ss, rr=rr):
            halo_down(j, ss, rr).wait_send()

    for q in range(wide):
        @pl.when(even | late)
        def _(q=q):
            part(0, q).wait_send()

        @pl.when(late_even)
        def _(q=q):
            part3(q).wait_send()

    @pl.when(even | late)
    def _():
        for r in range(mid):
            share(0, r).wait_send()

    if far:
        for i, e, ok, _ok in thirds_list:
            @pl.when(send3 if ok is None else send3 & ok)
            def _(i=i, e=e):
                third(i, e).wait_send()


def spread_kernel(
    nt, nf, fib,
    x_hbm, w1_hbm, b1_hbm, r1_hbm, w2_hbm, b2_hbm, r2_hbm, out_ref,
    xv, w1, b1, r1, w2, b2, r2, taps, mix, tall, pk, af, sf, ab, mf, mb, fs, fr,
    in_sem, w_sem, xs, xr, hs, hr, gs, gr,
):
    T = lax.axis_index("tm")
    F = lax.axis_index("fibre")
    odd = lax.rem(T, 2)
    partner = T + 1 - 2 * odd
    peers = [partner, lax.rem(T + 2, nt), lax.rem(partner + 2, nt)]
    chip = T - odd
    other = lax.rem(chip + 2, nt)
    ch = pk.shape[2]
    own = fib // 2
    out_ch = 2 * ch
    step = DILATION_ONE
    group = step // nt
    up, down = F + 1 < nf, F > 0
    lane = lax.broadcasted_iota(jnp.int32, (ch, step), 1)
    early_half = lane < 2 * group
    first_fibre = lax.rem(lane, 2 * group) < group

    def dev(t, f):
        return {"tm": t, "fibre": f}

    load = pltpu.make_async_copy(x_hbm, xv, in_sem.at[0])
    load.start()
    weights = [
        pltpu.make_async_copy(a, b, w_sem.at[i])
        for i, (a, b) in enumerate(
            [(w1_hbm, w1), (b1_hbm, b1), (r1_hbm, r1), (w2_hbm, w2), (b2_hbm, b2), (r2_hbm, r2)]
        )
    ]
    for c in weights:
        c.start()

    barrier = pltpu.get_barrier_semaphore()
    for p in peers:
        pl.semaphore_signal(barrier, inc=1, device_id=dev(p, F), device_id_type=pl.DeviceIdType.MESH)
    count = jnp.int32(len(peers))
    for e, ok in ((1, up), (-1, down)):
        @pl.when(ok)
        def _(e=e):
            pl.semaphore_signal(barrier, inc=1, device_id=dev(T, F + e), device_id_type=pl.DeviceIdType.MESH)
        count = count + ok.astype(jnp.int32)

    def swap(parts):
        a, b, c, d = parts
        half = 2 * group
        a, c = jnp.where(early_half, a, pltpu.roll(c, half, 1)), jnp.where(early_half, pltpu.roll(a, half, 1), c)
        b, d = jnp.where(early_half, b, pltpu.roll(d, half, 1)), jnp.where(early_half, pltpu.roll(b, half, 1), d)
        back = step - group
        a, b = jnp.where(first_fibre, a, pltpu.roll(b, group, 1)), jnp.where(first_fibre, pltpu.roll(a, back, 1), b)
        c, d = jnp.where(first_fibre, c, pltpu.roll(d, group, 1)), jnp.where(first_fibre, pltpu.roll(c, back, 1), d)
        return a, b, c, d

    load.wait()

    def pack(q):
        parts = [xv[pl.ds(h * fib + 2 * q + e, ch, stride=fib * 2), :] for h in range(2) for e in range(2)]
        for t, value in enumerate(swap(parts)):
            pk[t, q] = value

            @pl.when(T == t)
            def _(value=value):
                af[q + 1, t] = value

    pack(0)
    pl.semaphore_wait(barrier, count)

    def remote(src, dst, ssem, rsem, t, f):
        return pltpu.make_async_remote_copy(
            src_ref=src, dst_ref=dst, send_sem=ssem, recv_sem=rsem,
            device_id=dev(t, f), device_id_type=pl.DeviceIdType.MESH,
        )

    def signal_out(k, q):
        n = k * own + q - 1
        return remote(pk.at[peers[k], q - 1], af.at[q, T], xs.at[n], xr.at[n], peers[k], F)

    def signal_in(k, q):
        n = k * own + q - 1
        return remote(pk.at[peers[k], q - 1], af.at[q, peers[k]], xs.at[n], xr.at[n], peers[k], F)

    def halo_up(n):
        blocks = pl.ds((chip, other)[n], 2)
        return remote(af.at[own, blocks], af.at[0, blocks], hs.at[2 * n], hr.at[2 * n], T, F + 1)

    def halo_down(n):
        blocks = pl.ds((chip, other)[n], 2)
        return remote(af.at[1, blocks], af.at[own + 1, blocks], hs.at[2 * n + 1], hr.at[2 * n + 1], T, F - 1)

    def feature_out(k, p):
        n = k * own + p
        return remote(fs.at[p, peers[k]], fr.at[p, T], gs.at[n], gr.at[n], peers[k], F)

    def feature_in(k, p):
        n = k * own + p
        return remote(fs.at[p, peers[k]], fr.at[p, peers[k]], gs.at[n], gr.at[n], peers[k], F)

    def begin(i, carry):
        q = i + 1

        @pl.when(i > 0)
        def _():
            pack(i)
        for k in (1, 2, 0):
            signal_out(k, q).start()
        return carry

    lax.fori_loop(0, own, begin, 0)

    no_rows = jnp.zeros((nt, ch, step), F32)

    @pl.when(jnp.logical_not(down))
    def _():
        af[0] = no_rows

    @pl.when(jnp.logical_not(up))
    def _():
        af[own + 1] = no_rows

    for q in range(own + 2):
        for kind in range(2):
            ab[kind, 0, q, :, :, :step] = jnp.zeros((2, ch, step), BF)
            if q <= own:
                mb[kind, q, :, :, :2 * step] = jnp.zeros((2, ch, 2 * step), BF)

    for q in (1, own):
        signal_in(0, q).wait_recv()

    @pl.when(up)
    def _():
        halo_up(0).start()

    @pl.when(down)
    def _():
        halo_down(0).start()

    for c in weights:
        c.wait()

    def prepare(layer, w, r, bias):
        for a in range(3):
            for k in range(3):
                hi, lo = split(w[a, k].T)
                for i, piece in enumerate((hi, hi, lo)):
                    taps[layer, :, pl.ds((9 * a + 3 * k + i) * ch, ch)] = piece
        hi, lo = split(r[...])
        for i, piece in enumerate((hi, hi, lo)):
            mix[layer, :, pl.ds(i * ch, ch)] = piece
        tall[layer] = jnp.broadcast_to(bias[...], (out_ch, out_ch)).T

    prepare(0, w1, r1, b1)
    prepare(1, w2, r2, b2)

    def keep(ref, kind, q, values, lead, shifted):
        later = None
        for t, value in enumerate(values):
            at = pl.ds((t + lead) * step, step)
            hi, lo = split(value)
            if shifted:
                turned = pltpu.roll(value, 2 * group, 1)
                before = jnp.where(early_half, jnp.zeros_like(turned) if later is None else later, turned)
                later = turned
                ref[kind, 0, q, 0, :, at], ref[kind, 0, q, 1, :, at] = hi, lo
                hi, lo = split(before)
                ref[kind, 1, q, 0, :, at], ref[kind, 1, q, 1, :, at] = hi, lo
            else:
                ref[kind, q, 0, :, at], ref[kind, q, 1, :, at] = hi, lo

    def pair(q):
        keep(ab, 0, q, [af[q, t] for t in range(nt)], 1, True)

    def between(left, right):
        return jnp.where(first_fibre, pltpu.roll(left, step - group, 1), pltpu.roll(right, group, 1))

    def across(r):
        values = [between(af[r, t], af[r + 1, t]) for t in range(nt)]
        for t in range(nt):
            sf[r, :, pl.ds(t * step, step)] = values[t]
        keep(ab, 1, r, values, 1, True)

    def first_operand(r, first, n):
        pieces = []
        for kind, q in ((0, r), (1, r), (0, r + 1)):
            for early, back in ((0, 0), (1, 0), (0, 1)):
                lanes = slice((first + 1 - back) * step, (first + 1 - back + n) * step)
                hi, lo = ab[kind, early, q, 0, :, lanes], ab[kind, early, q, 1, :, lanes]
                pieces += [hi, lo, hi]
        return jnp.concatenate(pieces, axis=0)

    def second_operand(p, first):
        pieces = []
        for kind, q in ((0, p), (1, p), (0, p + 1)):
            for k in range(3):
                lanes = pl.ds(pl.multiple_of((2 - k + first) * step, step), 2 * step)
                hi, lo = mb[kind, q, 0, :, lanes], mb[kind, q, 1, :, lanes]
                pieces += [hi, lo, hi]
        return jnp.concatenate(pieces, axis=0)

    def layer_of(layer, right, base):
        total = jnp.dot(taps[layer], right, preferred_element_type=F32)
        pre = total + jnp.concatenate([tall[layer]] * (total.shape[1] // out_ch), axis=1)
        g = jnp.tanh(pre[:ch]) * (0.5 * jnp.tanh(0.5 * pre[ch:]) + 0.5)
        hi, lo = split(g)
        return base + jnp.dot(mix[layer], jnp.concatenate([hi, lo, hi], axis=0), preferred_element_type=F32)

    def middle(rows, first, n):
        value = layer_of(
            0,
            jnp.concatenate([first_operand(r, first, n) for r in rows], axis=1),
            jnp.concatenate([sf[r, :, first * step:(first + n) * step] for r in rows], axis=1),
        )
        for i, r in enumerate(rows):
            row = F * fib + 2 * r - 1
            ok = [((f >= 0) & (f < nf * fib)).astype(jnp.int32) for f in (row, row + 1)]
            inside = jnp.where(first_fibre, ok[0], ok[1]) == 1
            parts = [jnp.where(inside, value[:, t * step:(t + 1) * step], 0.0) for t in range(i * n, (i + 1) * n)]
            for t in range(n):
                mf[r, first + t] = parts[t]
            keep(mb, 0, r, parts, first + 2, False)

    def join(p, first, n):
        values = [between(mf[p, t], mf[p + 1, t]) for t in range(first, first + n)]
        keep(mb, 1, p, values, first + 2, False)
        for t in range(n):
            sf[p, :, pl.ds((first + t) * step, step)] = values[t]

    def two_blocks(p, first):
        return sf[p, :, pl.ds(pl.multiple_of(first * step, step), 2 * step)]

    def away(p, first):
        value = layer_of(1, second_operand(p, first), two_blocks(p, first))
        for t in range(2):
            fs[p, first + t] = value[:, t * step:(t + 1) * step]

    def home(ps):
        value = layer_of(
            1,
            jnp.concatenate([second_operand(p, chip) for p in ps], axis=1),
            jnp.concatenate([two_blocks(p, chip) for p in ps], axis=1),
        )
        for i, p in enumerate(ps):
            parts = [value[:, (2 * i + t) * step:(2 * i + t + 1) * step] for t in range(2)]
            fs[p, partner] = jnp.where(odd == 1, parts[0], parts[1])
            fr[p, T] = jnp.where(odd == 1, parts[1], parts[0])
            feature_out(0, p).start()

    pairs = list(range(1, own + 2)) + [0]
    rows = [0] + list(range(1, own + 1)) + [0]
    outs = [0, 0] + list(range(1, own)) + [0]

    def body(i, carry):
        q, r, p = pick(i, pairs), pick(i, rows), pick(i, outs)

        @pl.when(i < own)
        def _():
            for k in range(3):
                @pl.when((k > 0) | ((q != 1) & (q != own)))
                def _(k=k):
                    signal_in(k, q).wait_recv()

        @pl.when((q == 1) & down)
        def _():
            halo_down(1).start()

        @pl.when((q == own) & up)
        def _():
            halo_up(1).start()

        @pl.when((q == own + 1) & up)
        def _():
            for n in range(2):
                halo_down(n).wait_recv()

        @pl.when((q == 0) & down)
        def _():
            for n in range(2):
                halo_up(n).wait_recv()

        pair(q)

        for where, blocks, theirs in ((0, nt, 2), (2, 2, 0)):
            @pl.when((i >= 1) & (chip == where))
            def _(blocks=blocks):
                across(r)
                middle([r], 0, blocks)

            @pl.when((i >= 2) & (chip == where))
            def _(blocks=blocks, theirs=theirs):
                join(p, 0, blocks)
                away(p, theirs)

        @pl.when((i >= 2) & outer)
        def _():
            for k in (2, 1):
                feature_out(k, p).start()

        @pl.when((i >= 2) & jnp.logical_not(outer))
        def _():
            for k in (1, 2):
                feature_out(k, p).start()
        return carry

    outer = (T == 0) | (T == nt - 1)
    lax.fori_loop(0, own + 2, body, 0)

    @pl.when(chip == 2)
    def _():
        middle(list(range(own + 1)), 2, 2)
        for p in range(own):
            join(p, 2, 2)

    home(list(range(own)))

    def finish(i, carry):
        p = lax.rem(i + 1, own)
        for k in range(3):
            feature_in(k, p).wait_recv()
        for n, value in enumerate(swap([fr[p, t] for t in range(nt)])):
            out_ref[pl.ds(n // 2 * fib + 2 * p + n % 2, ch, stride=fib * 2), :] = value
        return carry

    lax.fori_loop(0, own, finish, 0)

    for k in range(3):
        for q in range(1, own + 1):
            signal_out(k, q).wait_send()
            feature_out(k, q - 1).wait_send()
    for n in range(2):
        @pl.when(up)
        def _(n=n):
            halo_up(n).wait_send()

        @pl.when(down)
        def _(n=n):
            halo_down(n).wait_send()


def solution(mesh):
    nt, nf = mesh.shape["tm"], mesh.shape["fibre"]
    placed = (P(None, "fibre", "tm"), P(), P(), P(), P(), P(), P())

    def body(signal, w1, b1, r1, w2, b2, r2):
        ch, fib, length = signal.shape
        assert length == DILATION_TWO == 2 * DILATION_ONE and nt % 2 == 0 and fib == FIB_DEV
        x = signal.reshape(ch, fib, length // 128, 128).transpose(0, 2, 1, 3).reshape(-1, 128)
        out_ch = w1.shape[2]
        own = fib // 2
        w1, w2 = jnp.transpose(w1, (0, 1, 3, 2)), jnp.transpose(w2, (0, 1, 3, 2))
        b1 = b1.reshape(1, out_ch)
        b2 = b2.reshape(1, out_ch)
        dma = lambda n: pltpu.SemaphoreType.DMA((n,))
        inputs = [
            pltpu.VMEM(x.shape, F32),
            pltpu.VMEM(w1.shape, F32), pltpu.VMEM(b1.shape, F32), pltpu.VMEM(r1.shape, F32),
            pltpu.VMEM(w2.shape, F32), pltpu.VMEM(b2.shape, F32), pltpu.VMEM(r2.shape, F32),
            pltpu.VMEM((2, out_ch, 27 * ch), BF), pltpu.VMEM((2, ch, 3 * ch), BF),
            pltpu.VMEM((2, out_ch, out_ch), F32),
        ]
        step = DILATION_ONE
        if nt == 4:
            form = spread_kernel
            scratch = inputs + [
                pltpu.VMEM((nt, own, ch, step), F32), pltpu.VMEM((own + 2, nt, ch, step), F32),
                pltpu.VMEM((own + 1, ch, nt * step), F32),
                pltpu.VMEM((2, 2, own + 2, 2, ch, (nt + 1) * step), BF),
                pltpu.VMEM((own + 1, nt, ch, step), F32),
                pltpu.VMEM((2, own + 1, 2, ch, (nt + 2) * step), BF),
                pltpu.VMEM((own, nt, ch, step), F32), pltpu.VMEM((own, nt, ch, step), F32),
                dma(1), dma(6), dma(3 * own), dma(3 * own), dma(4), dma(4), dma(3 * own), dma(3 * own),
            ]
        else:
            form = kernel
            scratch = [
                pltpu.VMEM((2, 4, own + 2, ch, 2 * length), F32),
                pltpu.VMEM((2, own + 2, 4 * length // step, 2, ch, 2 * step), BF),
            ] + inputs + [
                dma(1), dma(6), dma(2), dma(2), dma(2), dma(2), dma(own + 2), dma(own + 2),
                dma(own + 2), dma(own + 2), dma(own + 2), dma(own + 2),
                dma(own + 1), dma(own + 1), dma(3), dma(3),
                pltpu.SemaphoreType.REGULAR,
            ]
        out = pl.pallas_call(
            lambda *refs: form(nt, nf, fib, *refs),
            name="gated_layers",
            out_shape=pltpu.VMEM(x.shape, F32),
            in_specs=[pl.BlockSpec(memory_space=pl.ANY)] * 7,
            out_specs=pl.BlockSpec(memory_space=pltpu.VMEM),
            scratch_shapes=scratch,
            compiler_params=pltpu.CompilerParams(
                collective_id=0, has_side_effects=True, vmem_limit_bytes=60 * 1024 * 1024
            ),
        )(x, w1, b1, r1, w2, b2, r2)
        out = out.reshape(ch, length // 128, fib, 128).transpose(0, 2, 1, 3)
        return out.reshape(ch, fib, length)

    return jax.shard_map(body, mesh=mesh, in_specs=placed, out_specs=P(None, "fibre", "tm"), check_vma=False)
```

```python
import jax
import jax.numpy as jnp
from jax import lax
from jax.experimental import pallas as pl
from jax.experimental.pallas import tpu as pltpu
from jax.sharding import PartitionSpec as P

DILATION_ONE = 128
DILATION_TWO = 256
FIB_DEV = 8
BF = jnp.bfloat16
F32 = jnp.float32


def split(value):
    hi = value.astype(BF)
    return hi, (value - hi.astype(F32)).astype(BF)


def pick(i, values):
    out = jnp.int32(values[-1])
    for n in range(len(values) - 2, -1, -1):
        out = jnp.where(i == n, jnp.int32(values[n]), out)
    return out


def kernel(
    nt, nf, fib,
    x_hbm, w1_hbm, b1_hbm, r1_hbm, w2_hbm, b2_hbm, r2_hbm, out_ref,
    af, ab, xv, w1, b1, r1, w2, b2, r2, taps, mix, tall,
    in_sem, w_sem, h0s, h0r, h2s, h2r, xs, xr, ps, pr, ts, tr, ms, mr, es, er, go,
):
    s, m = af.at[0], af.at[1]
    T = lax.axis_index("tm")
    F = lax.axis_index("fibre")
    odd = lax.rem(T, 2)
    even = odd == 0
    isodd = odd == 1
    late = T >= 2
    partner = T + 1 - 2 * odd
    ch, length = af.shape[3], af.shape[4] // 2
    own = fib // 2
    wide = own + 2
    mid = own + 1
    out_ch = 2 * ch
    step = DILATION_ONE
    far = nt > 4
    up, down = F + 1 < nf, F > 0
    onward = T + 2 < nt
    inner = list(range(1, own + 1))
    arrive = [1, own] + list(range(2, own))
    edges = [0, own + 1]

    def dev(t, f):
        return {"tm": t, "fibre": f}

    load = pltpu.make_async_copy(x_hbm, xv, in_sem.at[0])
    load.start()
    weights = [
        pltpu.make_async_copy(a, b, w_sem.at[i])
        for i, (a, b) in enumerate(
            [(w1_hbm, w1), (b1_hbm, b1), (r1_hbm, r1), (w2_hbm, w2), (b2_hbm, b2), (r2_hbm, r2)]
        )
    ]
    for c in weights:
        c.start()

    barrier = pltpu.get_barrier_semaphore()
    friends = [(partner, F, None), (T, F + 1, up), (T, F - 1, down), (T + 2, F, onward), (T - 2, F, late)]
    if far:
        send3 = isodd & (T + 3 < nt)
        recv3 = even & (T >= 4)
        for e, ok in ((0, None), (1, up), (-1, down)):
            for d, okt in ((3, send3), (-3, recv3)):
                friends.append((T + d, F + e, okt if ok is None else okt & ok))
    count = jnp.int32(0)
    for t, f, ok in friends:
        if ok is None:
            pl.semaphore_signal(barrier, inc=1, device_id=dev(t, f), device_id_type=pl.DeviceIdType.MESH)
            count = count + 1
        else:
            @pl.when(ok)
            def _(t=t, f=f):
                pl.semaphore_signal(barrier, inc=1, device_id=dev(t, f), device_id_type=pl.DeviceIdType.MESH)
            count = count + ok.astype(jnp.int32)

    load.wait()
    for f in range(fib):
        for h in range(2):
            value = xv[pl.ds(h * fib + f, ch, stride=fib * 2), :]
            lanes = pl.ds((f % 2) * step, step)
            af[0, 0, 1 + f // 2, :, pl.ds((2 * h + f % 2) * step, step)] = value
            hi, lo = split(value)
            ab[0, 1 + f // 2, 6 + h, 0, :, lanes] = hi
            ab[0, 1 + f // 2, 6 + h, 1, :, lanes] = lo
    pl.semaphore_wait(barrier, count)

    def remote(src, dst, ssem, rsem, t, f):
        return pltpu.make_async_remote_copy(
            src_ref=src, dst_ref=dst, send_sem=ssem, recv_sem=rsem,
            device_id=dev(t, f), device_id_type=pl.DeviceIdType.MESH,
        )

    def halo_up(j, ss, rr):
        return remote(s.at[j, own], s.at[j, 0], ss.at[0], rr.at[0], T, F + 1)

    def halo_down(j, ss, rr):
        return remote(s.at[j, 1], s.at[j, own + 1], ss.at[1], rr.at[1], T, F - 1)

    def cross(q):
        return remote(s.at[0, q], s.at[2, q], xs.at[q], xr.at[q], T + 2, F)

    def part(src, q):
        return remote(s.at[src, q], s.at[1, q], ps.at[q], pr.at[q], partner, F)

    def part3(q):
        return remote(s.at[2, q], s.at[3, q], ts.at[q], tr.at[q], partner, F)

    def share(src, r):
        return remote(m.at[src, r], m.at[1, r], ms.at[r], mr.at[r], partner, F)

    @pl.when(onward & even)
    def _():
        for q in arrive:
            cross(q).start()

    @pl.when(up)
    def _():
        halo_up(0, h0s, h0r).start()

    @pl.when(down)
    def _():
        halo_down(0, h0s, h0r).start()

    @pl.when(even)
    def _():
        for q in arrive:
            part(0, q).start()

    if far:
        def third(i, e):
            if e == 0:
                src, dst = s.at[0, pl.ds(1, own)], s.at[3, pl.ds(1, own)]
            elif e == 1:
                src, dst = s.at[0, own], s.at[3, 0]
            else:
                src, dst = s.at[0, 1], s.at[3, own + 1]
            return remote(src, dst, es.at[i], er.at[i], T + 3, F + e)

        thirds_list = [(0, 0, None, None), (1, 1, up, down), (2, -1, down, up)]
        for i, e, ok, _ok in thirds_list:
            @pl.when(send3 if ok is None else send3 & ok)
            def _(i=i, e=e):
                third(i, e).start()

    zero = jnp.zeros(af.shape[3:], F32)

    def zero_halo(j):
        @pl.when(jnp.logical_not(down))
        def _():
            af[0, j, 0] = zero

        @pl.when(jnp.logical_not(up))
        def _():
            af[0, j, own + 1] = zero

    zero_halo(0)

    def no_chunks(layer, first, n):
        for q in range(wide if layer == 0 else mid):
            ab[layer, q, pl.ds(first, n)] = jnp.zeros((n,) + ab.shape[3:], BF)

    @pl.when(T == 0)
    def _():
        no_chunks(0, 4, 2)
        no_chunks(1, 4, 2)

    @pl.when(T < 2)
    def _():
        no_chunks(1, 2, 2)

    @pl.when(T == 2)
    def _():
        no_chunks(0, 0, 2)

    @pl.when(late)
    def _():
        zero_halo(2)

    if far:
        @pl.when(recv3)
        def _():
            zero_halo(3)

    for c in weights:
        c.wait()

    def prepare(layer, w, r, bias):
        for a in range(3):
            for k in range(3):
                hi, lo = split(w[a, k].T)
                for i, piece in enumerate((hi, hi, lo)):
                    taps[layer, :, pl.ds((9 * a + 3 * k + i) * ch, ch)] = piece
        hi, lo = split(r[...])
        for i, piece in enumerate((hi, hi, lo)):
            mix[layer, :, pl.ds(i * ch, ch)] = piece
        tall[layer] = jnp.broadcast_to(bias[...], (out_ch, out_ch)).T

    prepare(0, w1, r1, b1)
    prepare(1, w2, r2, b2)

    def ingest(layer, j, q):
        hi, lo = split(af[layer, j, q])
        for h in range(2):
            ab[layer, q, 2 * (3 - j) + h, 0] = hi[:, h * 2 * step:(h + 1) * 2 * step]
            ab[layer, q, 2 * (3 - j) + h, 1] = lo[:, h * 2 * step:(h + 1) * 2 * step]

    @pl.when(onward & even)
    def _():
        for q in arrive[:-1]:
            cross(q).wait_send()
        pl.semaphore_signal(go, inc=1, device_id=dev(partner, F), device_id_type=pl.DeviceIdType.MESH)

    @pl.when(onward & isodd)
    def _():
        pl.semaphore_wait(go, 1)
        for q in arrive:
            cross(q).start()

    if far:
        @pl.when(recv3)
        def _():
            for i, e, _ok, ok in thirds_list:
                if ok is None:
                    third(i, e).wait_recv()
                else:
                    @pl.when(ok)
                    def _(i=i, e=e):
                        third(i, e).wait_recv()

            def old(q, carry):
                ingest(0, 3, q)
                return carry

            lax.fori_loop(0, wide, old, 0)

    late_even, late_odd = late & even, late & isodd

    def halos_in(j, ss, rr):
        @pl.when(down)
        def _():
            halo_up(j, ss, rr).wait_recv()

        @pl.when(up)
        def _():
            halo_down(j, ss, rr).wait_recv()

    def crossed(q):
        cross(q).wait_recv()

        @pl.when(even)
        def _():
            part3(q).start()

        @pl.when(isodd)
        def _():
            part(2, q).start()

        if q == 1:
            @pl.when(down)
            def _():
                halo_down(2, h2s, h2r).start()

        if q == own:
            @pl.when(up)
            def _():
                halo_up(2, h2s, h2r).start()

    def event(i):
        if i == 0:
            @pl.when(late_even)
            def _():
                for q in arrive:
                    crossed(q)

            @pl.when(isodd)
            def _():
                for q in arrive:
                    part(0, q).wait_recv()
        if i == 1:
            @pl.when(late_odd)
            def _():
                crossed(arrive[0])

            halos_in(0, h0s, h0r)

            @pl.when(even)
            def _():
                for q in edges:
                    part(0, q).start()

            @pl.when(isodd)
            def _():
                for q in edges:
                    part(0, q).wait_recv()

            @pl.when(late_even)
            def _():
                halos_in(2, h2s, h2r)
                for q in edges:
                    part3(q).start()
        if i in (2, 3):
            now = arrive[:-1] if i == 2 else arrive[-1:]

            @pl.when(late_even)
            def _():
                for q in now:
                    part(0, q).wait_recv()

            @pl.when(late_odd)
            def _():
                for q in now:
                    if q != arrive[0]:
                        crossed(q)
                for q in now:
                    part3(q).wait_recv()
        if i == 4:
            @pl.when(late_even)
            def _():
                for q in edges:
                    part(0, q).wait_recv()

            @pl.when(late_odd)
            def _():
                halos_in(2, h2s, h2r)
                for q in edges:
                    part(2, q).start()
                for q in edges:
                    part3(q).wait_recv()
        if i == 5:
            @pl.when(T >= 1)
            def _():
                for r in range(1, own):
                    share(0, r).wait_recv()
        if i == 6:
            @pl.when(T >= 1)
            def _():
                for r in (0, own):
                    share(0, r).wait_recv()

    rows = [
        (("A", 1), ("A", 2)), (("A", 3), ("A", 0)), (("A", own), ("B", 1)), (("B", 2), ("B", 3)), (("B", 0), ("B", own)),
        (("C", 1), ("C", 2)), (("C", 0), ("C", own - 1)),
    ]
    steps = len(rows)
    first_of_two = steps - 2
    ja = jnp.where(late_even, 2, 0)
    jb = jnp.where(even, 0, 2)
    start = [1, 0, 1, 3, 0, 1, 0]
    number = [own, 2, 2, own - 2, 2, own - 1, 2]
    stride = [1, own + 1, 1, 1, own + 1, 1, own]
    le = [(2,), (0, 2), (1,), (1,), (1,), (1,), (1,)]
    lo_ = [(1,), (0, 1), (2, 3), (2, 3), (2, 3), (1,), (1,)]
    ee = [(), (0,), (), (), (), (), ()]
    eo = [(1,), (0, 1), (), (), (), (1,), (1,)]

    def by_class(i, of):
        table = [pick(i, [of(entry) for entry in c]) for c in (le, lo_, ee, eo)]
        return jnp.where(late, jnp.where(even, table[0], table[1]), jnp.where(even, table[2], table[3]))

    def operand(layer, r, b, d):
        pieces = []
        for a in range(3):
            for k in range(3):
                both = []
                for part_ in range(2):
                    cols = []
                    for h in range(2):
                        c = 2 * b + h - k * d
                        if a == 0:
                            cols.append(ab[layer, r, c, part_])
                        elif a == 2:
                            cols.append(ab[layer, r + 1, c, part_])
                        else:
                            cols += [ab[layer, r, c, part_, :, step:], ab[layer, r + 1, c, part_, :, :step]]
                    both.append(jnp.concatenate(cols, axis=1))
                pieces += [both[0], both[1], both[0]]
        return jnp.concatenate(pieces, axis=0)

    def straddle(layer, j, r):
        cols = []
        for h in range(2):
            cols += [af[layer, j, r, :, (2 * h + 1) * step:(2 * h + 2) * step], af[layer, j, r + 1, :, 2 * h * step:(2 * h + 1) * step]]
        return jnp.concatenate(cols, axis=1)

    def compute(layer, d, units):
        right = jnp.concatenate([operand(layer, r, 3 - j, d) for r, j in units], axis=1)
        total = jnp.dot(taps[layer], right, preferred_element_type=F32)
        pre = total + jnp.concatenate([tall[layer]] * (total.shape[1] // out_ch), axis=1)
        g = jnp.tanh(pre[:ch]) * (0.5 * jnp.tanh(0.5 * pre[ch:]) + 0.5)
        hi, lo = split(g)
        base = jnp.concatenate([straddle(layer, j, r) for r, j in units], axis=1)
        return base + jnp.dot(mix[layer], jnp.concatenate([hi, lo, hi], axis=0), preferred_element_type=F32)

    def body(i, carry):
        for n in range(steps):
            @pl.when(i == n)
            def _(n=n):
                event(n)

        first, each, pace = pick(i, start), pick(i, number), pick(i, stride)
        j0 = by_class(i, lambda e: e[0] if e else 0)
        j1 = by_class(i, lambda e: e[1] if len(e) > 1 else 0)
        blocks = by_class(i, len)
        layer = (i >= first_of_two).astype(jnp.int32)

        def take(n, carry):
            second = n >= each
            q = first + pace * jnp.where(second, n - each, n)
            ingest(layer, jnp.where(second, j1, j0), q)
            return carry

        lax.fori_loop(0, each * blocks, take, 0)

        units = []
        for lane in range(2):
            r = pick(i, [pair[lane][1] for pair in rows])
            kind = pick(i, ["ABC".index(pair[lane][0]) for pair in rows])
            if any(pair[lane][0] == "B" and pair[0][0] == "A" for pair in rows):
                r = jnp.where((kind == 1) & jnp.logical_not(late), own, r)
            j = jnp.where(kind == 0, ja, jnp.where(kind == 1, jnp.where(late, jb, 0), 0))
            units.append((r, j, kind))

        @pl.when(late | (i < 3) | (i >= first_of_two))
        def _():
            value = compute(layer, layer + 1, [(r, j) for r, j, _ in units])

            @pl.when(layer == 0)
            def _():
                for n, (r, j, kind) in enumerate(units):
                    v = value[:, n * 2 * length:(n + 1) * 2 * length]
                    row = F * fib + 2 * r - 1
                    ok = [(row >= 0) & (row < nf * fib), (row + 1 >= 0) & (row + 1 < nf * fib)]
                    v = jnp.concatenate([jnp.where(ok[p % 2], v[:, p * step:(p + 1) * step], 0.0) for p in range(4)], axis=1)
                    af[1, j, r] = v
                    hi, lo = split(v)
                    for h in range(2):
                        ab[1, r, 2 * (3 - j) + h, 0] = hi[:, h * 2 * step:(h + 1) * 2 * step]
                        ab[1, r, 2 * (3 - j) + h, 1] = lo[:, h * 2 * step:(h + 1) * 2 * step]

                for r, j, kind in units:
                    @pl.when((late & (kind == 1)) | ((T == 0) & (kind == 0)))
                    def _(r=r, j=j):
                        share(j, r).start()

            @pl.when(layer == 1)
            def _():
                for n, (r, j, kind) in enumerate(units):
                    for p in range(4):
                        h, e = p // 2, p % 2
                        at = n * 2 * length + p * step
                        out_ref[pl.ds(h * fib + 2 * r + e, ch, stride=fib * 2), :] = value[:, at:at + step]
        return carry

    lax.fori_loop(0, steps, body, 0)

    @pl.when(onward & even)
    def _():
        cross(arrive[-1]).wait_send()

    @pl.when(onward & isodd)
    def _():
        for q in arrive:
            cross(q).wait_send()

    for j, ss, rr, ok in ((0, h0s, h0r, None), (2, h2s, h2r, late)):
        @pl.when(up if ok is None else up & ok)
        def _(j=j, ss=ss, rr=rr):
            halo_up(j, ss, rr).wait_send()

        @pl.when(down if ok is None else down & ok)
        def _(j=j, ss=ss, rr=rr):
            halo_down(j, ss, rr).wait_send()

    for q in range(wide):
        @pl.when(even | late)
        def _(q=q):
            part(0, q).wait_send()

        @pl.when(late_even)
        def _(q=q):
            part3(q).wait_send()

    @pl.when(even | late)
    def _():
        for r in range(mid):
            share(0, r).wait_send()

    if far:
        for i, e, ok, _ok in thirds_list:
            @pl.when(send3 if ok is None else send3 & ok)
            def _(i=i, e=e):
                third(i, e).wait_send()


def spread_kernel(
    nt, nf, fib,
    x_hbm, w1_hbm, b1_hbm, r1_hbm, w2_hbm, b2_hbm, r2_hbm, out_ref,
    xv, w1, b1, r1, w2, b2, r2, taps, mix, tall, pk, af, sf, ab, mf, mb, fs, fr, held,
    in_sem, w_sem, xs, xr, hs, hr, gs, gr, us, ur, vs, vr,
):
    T = lax.axis_index("tm")
    F = lax.axis_index("fibre")
    odd = lax.rem(T, 2)
    partner = T + 1 - 2 * odd
    peers = [partner, lax.rem(T + 2, nt), lax.rem(partner + 2, nt)]
    chip = T - odd
    other = lax.rem(chip + 2, nt)
    ch = pk.shape[2]
    own = fib // 2
    out_ch = 2 * ch
    step = DILATION_ONE
    group = step // nt
    up, down = F + 1 < nf, F > 0
    lane = lax.broadcasted_iota(jnp.int32, (ch, step), 1)
    early_half = lane < 2 * group
    first_fibre = lax.rem(lane, 2 * group) < group

    def dev(t, f):
        return {"tm": t, "fibre": f}

    load = pltpu.make_async_copy(x_hbm, xv, in_sem.at[0])
    load.start()
    weights = [
        pltpu.make_async_copy(a, b, w_sem.at[i])
        for i, (a, b) in enumerate(
            [(w1_hbm, w1), (b1_hbm, b1), (r1_hbm, r1), (w2_hbm, w2), (b2_hbm, b2), (r2_hbm, r2)]
        )
    ]
    for c in weights:
        c.start()

    barrier = pltpu.get_barrier_semaphore()
    for p in peers:
        pl.semaphore_signal(barrier, inc=1, device_id=dev(p, F), device_id_type=pl.DeviceIdType.MESH)
    count = jnp.int32(len(peers))
    for e, ok in ((1, up), (-1, down)):
        @pl.when(ok)
        def _(e=e):
            pl.semaphore_signal(barrier, inc=1, device_id=dev(T, F + e), device_id_type=pl.DeviceIdType.MESH)
        count = count + ok.astype(jnp.int32)

    def swap(parts):
        a, b, c, d = parts
        half = 2 * group
        a, c = jnp.where(early_half, a, pltpu.roll(c, half, 1)), jnp.where(early_half, pltpu.roll(a, half, 1), c)
        b, d = jnp.where(early_half, b, pltpu.roll(d, half, 1)), jnp.where(early_half, pltpu.roll(b, half, 1), d)
        back = step - group
        a, b = jnp.where(first_fibre, a, pltpu.roll(b, group, 1)), jnp.where(first_fibre, pltpu.roll(a, back, 1), b)
        c, d = jnp.where(first_fibre, c, pltpu.roll(d, group, 1)), jnp.where(first_fibre, pltpu.roll(c, back, 1), d)
        return a, b, c, d

    load.wait()

    def pack(q):
        parts = [xv[pl.ds(h * fib + 2 * q + e, ch, stride=fib * 2), :] for h in range(2) for e in range(2)]
        for t, value in enumerate(swap(parts)):
            pk[t, q] = value

            @pl.when(T == t)
            def _(value=value):
                af[q + 1, t] = value

    pack(0)
    pl.semaphore_wait(barrier, count)

    def remote(src, dst, ssem, rsem, t, f):
        return pltpu.make_async_remote_copy(
            src_ref=src, dst_ref=dst, send_sem=ssem, recv_sem=rsem,
            device_id=dev(t, f), device_id_type=pl.DeviceIdType.MESH,
        )

    def signal_out(k, q):
        n = k * own + q - 1
        return remote(pk.at[peers[k], q - 1], af.at[q, T], xs.at[n], xr.at[n], peers[k], F)

    def signal_in(k, q):
        n = k * own + q - 1
        return remote(pk.at[peers[k], q - 1], af.at[q, peers[k]], xs.at[n], xr.at[n], peers[k], F)

    def halo_up(n):
        blocks = pl.ds((chip, other)[n], 2)
        return remote(af.at[own, blocks], af.at[0, blocks], hs.at[2 * n], hr.at[2 * n], T, F + 1)

    def halo_down(n):
        blocks = pl.ds((chip, other)[n], 2)
        return remote(af.at[1, blocks], af.at[own + 1, blocks], hs.at[2 * n + 1], hr.at[2 * n + 1], T, F - 1)

    def edge_up(k):
        return remote(pk.at[peers[k], own - 1], held.at[k - 1], us.at[k - 1], ur.at[k - 1], T, F + 1)

    def relay_out(k):
        return remote(held.at[k - 1], af.at[0, T], vs.at[k - 1], vr.at[k - 1], peers[k], F)

    def relay_in(k):
        return remote(held.at[k - 1], af.at[0, peers[k]], vs.at[k - 1], vr.at[k - 1], peers[k], F)

    def feature_out(k, p):
        n = k * own + p
        return remote(fs.at[p, peers[k]], fr.at[p, T], gs.at[n], gr.at[n], peers[k], F)

    def feature_in(k, p):
        n = k * own + p
        return remote(fs.at[p, peers[k]], fr.at[p, peers[k]], gs.at[n], gr.at[n], peers[k], F)

    def begin(i, carry):
        q = i + 1

        @pl.when(i > 0)
        def _():
            pack(i)
        for k in (1, 2, 0):
            signal_out(k, q).start()
        return carry

    lax.fori_loop(0, own, begin, 0)

    @pl.when(up)
    def _():
        for k in (1, 2):
            edge_up(k).start()

    no_rows = jnp.zeros((nt, ch, step), F32)

    @pl.when(jnp.logical_not(down))
    def _():
        af[0] = no_rows

    @pl.when(jnp.logical_not(up))
    def _():
        af[own + 1] = no_rows

    for q in range(own + 2):
        for kind in range(2):
            ab[kind, 0, q, :, :, :step] = jnp.zeros((2, ch, step), BF)
            if q <= own:
                mb[kind, q, :, :, :2 * step] = jnp.zeros((2, ch, 2 * step), BF)

    for q in (1, own):
        signal_in(0, q).wait_recv()

    @pl.when(up)
    def _():
        halo_up(0).start()

    @pl.when(down)
    def _():
        halo_down(0).start()

    for c in weights:
        c.wait()

    def prepare(layer, w, r, bias):
        for a in range(3):
            for k in range(3):
                hi, lo = split(w[a, k].T)
                for i, piece in enumerate((hi, hi, lo)):
                    taps[layer, :, pl.ds((9 * a + 3 * k + i) * ch, ch)] = piece
        hi, lo = split(r[...])
        for i, piece in enumerate((hi, hi, lo)):
            mix[layer, :, pl.ds(i * ch, ch)] = piece
        tall[layer] = jnp.broadcast_to(bias[...], (out_ch, out_ch)).T

    prepare(0, w1, r1, b1)
    prepare(1, w2, r2, b2)

    def keep(ref, kind, q, values, lead, shifted):
        later = None
        for t, value in enumerate(values):
            at = pl.ds((t + lead) * step, step)
            hi, lo = split(value)
            if shifted:
                turned = pltpu.roll(value, 2 * group, 1)
                before = jnp.where(early_half, jnp.zeros_like(turned) if later is None else later, turned)
                later = turned
                ref[kind, 0, q, 0, :, at], ref[kind, 0, q, 1, :, at] = hi, lo
                hi, lo = split(before)
                ref[kind, 1, q, 0, :, at], ref[kind, 1, q, 1, :, at] = hi, lo
            else:
                ref[kind, q, 0, :, at], ref[kind, q, 1, :, at] = hi, lo

    def pair(q):
        keep(ab, 0, q, [af[q, t] for t in range(nt)], 1, True)

    def between(left, right):
        return jnp.where(first_fibre, pltpu.roll(left, step - group, 1), pltpu.roll(right, group, 1))

    def across(r):
        values = [between(af[r, t], af[r + 1, t]) for t in range(nt)]
        for t in range(nt):
            sf[r, :, pl.ds(t * step, step)] = values[t]
        keep(ab, 1, r, values, 1, True)

    def first_operand(r, first, n):
        pieces = []
        for kind, q in ((0, r), (1, r), (0, r + 1)):
            for early, back in ((0, 0), (1, 0), (0, 1)):
                lanes = slice((first + 1 - back) * step, (first + 1 - back + n) * step)
                hi, lo = ab[kind, early, q, 0, :, lanes], ab[kind, early, q, 1, :, lanes]
                pieces += [hi, lo, hi]
        return jnp.concatenate(pieces, axis=0)

    def second_operand(p, first, n):
        pieces = []
        for kind, q in ((0, p), (1, p), (0, p + 1)):
            for k in range(3):
                lanes = pl.ds(pl.multiple_of((2 - k + first) * step, step), n * step)
                hi, lo = mb[kind, q, 0, :, lanes], mb[kind, q, 1, :, lanes]
                pieces += [hi, lo, hi]
        return jnp.concatenate(pieces, axis=0)

    def layer_of(layer, right, base):
        total = jnp.dot(taps[layer], right, preferred_element_type=F32)
        pre = total + jnp.concatenate([tall[layer]] * (total.shape[1] // out_ch), axis=1)
        g = jnp.tanh(pre[:ch]) * (0.5 * jnp.tanh(0.5 * pre[ch:]) + 0.5)
        hi, lo = split(g)
        return base + jnp.dot(mix[layer], jnp.concatenate([hi, lo, hi], axis=0), preferred_element_type=F32)

    def middle(rows, first, n):
        value = layer_of(
            0,
            jnp.concatenate([first_operand(r, first, n) for r in rows], axis=1),
            jnp.concatenate([sf[r, :, first * step:(first + n) * step] for r in rows], axis=1),
        )
        for i, r in enumerate(rows):
            row = F * fib + 2 * r - 1
            ok = [((f >= 0) & (f < nf * fib)).astype(jnp.int32) for f in (row, row + 1)]
            inside = jnp.where(first_fibre, ok[0], ok[1]) == 1
            parts = [jnp.where(inside, value[:, t * step:(t + 1) * step], 0.0) for t in range(i * n, (i + 1) * n)]
            for t in range(n):
                mf[r, first + t] = parts[t]
            keep(mb, 0, r, parts, first + 2, False)

    def join(p, first, n):
        values = [between(mf[p, t], mf[p + 1, t]) for t in range(first, first + n)]
        keep(mb, 1, p, values, first + 2, False)
        for t in range(n):
            sf[p, :, pl.ds((first + t) * step, step)] = values[t]

    def blocks_of(p, first, n):
        return sf[p, :, pl.ds(pl.multiple_of(first * step, step), n * step)]

    def away(p, first):
        value = layer_of(1, second_operand(p, first, 2), blocks_of(p, first, 2))
        for t in range(2):
            fs[p, first + t] = value[:, t * step:(t + 1) * step]

    def home(ps):
        def half(n, carry):
            t = jnp.where(n == 0, partner, T)
            value = layer_of(
                1,
                jnp.concatenate([second_operand(p, t, 1) for p in ps], axis=1),
                jnp.concatenate([blocks_of(p, t, 1) for p in ps], axis=1),
            )
            parts = [value[:, i * step:(i + 1) * step] for i in range(len(ps))]

            @pl.when(n == 0)
            def _():
                for part, p in zip(parts, ps):
                    fs[p, partner] = part
                    feature_out(0, p).start()

            @pl.when(n == 1)
            def _():
                for part, p in zip(parts, ps):
                    fr[p, T] = part
            return carry

        lax.fori_loop(0, 2, half, 0)

    pairs = list(range(1, own + 2)) + [0]
    rows = [0] + list(range(1, own + 1)) + [0]
    outs = [0, 0] + list(range(1, own)) + [0]
    pairs_first = [1, 2, 0] + list(range(3, own + 2))
    rows_first = [0, 1, 0] + list(range(2, own + 1))
    outs_first = [0, 0, 0] + list(range(1, own))

    def body(i, carry):
        q, r, p = (
            jnp.where(down, pick(i, usual), pick(i, first))
            for usual, first in ((pairs, pairs_first), (rows, rows_first), (outs, outs_first))
        )

        @pl.when((q >= 1) & (q <= own))
        def _():
            for k in range(3):
                @pl.when((k > 0) | ((q != 1) & (q != own)))
                def _(k=k):
                    signal_in(k, q).wait_recv()

        @pl.when((q == 1) & down)
        def _():
            halo_down(1).start()

        @pl.when((q == 2) & down)
        def _():
            for k in (1, 2):
                edge_up(k).wait_recv()
                relay_out(k).start()

        @pl.when((q == own + 1) & up)
        def _():
            for n in range(2):
                halo_down(n).wait_recv()

        @pl.when((q == 0) & down)
        def _():
            halo_up(0).wait_recv()
            for k in (1, 2):
                relay_in(k).wait_recv()

        pair(q)

        for where, blocks, theirs in ((0, nt, 2), (2, 2, 0)):
            @pl.when((i >= 1) & (chip == where))
            def _(blocks=blocks):
                across(r)
                middle([r], 0, blocks)

            @pl.when((i >= 2) & (chip == where))
            def _(blocks=blocks, theirs=theirs):
                join(p, 0, blocks)
                away(p, theirs)

        @pl.when((i >= 2) & outer)
        def _():
            for k in (2, 1):
                feature_out(k, p).start()

        @pl.when((i >= 2) & jnp.logical_not(outer))
        def _():
            for k in (1, 2):
                feature_out(k, p).start()
        return carry

    outer = (T == 0) | (T == nt - 1)
    lax.fori_loop(0, own + 2, body, 0)

    @pl.when(chip == 2)
    def _():
        middle(list(range(own + 1)), 2, 2)
        for p in range(own):
            join(p, 2, 2)

    home(list(range(own)))

    def finish(i, carry):
        p = jnp.where(down, lax.rem(i + 1, own), i)
        for k in range(3):
            feature_in(k, p).wait_recv()
        for n, value in enumerate(swap([fr[p, t] for t in range(nt)])):
            out_ref[pl.ds(n // 2 * fib + 2 * p + n % 2, ch, stride=fib * 2), :] = value
        return carry

    lax.fori_loop(0, own, finish, 0)

    for k in range(3):
        for q in range(1, own + 1):
            signal_out(k, q).wait_send()
            feature_out(k, q - 1).wait_send()
    @pl.when(up)
    def _():
        halo_up(0).wait_send()
        for k in (1, 2):
            edge_up(k).wait_send()

    @pl.when(down)
    def _():
        for n in range(2):
            halo_down(n).wait_send()
        for k in (1, 2):
            relay_out(k).wait_send()


def solution(mesh):
    nt, nf = mesh.shape["tm"], mesh.shape["fibre"]
    placed = (P(None, "fibre", "tm"), P(), P(), P(), P(), P(), P())

    def body(signal, w1, b1, r1, w2, b2, r2):
        ch, fib, length = signal.shape
        assert length == DILATION_TWO == 2 * DILATION_ONE and nt % 2 == 0 and fib == FIB_DEV
        x = signal.reshape(ch, fib, length // 128, 128).transpose(0, 2, 1, 3).reshape(-1, 128)
        out_ch = w1.shape[2]
        own = fib // 2
        w1, w2 = jnp.transpose(w1, (0, 1, 3, 2)), jnp.transpose(w2, (0, 1, 3, 2))
        b1 = b1.reshape(1, out_ch)
        b2 = b2.reshape(1, out_ch)
        dma = lambda n: pltpu.SemaphoreType.DMA((n,))
        inputs = [
            pltpu.VMEM(x.shape, F32),
            pltpu.VMEM(w1.shape, F32), pltpu.VMEM(b1.shape, F32), pltpu.VMEM(r1.shape, F32),
            pltpu.VMEM(w2.shape, F32), pltpu.VMEM(b2.shape, F32), pltpu.VMEM(r2.shape, F32),
            pltpu.VMEM((2, out_ch, 27 * ch), BF), pltpu.VMEM((2, ch, 3 * ch), BF),
            pltpu.VMEM((2, out_ch, out_ch), F32),
        ]
        step = DILATION_ONE
        if nt == 4:
            form = spread_kernel
            scratch = inputs + [
                pltpu.VMEM((nt, own, ch, step), F32), pltpu.VMEM((own + 2, nt, ch, step), F32),
                pltpu.VMEM((own + 1, ch, nt * step), F32),
                pltpu.VMEM((2, 2, own + 2, 2, ch, (nt + 1) * step), BF),
                pltpu.VMEM((own + 1, nt, ch, step), F32),
                pltpu.VMEM((2, own + 1, 2, ch, (nt + 2) * step), BF),
                pltpu.VMEM((own, nt, ch, step), F32), pltpu.VMEM((own, nt, ch, step), F32),
                pltpu.VMEM((2, ch, step), F32),
                dma(1), dma(6), dma(3 * own), dma(3 * own), dma(4), dma(4), dma(3 * own), dma(3 * own),
                dma(2), dma(2), dma(2), dma(2),
            ]
        else:
            form = kernel
            scratch = [
                pltpu.VMEM((2, 4, own + 2, ch, 2 * length), F32),
                pltpu.VMEM((2, own + 2, 4 * length // step, 2, ch, 2 * step), BF),
            ] + inputs + [
                dma(1), dma(6), dma(2), dma(2), dma(2), dma(2), dma(own + 2), dma(own + 2),
                dma(own + 2), dma(own + 2), dma(own + 2), dma(own + 2),
                dma(own + 1), dma(own + 1), dma(3), dma(3),
                pltpu.SemaphoreType.REGULAR,
            ]
        out = pl.pallas_call(
            lambda *refs: form(nt, nf, fib, *refs),
            name="gated_layers",
            out_shape=pltpu.VMEM(x.shape, F32),
            in_specs=[pl.BlockSpec(memory_space=pl.ANY)] * 7,
            out_specs=pl.BlockSpec(memory_space=pltpu.VMEM),
            scratch_shapes=scratch,
            compiler_params=pltpu.CompilerParams(
                collective_id=0, has_side_effects=True, vmem_limit_bytes=60 * 1024 * 1024
            ),
        )(x, w1, b1, r1, w2, b2, r2)
        out = out.reshape(ch, length // 128, fib, 128).transpose(0, 2, 1, 3)
        return out.reshape(ch, fib, length)

    return jax.shard_map(body, mesh=mesh, in_specs=placed, out_specs=P(None, "fibre", "tm"), check_vma=False)
```

```python
import jax
import jax.numpy as jnp
from jax import lax
from jax.experimental import pallas as pl
from jax.experimental.pallas import tpu as pltpu
from jax.sharding import PartitionSpec as P

DILATION_ONE = 128
DILATION_TWO = 256
FIB_DEV = 8
BF = jnp.bfloat16
F32 = jnp.float32


def split(value):
    hi = value.astype(BF)
    return hi, (value - hi.astype(F32)).astype(BF)


def pick(i, values):
    out = jnp.int32(values[-1])
    for n in range(len(values) - 2, -1, -1):
        out = jnp.where(i == n, jnp.int32(values[n]), out)
    return out


def kernel(
    nt, nf, fib,
    x_hbm, w1_hbm, b1_hbm, r1_hbm, w2_hbm, b2_hbm, r2_hbm, out_ref,
    af, ab, xv, w1, b1, r1, w2, b2, r2, taps, mix, tall,
    in_sem, w_sem, h0s, h0r, h2s, h2r, xs, xr, ps, pr, ts, tr, ms, mr, es, er, go,
):
    s, m = af.at[0], af.at[1]
    T = lax.axis_index("tm")
    F = lax.axis_index("fibre")
    odd = lax.rem(T, 2)
    even = odd == 0
    isodd = odd == 1
    late = T >= 2
    partner = T + 1 - 2 * odd
    ch, length = af.shape[3], af.shape[4] // 2
    own = fib // 2
    wide = own + 2
    mid = own + 1
    out_ch = 2 * ch
    step = DILATION_ONE
    far = nt > 4
    up, down = F + 1 < nf, F > 0
    onward = T + 2 < nt
    inner = list(range(1, own + 1))
    arrive = [1, own] + list(range(2, own))
    edges = [0, own + 1]

    def dev(t, f):
        return {"tm": t, "fibre": f}

    load = pltpu.make_async_copy(x_hbm, xv, in_sem.at[0])
    load.start()
    weights = [
        pltpu.make_async_copy(a, b, w_sem.at[i])
        for i, (a, b) in enumerate(
            [(w1_hbm, w1), (b1_hbm, b1), (r1_hbm, r1), (w2_hbm, w2), (b2_hbm, b2), (r2_hbm, r2)]
        )
    ]
    for c in weights:
        c.start()

    barrier = pltpu.get_barrier_semaphore()
    friends = [(partner, F, None), (T, F + 1, up), (T, F - 1, down), (T + 2, F, onward), (T - 2, F, late)]
    if far:
        send3 = isodd & (T + 3 < nt)
        recv3 = even & (T >= 4)
        for e, ok in ((0, None), (1, up), (-1, down)):
            for d, okt in ((3, send3), (-3, recv3)):
                friends.append((T + d, F + e, okt if ok is None else okt & ok))
    count = jnp.int32(0)
    for t, f, ok in friends:
        if ok is None:
            pl.semaphore_signal(barrier, inc=1, device_id=dev(t, f), device_id_type=pl.DeviceIdType.MESH)
            count = count + 1
        else:
            @pl.when(ok)
            def _(t=t, f=f):
                pl.semaphore_signal(barrier, inc=1, device_id=dev(t, f), device_id_type=pl.DeviceIdType.MESH)
            count = count + ok.astype(jnp.int32)

    load.wait()
    for f in range(fib):
        for h in range(2):
            value = xv[pl.ds(h * fib + f, ch, stride=fib * 2), :]
            lanes = pl.ds((f % 2) * step, step)
            af[0, 0, 1 + f // 2, :, pl.ds((2 * h + f % 2) * step, step)] = value
            hi, lo = split(value)
            ab[0, 1 + f // 2, 6 + h, 0, :, lanes] = hi
            ab[0, 1 + f // 2, 6 + h, 1, :, lanes] = lo
    pl.semaphore_wait(barrier, count)

    def remote(src, dst, ssem, rsem, t, f):
        return pltpu.make_async_remote_copy(
            src_ref=src, dst_ref=dst, send_sem=ssem, recv_sem=rsem,
            device_id=dev(t, f), device_id_type=pl.DeviceIdType.MESH,
        )

    def halo_up(j, ss, rr):
        return remote(s.at[j, own], s.at[j, 0], ss.at[0], rr.at[0], T, F + 1)

    def halo_down(j, ss, rr):
        return remote(s.at[j, 1], s.at[j, own + 1], ss.at[1], rr.at[1], T, F - 1)

    def cross(q):
        return remote(s.at[0, q], s.at[2, q], xs.at[q], xr.at[q], T + 2, F)

    def part(src, q):
        return remote(s.at[src, q], s.at[1, q], ps.at[q], pr.at[q], partner, F)

    def part3(q):
        return remote(s.at[2, q], s.at[3, q], ts.at[q], tr.at[q], partner, F)

    def share(src, r):
        return remote(m.at[src, r], m.at[1, r], ms.at[r], mr.at[r], partner, F)

    @pl.when(onward & even)
    def _():
        for q in arrive:
            cross(q).start()

    @pl.when(up)
    def _():
        halo_up(0, h0s, h0r).start()

    @pl.when(down)
    def _():
        halo_down(0, h0s, h0r).start()

    @pl.when(even)
    def _():
        for q in arrive:
            part(0, q).start()

    if far:
        def third(i, e):
            if e == 0:
                src, dst = s.at[0, pl.ds(1, own)], s.at[3, pl.ds(1, own)]
            elif e == 1:
                src, dst = s.at[0, own], s.at[3, 0]
            else:
                src, dst = s.at[0, 1], s.at[3, own + 1]
            return remote(src, dst, es.at[i], er.at[i], T + 3, F + e)

        thirds_list = [(0, 0, None, None), (1, 1, up, down), (2, -1, down, up)]
        for i, e, ok, _ok in thirds_list:
            @pl.when(send3 if ok is None else send3 & ok)
            def _(i=i, e=e):
                third(i, e).start()

    zero = jnp.zeros(af.shape[3:], F32)

    def zero_halo(j):
        @pl.when(jnp.logical_not(down))
        def _():
            af[0, j, 0] = zero

        @pl.when(jnp.logical_not(up))
        def _():
            af[0, j, own + 1] = zero

    zero_halo(0)

    def no_chunks(layer, first, n):
        for q in range(wide if layer == 0 else mid):
            ab[layer, q, pl.ds(first, n)] = jnp.zeros((n,) + ab.shape[3:], BF)

    @pl.when(T == 0)
    def _():
        no_chunks(0, 4, 2)
        no_chunks(1, 4, 2)

    @pl.when(T < 2)
    def _():
        no_chunks(1, 2, 2)

    @pl.when(T == 2)
    def _():
        no_chunks(0, 0, 2)

    @pl.when(late)
    def _():
        zero_halo(2)

    if far:
        @pl.when(recv3)
        def _():
            zero_halo(3)

    for c in weights:
        c.wait()

    def prepare(layer, w, r, bias):
        for a in range(3):
            for k in range(3):
                hi, lo = split(w[a, k].T)
                for i, piece in enumerate((hi, hi, lo)):
                    taps[layer, :, pl.ds((9 * a + 3 * k + i) * ch, ch)] = piece
        hi, lo = split(r[...])
        for i, piece in enumerate((hi, hi, lo)):
            mix[layer, :, pl.ds(i * ch, ch)] = piece
        tall[layer] = jnp.broadcast_to(bias[...], (out_ch, out_ch)).T

    prepare(0, w1, r1, b1)
    prepare(1, w2, r2, b2)

    def ingest(layer, j, q):
        hi, lo = split(af[layer, j, q])
        for h in range(2):
            ab[layer, q, 2 * (3 - j) + h, 0] = hi[:, h * 2 * step:(h + 1) * 2 * step]
            ab[layer, q, 2 * (3 - j) + h, 1] = lo[:, h * 2 * step:(h + 1) * 2 * step]

    @pl.when(onward & even)
    def _():
        for q in arrive[:-1]:
            cross(q).wait_send()
        pl.semaphore_signal(go, inc=1, device_id=dev(partner, F), device_id_type=pl.DeviceIdType.MESH)

    @pl.when(onward & isodd)
    def _():
        pl.semaphore_wait(go, 1)
        for q in arrive:
            cross(q).start()

    if far:
        @pl.when(recv3)
        def _():
            for i, e, _ok, ok in thirds_list:
                if ok is None:
                    third(i, e).wait_recv()
                else:
                    @pl.when(ok)
                    def _(i=i, e=e):
                        third(i, e).wait_recv()

            def old(q, carry):
                ingest(0, 3, q)
                return carry

            lax.fori_loop(0, wide, old, 0)

    late_even, late_odd = late & even, late & isodd

    def halos_in(j, ss, rr):
        @pl.when(down)
        def _():
            halo_up(j, ss, rr).wait_recv()

        @pl.when(up)
        def _():
            halo_down(j, ss, rr).wait_recv()

    def crossed(q):
        cross(q).wait_recv()

        @pl.when(even)
        def _():
            part3(q).start()

        @pl.when(isodd)
        def _():
            part(2, q).start()

        if q == 1:
            @pl.when(down)
            def _():
                halo_down(2, h2s, h2r).start()

        if q == own:
            @pl.when(up)
            def _():
                halo_up(2, h2s, h2r).start()

    def event(i):
        if i == 0:
            @pl.when(late_even)
            def _():
                for q in arrive:
                    crossed(q)

            @pl.when(isodd)
            def _():
                for q in arrive:
                    part(0, q).wait_recv()
        if i == 1:
            @pl.when(late_odd)
            def _():
                crossed(arrive[0])

            halos_in(0, h0s, h0r)

            @pl.when(even)
            def _():
                for q in edges:
                    part(0, q).start()

            @pl.when(isodd)
            def _():
                for q in edges:
                    part(0, q).wait_recv()

            @pl.when(late_even)
            def _():
                halos_in(2, h2s, h2r)
                for q in edges:
                    part3(q).start()
        if i in (2, 3):
            now = arrive[:-1] if i == 2 else arrive[-1:]

            @pl.when(late_even)
            def _():
                for q in now:
                    part(0, q).wait_recv()

            @pl.when(late_odd)
            def _():
                for q in now:
                    if q != arrive[0]:
                        crossed(q)
                for q in now:
                    part3(q).wait_recv()
        if i == 4:
            @pl.when(late_even)
            def _():
                for q in edges:
                    part(0, q).wait_recv()

            @pl.when(late_odd)
            def _():
                halos_in(2, h2s, h2r)
                for q in edges:
                    part(2, q).start()
                for q in edges:
                    part3(q).wait_recv()
        if i == 5:
            @pl.when(T >= 1)
            def _():
                for r in range(1, own):
                    share(0, r).wait_recv()
        if i == 6:
            @pl.when(T >= 1)
            def _():
                for r in (0, own):
                    share(0, r).wait_recv()

    rows = [
        (("A", 1), ("A", 2)), (("A", 3), ("A", 0)), (("A", own), ("B", 1)), (("B", 2), ("B", 3)), (("B", 0), ("B", own)),
        (("C", 1), ("C", 2)), (("C", 0), ("C", own - 1)),
    ]
    steps = len(rows)
    first_of_two = steps - 2
    ja = jnp.where(late_even, 2, 0)
    jb = jnp.where(even, 0, 2)
    start = [1, 0, 1, 3, 0, 1, 0]
    number = [own, 2, 2, own - 2, 2, own - 1, 2]
    stride = [1, own + 1, 1, 1, own + 1, 1, own]
    le = [(2,), (0, 2), (1,), (1,), (1,), (1,), (1,)]
    lo_ = [(1,), (0, 1), (2, 3), (2, 3), (2, 3), (1,), (1,)]
    ee = [(), (0,), (), (), (), (), ()]
    eo = [(1,), (0, 1), (), (), (), (1,), (1,)]

    def by_class(i, of):
        table = [pick(i, [of(entry) for entry in c]) for c in (le, lo_, ee, eo)]
        return jnp.where(late, jnp.where(even, table[0], table[1]), jnp.where(even, table[2], table[3]))

    def operand(layer, r, b, d):
        pieces = []
        for a in range(3):
            for k in range(3):
                both = []
                for part_ in range(2):
                    cols = []
                    for h in range(2):
                        c = 2 * b + h - k * d
                        if a == 0:
                            cols.append(ab[layer, r, c, part_])
                        elif a == 2:
                            cols.append(ab[layer, r + 1, c, part_])
                        else:
                            cols += [ab[layer, r, c, part_, :, step:], ab[layer, r + 1, c, part_, :, :step]]
                    both.append(jnp.concatenate(cols, axis=1))
                pieces += [both[0], both[1], both[0]]
        return jnp.concatenate(pieces, axis=0)

    def straddle(layer, j, r):
        cols = []
        for h in range(2):
            cols += [af[layer, j, r, :, (2 * h + 1) * step:(2 * h + 2) * step], af[layer, j, r + 1, :, 2 * h * step:(2 * h + 1) * step]]
        return jnp.concatenate(cols, axis=1)

    def compute(layer, d, units):
        right = jnp.concatenate([operand(layer, r, 3 - j, d) for r, j in units], axis=1)
        total = jnp.dot(taps[layer], right, preferred_element_type=F32)
        pre = total + jnp.concatenate([tall[layer]] * (total.shape[1] // out_ch), axis=1)
        g = jnp.tanh(pre[:ch]) * (0.5 * jnp.tanh(0.5 * pre[ch:]) + 0.5)
        hi, lo = split(g)
        base = jnp.concatenate([straddle(layer, j, r) for r, j in units], axis=1)
        return base + jnp.dot(mix[layer], jnp.concatenate([hi, lo, hi], axis=0), preferred_element_type=F32)

    def body(i, carry):
        for n in range(steps):
            @pl.when(i == n)
            def _(n=n):
                event(n)

        first, each, pace = pick(i, start), pick(i, number), pick(i, stride)
        j0 = by_class(i, lambda e: e[0] if e else 0)
        j1 = by_class(i, lambda e: e[1] if len(e) > 1 else 0)
        blocks = by_class(i, len)
        layer = (i >= first_of_two).astype(jnp.int32)

        def take(n, carry):
            second = n >= each
            q = first + pace * jnp.where(second, n - each, n)
            ingest(layer, jnp.where(second, j1, j0), q)
            return carry

        lax.fori_loop(0, each * blocks, take, 0)

        units = []
        for lane in range(2):
            r = pick(i, [pair[lane][1] for pair in rows])
            kind = pick(i, ["ABC".index(pair[lane][0]) for pair in rows])
            if any(pair[lane][0] == "B" and pair[0][0] == "A" for pair in rows):
                r = jnp.where((kind == 1) & jnp.logical_not(late), own, r)
            j = jnp.where(kind == 0, ja, jnp.where(kind == 1, jnp.where(late, jb, 0), 0))
            units.append((r, j, kind))

        @pl.when(late | (i < 3) | (i >= first_of_two))
        def _():
            value = compute(layer, layer + 1, [(r, j) for r, j, _ in units])

            @pl.when(layer == 0)
            def _():
                for n, (r, j, kind) in enumerate(units):
                    v = value[:, n * 2 * length:(n + 1) * 2 * length]
                    row = F * fib + 2 * r - 1
                    ok = [(row >= 0) & (row < nf * fib), (row + 1 >= 0) & (row + 1 < nf * fib)]
                    v = jnp.concatenate([jnp.where(ok[p % 2], v[:, p * step:(p + 1) * step], 0.0) for p in range(4)], axis=1)
                    af[1, j, r] = v
                    hi, lo = split(v)
                    for h in range(2):
                        ab[1, r, 2 * (3 - j) + h, 0] = hi[:, h * 2 * step:(h + 1) * 2 * step]
                        ab[1, r, 2 * (3 - j) + h, 1] = lo[:, h * 2 * step:(h + 1) * 2 * step]

                for r, j, kind in units:
                    @pl.when((late & (kind == 1)) | ((T == 0) & (kind == 0)))
                    def _(r=r, j=j):
                        share(j, r).start()

            @pl.when(layer == 1)
            def _():
                for n, (r, j, kind) in enumerate(units):
                    for p in range(4):
                        h, e = p // 2, p % 2
                        at = n * 2 * length + p * step
                        out_ref[pl.ds(h * fib + 2 * r + e, ch, stride=fib * 2), :] = value[:, at:at + step]
        return carry

    lax.fori_loop(0, steps, body, 0)

    @pl.when(onward & even)
    def _():
        cross(arrive[-1]).wait_send()

    @pl.when(onward & isodd)
    def _():
        for q in arrive:
            cross(q).wait_send()

    for j, ss, rr, ok in ((0, h0s, h0r, None), (2, h2s, h2r, late)):
        @pl.when(up if ok is None else up & ok)
        def _(j=j, ss=ss, rr=rr):
            halo_up(j, ss, rr).wait_send()

        @pl.when(down if ok is None else down & ok)
        def _(j=j, ss=ss, rr=rr):
            halo_down(j, ss, rr).wait_send()

    for q in range(wide):
        @pl.when(even | late)
        def _(q=q):
            part(0, q).wait_send()

        @pl.when(late_even)
        def _(q=q):
            part3(q).wait_send()

    @pl.when(even | late)
    def _():
        for r in range(mid):
            share(0, r).wait_send()

    if far:
        for i, e, ok, _ok in thirds_list:
            @pl.when(send3 if ok is None else send3 & ok)
            def _(i=i, e=e):
                third(i, e).wait_send()


def spread_kernel(
    nt, nf, fib,
    x_hbm, w1_hbm, b1_hbm, r1_hbm, w2_hbm, b2_hbm, r2_hbm, out_ref,
    xv, w1, b1, r1, w2, b2, r2, taps, mix, tall, pk, af, sf, ab, mf, mb, fs, fr, held,
    in_sem, w_sem, xs, xr, hs, hr, gs, gr, us, ur, vs, vr,
):
    T = lax.axis_index("tm")
    F = lax.axis_index("fibre")
    odd = lax.rem(T, 2)
    partner = T + 1 - 2 * odd
    peers = [partner, lax.rem(T + 2, nt), lax.rem(partner + 2, nt)]
    chip = T - odd
    other = lax.rem(chip + 2, nt)
    ch = pk.shape[2]
    own = fib // 2
    out_ch = 2 * ch
    step = DILATION_ONE
    group = step // nt
    up, down = F + 1 < nf, F > 0
    lane = lax.broadcasted_iota(jnp.int32, (ch, step), 1)
    early_half = lane < 2 * group
    first_fibre = lax.rem(lane, 2 * group) < group

    def dev(t, f):
        return {"tm": t, "fibre": f}

    barrier = pltpu.get_barrier_semaphore()
    for p in peers:
        pl.semaphore_signal(barrier, inc=1, device_id=dev(p, F), device_id_type=pl.DeviceIdType.MESH)
    count = jnp.int32(len(peers))
    for e, ok in ((1, up), (-1, down)):
        @pl.when(ok)
        def _(e=e):
            pl.semaphore_signal(barrier, inc=1, device_id=dev(T, F + e), device_id_type=pl.DeviceIdType.MESH)
        count = count + ok.astype(jnp.int32)

    load = pltpu.make_async_copy(x_hbm, xv, in_sem.at[0])
    load.start()
    weights = [
        pltpu.make_async_copy(a, b, w_sem.at[i])
        for i, (a, b) in enumerate(
            [(w1_hbm, w1), (b1_hbm, b1), (r1_hbm, r1), (w2_hbm, w2), (b2_hbm, b2), (r2_hbm, r2)]
        )
    ]
    for c in weights:
        c.start()

    def swap(parts):
        a, b, c, d = parts
        half = 2 * group
        a, c = jnp.where(early_half, a, pltpu.roll(c, half, 1)), jnp.where(early_half, pltpu.roll(a, half, 1), c)
        b, d = jnp.where(early_half, b, pltpu.roll(d, half, 1)), jnp.where(early_half, pltpu.roll(b, half, 1), d)
        back = step - group
        a, b = jnp.where(first_fibre, a, pltpu.roll(b, group, 1)), jnp.where(first_fibre, pltpu.roll(a, back, 1), b)
        c, d = jnp.where(first_fibre, c, pltpu.roll(d, group, 1)), jnp.where(first_fibre, pltpu.roll(c, back, 1), d)
        return a, b, c, d

    load.wait()

    def pack(q):
        parts = [xv[pl.ds(h * fib + 2 * q + e, ch, stride=fib * 2), :] for h in range(2) for e in range(2)]
        for t, value in enumerate(swap(parts)):
            pk[t, q] = value

            @pl.when(T == t)
            def _(value=value):
                af[q + 1, t] = value

    pack(0)
    pl.semaphore_wait(barrier, count)

    def remote(src, dst, ssem, rsem, t, f):
        return pltpu.make_async_remote_copy(
            src_ref=src, dst_ref=dst, send_sem=ssem, recv_sem=rsem,
            device_id=dev(t, f), device_id_type=pl.DeviceIdType.MESH,
        )

    def signal_out(k, q):
        n = k * own + q - 1
        return remote(pk.at[peers[k], q - 1], af.at[q, T], xs.at[n], xr.at[n], peers[k], F)

    def signal_in(k, q):
        n = k * own + q - 1
        return remote(pk.at[peers[k], q - 1], af.at[q, peers[k]], xs.at[n], xr.at[n], peers[k], F)

    def halo_up(n):
        blocks = pl.ds((chip, other)[n], 2)
        return remote(af.at[own, blocks], af.at[0, blocks], hs.at[2 * n], hr.at[2 * n], T, F + 1)

    def halo_down(n):
        blocks = pl.ds((chip, other)[n], 2)
        return remote(af.at[1, blocks], af.at[own + 1, blocks], hs.at[2 * n + 1], hr.at[2 * n + 1], T, F - 1)

    def edge_up(k):
        return remote(pk.at[peers[k], own - 1], held.at[k - 1], us.at[k - 1], ur.at[k - 1], T, F + 1)

    def relay_out(k):
        return remote(held.at[k - 1], af.at[0, T], vs.at[k - 1], vr.at[k - 1], peers[k], F)

    def relay_in(k):
        return remote(held.at[k - 1], af.at[0, peers[k]], vs.at[k - 1], vr.at[k - 1], peers[k], F)

    def feature_out(k, p):
        n = k * own + p
        return remote(fs.at[p, peers[k]], fr.at[p, T], gs.at[n], gr.at[n], peers[k], F)

    def feature_in(k, p):
        n = k * own + p
        return remote(fs.at[p, peers[k]], fr.at[p, peers[k]], gs.at[n], gr.at[n], peers[k], F)

    def begin(i, carry):
        q = i + 1

        @pl.when(i > 0)
        def _():
            pack(i)
        for k in (1, 2, 0):
            signal_out(k, q).start()
        return carry

    lax.fori_loop(0, own, begin, 0)

    @pl.when(up)
    def _():
        for k in (1, 2):
            edge_up(k).start()

    no_rows = jnp.zeros((nt, ch, step), F32)

    @pl.when(jnp.logical_not(down))
    def _():
        af[0] = no_rows

    @pl.when(jnp.logical_not(up))
    def _():
        af[own + 1] = no_rows

    for q in range(own + 2):
        for kind in range(2):
            ab[kind, 0, q, :, :, :step] = jnp.zeros((2, ch, step), BF)
            if q <= own:
                mb[kind, q, :, :, :2 * step] = jnp.zeros((2, ch, 2 * step), BF)

    for q in (1, own):
        signal_in(0, q).wait_recv()

    @pl.when(up)
    def _():
        halo_up(0).start()

    @pl.when(down)
    def _():
        halo_down(0).start()

    for c in weights:
        c.wait()

    def prepare(layer, w, r, bias):
        for a in range(3):
            for k in range(3):
                hi, lo = split(w[a, k].T)
                for i, piece in enumerate((hi, hi, lo)):
                    taps[layer, :, pl.ds((9 * a + 3 * k + i) * ch, ch)] = piece
        hi, lo = split(r[...])
        for i, piece in enumerate((hi, hi, lo)):
            mix[layer, :, pl.ds(i * ch, ch)] = piece
        tall[layer] = jnp.broadcast_to(bias[...], (out_ch, out_ch)).T

    prepare(0, w1, r1, b1)
    prepare(1, w2, r2, b2)

    def keep(ref, kind, q, values, lead, shifted, later=None):
        for t, value in enumerate(values):
            at = pl.ds((t + lead) * step, step)
            hi, lo = split(value)
            if shifted:
                turned = pltpu.roll(value, 2 * group, 1)
                before = jnp.where(early_half, jnp.zeros_like(turned) if later is None else later, turned)
                later = turned
                ref[kind, 0, q, 0, :, at], ref[kind, 0, q, 1, :, at] = hi, lo
                hi, lo = split(before)
                ref[kind, 1, q, 0, :, at], ref[kind, 1, q, 1, :, at] = hi, lo
            else:
                ref[kind, q, 0, :, at], ref[kind, q, 1, :, at] = hi, lo

    def pair(q, first, n):
        later = pltpu.roll(af[q, first - 1], 2 * group, 1) if first else None
        keep(ab, 0, q, [af[q, t] for t in range(first, first + n)], first + 1, True, later)

    def between(left, right):
        return jnp.where(first_fibre, pltpu.roll(left, step - group, 1), pltpu.roll(right, group, 1))

    def across(r, first, n):
        values = [between(af[r, t], af[r + 1, t]) for t in range(first, first + n)]
        for t in range(n):
            sf[r, :, pl.ds((first + t) * step, step)] = values[t]
        later = pltpu.roll(between(af[r, first - 1], af[r + 1, first - 1]), 2 * group, 1) if first else None
        keep(ab, 1, r, values, first + 1, True, later)

    def first_operand(r, first, n):
        pieces = []
        for kind, q in ((0, r), (1, r), (0, r + 1)):
            for early, back in ((0, 0), (1, 0), (0, 1)):
                lanes = slice((first + 1 - back) * step, (first + 1 - back + n) * step)
                hi, lo = ab[kind, early, q, 0, :, lanes], ab[kind, early, q, 1, :, lanes]
                pieces += [hi, lo, hi]
        return jnp.concatenate(pieces, axis=0)

    def second_operand(p, first, n):
        pieces = []
        for kind, q in ((0, p), (1, p), (0, p + 1)):
            for k in range(3):
                lanes = pl.ds(pl.multiple_of((2 - k + first) * step, step), n * step)
                hi, lo = mb[kind, q, 0, :, lanes], mb[kind, q, 1, :, lanes]
                pieces += [hi, lo, hi]
        return jnp.concatenate(pieces, axis=0)

    def layer_of(layer, right, base):
        total = jnp.dot(taps[layer], right, preferred_element_type=F32)
        pre = total + jnp.concatenate([tall[layer]] * (total.shape[1] // out_ch), axis=1)
        g = jnp.tanh(pre[:ch]) * (0.5 * jnp.tanh(0.5 * pre[ch:]) + 0.5)
        hi, lo = split(g)
        return base + jnp.dot(mix[layer], jnp.concatenate([hi, lo, hi], axis=0), preferred_element_type=F32)

    def middle(rows, first, n):
        value = layer_of(
            0,
            jnp.concatenate([first_operand(r, first, n) for r in rows], axis=1),
            jnp.concatenate([sf[r, :, first * step:(first + n) * step] for r in rows], axis=1),
        )
        for i, r in enumerate(rows):
            row = F * fib + 2 * r - 1
            ok = [((f >= 0) & (f < nf * fib)).astype(jnp.int32) for f in (row, row + 1)]
            inside = jnp.where(first_fibre, ok[0], ok[1]) == 1
            parts = [jnp.where(inside, value[:, t * step:(t + 1) * step], 0.0) for t in range(i * n, (i + 1) * n)]
            for t in range(n):
                mf[r, first + t] = parts[t]
            keep(mb, 0, r, parts, first + 2, False)

    def join(p, first, n):
        values = [between(mf[p, t], mf[p + 1, t]) for t in range(first, first + n)]
        keep(mb, 1, p, values, first + 2, False)
        for t in range(n):
            sf[p, :, pl.ds((first + t) * step, step)] = values[t]

    def blocks_of(p, first, n):
        return sf[p, :, pl.ds(pl.multiple_of(first * step, step), n * step)]

    def away(p, first):
        value = layer_of(1, second_operand(p, first, 2), blocks_of(p, first, 2))
        for t in range(2):
            fs[p, first + t] = value[:, t * step:(t + 1) * step]

    def home(ps):
        def half(n, carry):
            t = jnp.where(n == 0, partner, T)
            value = layer_of(
                1,
                jnp.concatenate([second_operand(p, t, 1) for p in ps], axis=1),
                jnp.concatenate([blocks_of(p, t, 1) for p in ps], axis=1),
            )
            parts = [value[:, i * step:(i + 1) * step] for i in range(len(ps))]

            @pl.when(n == 0)
            def _():
                for part, p in zip(parts, ps):
                    fs[p, partner] = part
                    feature_out(0, p).start()

            @pl.when(n == 1)
            def _():
                for part, p in zip(parts, ps):
                    fr[p, T] = part
            return carry

        lax.fori_loop(0, 2, half, 0)

    pairs = list(range(1, own + 2)) + [0]
    rows = [0] + list(range(1, own + 1)) + [0]
    outs = [0, 0] + list(range(1, own)) + [0]
    pairs_first = [1, 0] + list(range(2, own + 2))
    rows_first = [0, 0] + list(range(1, own + 1))
    outs_first = [0, 0] + list(range(own))

    def body(i, carry):
        q, r, p = (
            jnp.where(down, pick(i, usual), pick(i, first))
            for usual, first in ((pairs, pairs_first), (rows, rows_first), (outs, outs_first))
        )

        @pl.when((q >= 1) & (q <= own))
        def _():
            for k in (1, 2):
                signal_in(k, q).wait_recv()

        @pl.when((q == 1) & down)
        def _():
            halo_down(1).start()

        @pl.when((q == 2) & down)
        def _():
            for k in (1, 2):
                edge_up(k).wait_recv()
                relay_out(k).start()

        @pl.when((q == own + 1) & up)
        def _():
            for n in range(2):
                halo_down(n).wait_recv()

        @pl.when((q == 0) & down)
        def _():
            halo_up(0).wait_recv()
            for k in (1, 2):
                relay_in(k).wait_recv()

        inner_pair = (q >= 1) & (q <= own) & (chip == 0)
        inner_row = (r >= 1) & (r <= own - 1) & (chip == 0)

        @pl.when(inner_pair)
        def _():
            pair(q, 2, 2)

        @pl.when(jnp.logical_not(inner_pair))
        def _():
            pair(q, 0, nt)

        @pl.when((i >= 1) & inner_row)
        def _():
            across(r, 2, 2)
            middle([r], 2, 2)

        for where, blocks in ((jnp.logical_not(inner_row) & (chip == 0), nt), (chip == 2, 2)):
            @pl.when((i >= 1) & where)
            def _(blocks=blocks):
                across(r, 0, nt)
                middle([r], 0, blocks)

        for where, blocks, theirs in ((0, nt, 2), (2, 2, 0)):
            @pl.when((i >= 2) & (chip == where))
            def _(blocks=blocks, theirs=theirs):
                join(p, 0, blocks)
                away(p, theirs)

        @pl.when((i >= 2) & outer)
        def _():
            for k in (2, 1):
                feature_out(k, p).start()

        @pl.when((i >= 2) & jnp.logical_not(outer))
        def _():
            for k in (1, 2):
                feature_out(k, p).start()
        return carry

    outer = (T == 0) | (T == nt - 1)
    for q in range(2, own):
        signal_in(0, q).wait_recv()

    @pl.when(chip == 0)
    def _():
        def pairs_of_chip(n, carry):
            pair(n + 1, 0, 2)
            return carry

        def rows_of_chip(n, carry):
            across(n + 1, 0, 2)
            return carry

        lax.fori_loop(0, own, pairs_of_chip, 0)
        lax.fori_loop(0, own - 1, rows_of_chip, 0)
        middle(list(range(1, own)), 0, 2)

    lax.fori_loop(0, own + 2, body, 0)

    @pl.when(chip == 2)
    def _():
        middle(list(range(own + 1)), 2, 2)
        for p in range(own):
            join(p, 2, 2)

    home(list(range(own)))

    def finish(i, carry):
        p = jnp.where(down, lax.rem(i + 1, own), i)
        for k in range(3):
            feature_in(k, p).wait_recv()
        for n, value in enumerate(swap([fr[p, t] for t in range(nt)])):
            out_ref[pl.ds(n // 2 * fib + 2 * p + n % 2, ch, stride=fib * 2), :] = value
        return carry

    lax.fori_loop(0, own, finish, 0)

    for k in range(3):
        for q in range(1, own + 1):
            signal_out(k, q).wait_send()
            feature_out(k, q - 1).wait_send()
    @pl.when(up)
    def _():
        halo_up(0).wait_send()
        for k in (1, 2):
            edge_up(k).wait_send()

    @pl.when(down)
    def _():
        for n in range(2):
            halo_down(n).wait_send()
        for k in (1, 2):
            relay_out(k).wait_send()


def solution(mesh):
    nt, nf = mesh.shape["tm"], mesh.shape["fibre"]
    placed = (P(None, "fibre", "tm"), P(), P(), P(), P(), P(), P())

    def body(signal, w1, b1, r1, w2, b2, r2):
        ch, fib, length = signal.shape
        assert length == DILATION_TWO == 2 * DILATION_ONE and nt % 2 == 0 and fib == FIB_DEV
        x = signal.reshape(ch, fib, length // 128, 128).transpose(0, 2, 1, 3).reshape(-1, 128)
        out_ch = w1.shape[2]
        own = fib // 2
        w1, w2 = jnp.transpose(w1, (0, 1, 3, 2)), jnp.transpose(w2, (0, 1, 3, 2))
        b1 = b1.reshape(1, out_ch)
        b2 = b2.reshape(1, out_ch)
        dma = lambda n: pltpu.SemaphoreType.DMA((n,))
        inputs = [
            pltpu.VMEM(x.shape, F32),
            pltpu.VMEM(w1.shape, F32), pltpu.VMEM(b1.shape, F32), pltpu.VMEM(r1.shape, F32),
            pltpu.VMEM(w2.shape, F32), pltpu.VMEM(b2.shape, F32), pltpu.VMEM(r2.shape, F32),
            pltpu.VMEM((2, out_ch, 27 * ch), BF), pltpu.VMEM((2, ch, 3 * ch), BF),
            pltpu.VMEM((2, out_ch, out_ch), F32),
        ]
        step = DILATION_ONE
        if nt == 4:
            form = spread_kernel
            scratch = inputs + [
                pltpu.VMEM((nt, own, ch, step), F32), pltpu.VMEM((own + 2, nt, ch, step), F32),
                pltpu.VMEM((own + 1, ch, nt * step), F32),
                pltpu.VMEM((2, 2, own + 2, 2, ch, (nt + 1) * step), BF),
                pltpu.VMEM((own + 1, nt, ch, step), F32),
                pltpu.VMEM((2, own + 1, 2, ch, (nt + 2) * step), BF),
                pltpu.VMEM((own, nt, ch, step), F32), pltpu.VMEM((own, nt, ch, step), F32),
                pltpu.VMEM((2, ch, step), F32),
                dma(1), dma(6), dma(3 * own), dma(3 * own), dma(4), dma(4), dma(3 * own), dma(3 * own),
                dma(2), dma(2), dma(2), dma(2),
            ]
        else:
            form = kernel
            scratch = [
                pltpu.VMEM((2, 4, own + 2, ch, 2 * length), F32),
                pltpu.VMEM((2, own + 2, 4 * length // step, 2, ch, 2 * step), BF),
            ] + inputs + [
                dma(1), dma(6), dma(2), dma(2), dma(2), dma(2), dma(own + 2), dma(own + 2),
                dma(own + 2), dma(own + 2), dma(own + 2), dma(own + 2),
                dma(own + 1), dma(own + 1), dma(3), dma(3),
                pltpu.SemaphoreType.REGULAR,
            ]
        out = pl.pallas_call(
            lambda *refs: form(nt, nf, fib, *refs),
            name="gated_layers",
            out_shape=pltpu.VMEM(x.shape, F32),
            in_specs=[pl.BlockSpec(memory_space=pl.ANY)] * 7,
            out_specs=pl.BlockSpec(memory_space=pltpu.VMEM),
            scratch_shapes=scratch,
            compiler_params=pltpu.CompilerParams(
                collective_id=0, has_side_effects=True, vmem_limit_bytes=60 * 1024 * 1024
            ),
        )(x, w1, b1, r1, w2, b2, r2)
        out = out.reshape(ch, length // 128, fib, 128).transpose(0, 2, 1, 3)
        return out.reshape(ch, fib, length)

    return jax.shard_map(body, mesh=mesh, in_specs=placed, out_specs=P(None, "fibre", "tm"), check_vma=False)
```

```python
import jax
import jax.numpy as jnp
from jax import lax
from jax.experimental import pallas as pl
from jax.experimental.pallas import tpu as pltpu
from jax.sharding import PartitionSpec as P

DILATION_ONE = 128
DILATION_TWO = 256
FIB_DEV = 8
BF = jnp.bfloat16
F32 = jnp.float32


def split(value):
    hi = value.astype(BF)
    return hi, (value - hi.astype(F32)).astype(BF)


def pick(i, values):
    out = jnp.int32(values[-1])
    for n in range(len(values) - 2, -1, -1):
        out = jnp.where(i == n, jnp.int32(values[n]), out)
    return out


def kernel(
    nt, nf, fib,
    x_hbm, w1_hbm, b1_hbm, r1_hbm, w2_hbm, b2_hbm, r2_hbm, out_ref,
    af, ab, xv, w1, b1, r1, w2, b2, r2, taps, mix, tall,
    in_sem, w_sem, h0s, h0r, h2s, h2r, xs, xr, ps, pr, ts, tr, ms, mr, es, er, go,
):
    s, m = af.at[0], af.at[1]
    T = lax.axis_index("tm")
    F = lax.axis_index("fibre")
    odd = lax.rem(T, 2)
    even = odd == 0
    isodd = odd == 1
    late = T >= 2
    partner = T + 1 - 2 * odd
    ch, length = af.shape[3], af.shape[4] // 2
    own = fib // 2
    wide = own + 2
    mid = own + 1
    out_ch = 2 * ch
    step = DILATION_ONE
    far = nt > 4
    up, down = F + 1 < nf, F > 0
    onward = T + 2 < nt
    inner = list(range(1, own + 1))
    arrive = [1, own] + list(range(2, own))
    edges = [0, own + 1]

    def dev(t, f):
        return {"tm": t, "fibre": f}

    load = pltpu.make_async_copy(x_hbm, xv, in_sem.at[0])
    load.start()
    weights = [
        pltpu.make_async_copy(a, b, w_sem.at[i])
        for i, (a, b) in enumerate(
            [(w1_hbm, w1), (b1_hbm, b1), (r1_hbm, r1), (w2_hbm, w2), (b2_hbm, b2), (r2_hbm, r2)]
        )
    ]
    for c in weights:
        c.start()

    barrier = pltpu.get_barrier_semaphore()
    friends = [(partner, F, None), (T, F + 1, up), (T, F - 1, down), (T + 2, F, onward), (T - 2, F, late)]
    if far:
        send3 = isodd & (T + 3 < nt)
        recv3 = even & (T >= 4)
        for e, ok in ((0, None), (1, up), (-1, down)):
            for d, okt in ((3, send3), (-3, recv3)):
                friends.append((T + d, F + e, okt if ok is None else okt & ok))
    count = jnp.int32(0)
    for t, f, ok in friends:
        if ok is None:
            pl.semaphore_signal(barrier, inc=1, device_id=dev(t, f), device_id_type=pl.DeviceIdType.MESH)
            count = count + 1
        else:
            @pl.when(ok)
            def _(t=t, f=f):
                pl.semaphore_signal(barrier, inc=1, device_id=dev(t, f), device_id_type=pl.DeviceIdType.MESH)
            count = count + ok.astype(jnp.int32)

    load.wait()
    for f in range(fib):
        for h in range(2):
            value = xv[pl.ds(h * fib + f, ch, stride=fib * 2), :]
            lanes = pl.ds((f % 2) * step, step)
            af[0, 0, 1 + f // 2, :, pl.ds((2 * h + f % 2) * step, step)] = value
            hi, lo = split(value)
            ab[0, 1 + f // 2, 6 + h, 0, :, lanes] = hi
            ab[0, 1 + f // 2, 6 + h, 1, :, lanes] = lo
    pl.semaphore_wait(barrier, count)

    def remote(src, dst, ssem, rsem, t, f):
        return pltpu.make_async_remote_copy(
            src_ref=src, dst_ref=dst, send_sem=ssem, recv_sem=rsem,
            device_id=dev(t, f), device_id_type=pl.DeviceIdType.MESH,
        )

    def halo_up(j, ss, rr):
        return remote(s.at[j, own], s.at[j, 0], ss.at[0], rr.at[0], T, F + 1)

    def halo_down(j, ss, rr):
        return remote(s.at[j, 1], s.at[j, own + 1], ss.at[1], rr.at[1], T, F - 1)

    def cross(q):
        return remote(s.at[0, q], s.at[2, q], xs.at[q], xr.at[q], T + 2, F)

    def part(src, q):
        return remote(s.at[src, q], s.at[1, q], ps.at[q], pr.at[q], partner, F)

    def part3(q):
        return remote(s.at[2, q], s.at[3, q], ts.at[q], tr.at[q], partner, F)

    def share(src, r):
        return remote(m.at[src, r], m.at[1, r], ms.at[r], mr.at[r], partner, F)

    @pl.when(onward & even)
    def _():
        for q in arrive:
            cross(q).start()

    @pl.when(up)
    def _():
        halo_up(0, h0s, h0r).start()

    @pl.when(down)
    def _():
        halo_down(0, h0s, h0r).start()

    @pl.when(even)
    def _():
        for q in arrive:
            part(0, q).start()

    if far:
        def third(i, e):
            if e == 0:
                src, dst = s.at[0, pl.ds(1, own)], s.at[3, pl.ds(1, own)]
            elif e == 1:
                src, dst = s.at[0, own], s.at[3, 0]
            else:
                src, dst = s.at[0, 1], s.at[3, own + 1]
            return remote(src, dst, es.at[i], er.at[i], T + 3, F + e)

        thirds_list = [(0, 0, None, None), (1, 1, up, down), (2, -1, down, up)]
        for i, e, ok, _ok in thirds_list:
            @pl.when(send3 if ok is None else send3 & ok)
            def _(i=i, e=e):
                third(i, e).start()

    zero = jnp.zeros(af.shape[3:], F32)

    def zero_halo(j):
        @pl.when(jnp.logical_not(down))
        def _():
            af[0, j, 0] = zero

        @pl.when(jnp.logical_not(up))
        def _():
            af[0, j, own + 1] = zero

    zero_halo(0)

    def no_chunks(layer, first, n):
        for q in range(wide if layer == 0 else mid):
            ab[layer, q, pl.ds(first, n)] = jnp.zeros((n,) + ab.shape[3:], BF)

    @pl.when(T == 0)
    def _():
        no_chunks(0, 4, 2)
        no_chunks(1, 4, 2)

    @pl.when(T < 2)
    def _():
        no_chunks(1, 2, 2)

    @pl.when(T == 2)
    def _():
        no_chunks(0, 0, 2)

    @pl.when(late)
    def _():
        zero_halo(2)

    if far:
        @pl.when(recv3)
        def _():
            zero_halo(3)

    for c in weights:
        c.wait()

    def prepare(layer, w, r, bias):
        for a in range(3):
            for k in range(3):
                hi, lo = split(w[a, k].T)
                for i, piece in enumerate((hi, hi, lo)):
                    taps[layer, :, pl.ds((9 * a + 3 * k + i) * ch, ch)] = piece
        hi, lo = split(r[...])
        for i, piece in enumerate((hi, hi, lo)):
            mix[layer, :, pl.ds(i * ch, ch)] = piece
        tall[layer] = jnp.broadcast_to(bias[...], (out_ch, out_ch)).T

    prepare(0, w1, r1, b1)
    prepare(1, w2, r2, b2)

    def ingest(layer, j, q):
        hi, lo = split(af[layer, j, q])
        for h in range(2):
            ab[layer, q, 2 * (3 - j) + h, 0] = hi[:, h * 2 * step:(h + 1) * 2 * step]
            ab[layer, q, 2 * (3 - j) + h, 1] = lo[:, h * 2 * step:(h + 1) * 2 * step]

    @pl.when(onward & even)
    def _():
        for q in arrive[:-1]:
            cross(q).wait_send()
        pl.semaphore_signal(go, inc=1, device_id=dev(partner, F), device_id_type=pl.DeviceIdType.MESH)

    @pl.when(onward & isodd)
    def _():
        pl.semaphore_wait(go, 1)
        for q in arrive:
            cross(q).start()

    if far:
        @pl.when(recv3)
        def _():
            for i, e, _ok, ok in thirds_list:
                if ok is None:
                    third(i, e).wait_recv()
                else:
                    @pl.when(ok)
                    def _(i=i, e=e):
                        third(i, e).wait_recv()

            def old(q, carry):
                ingest(0, 3, q)
                return carry

            lax.fori_loop(0, wide, old, 0)

    late_even, late_odd = late & even, late & isodd

    def halos_in(j, ss, rr):
        @pl.when(down)
        def _():
            halo_up(j, ss, rr).wait_recv()

        @pl.when(up)
        def _():
            halo_down(j, ss, rr).wait_recv()

    def crossed(q):
        cross(q).wait_recv()

        @pl.when(even)
        def _():
            part3(q).start()

        @pl.when(isodd)
        def _():
            part(2, q).start()

        if q == 1:
            @pl.when(down)
            def _():
                halo_down(2, h2s, h2r).start()

        if q == own:
            @pl.when(up)
            def _():
                halo_up(2, h2s, h2r).start()

    def event(i):
        if i == 0:
            @pl.when(late_even)
            def _():
                for q in arrive:
                    crossed(q)

            @pl.when(isodd)
            def _():
                for q in arrive:
                    part(0, q).wait_recv()
        if i == 1:
            @pl.when(late_odd)
            def _():
                crossed(arrive[0])

            halos_in(0, h0s, h0r)

            @pl.when(even)
            def _():
                for q in edges:
                    part(0, q).start()

            @pl.when(isodd)
            def _():
                for q in edges:
                    part(0, q).wait_recv()

            @pl.when(late_even)
            def _():
                halos_in(2, h2s, h2r)
                for q in edges:
                    part3(q).start()
        if i in (2, 3):
            now = arrive[:-1] if i == 2 else arrive[-1:]

            @pl.when(late_even)
            def _():
                for q in now:
                    part(0, q).wait_recv()

            @pl.when(late_odd)
            def _():
                for q in now:
                    if q != arrive[0]:
                        crossed(q)
                for q in now:
                    part3(q).wait_recv()
        if i == 4:
            @pl.when(late_even)
            def _():
                for q in edges:
                    part(0, q).wait_recv()

            @pl.when(late_odd)
            def _():
                halos_in(2, h2s, h2r)
                for q in edges:
                    part(2, q).start()
                for q in edges:
                    part3(q).wait_recv()
        if i == 5:
            @pl.when(T >= 1)
            def _():
                for r in range(1, own):
                    share(0, r).wait_recv()
        if i == 6:
            @pl.when(T >= 1)
            def _():
                for r in (0, own):
                    share(0, r).wait_recv()

    rows = [
        (("A", 1), ("A", 2)), (("A", 3), ("A", 0)), (("A", own), ("B", 1)), (("B", 2), ("B", 3)), (("B", 0), ("B", own)),
        (("C", 1), ("C", 2)), (("C", 0), ("C", own - 1)),
    ]
    steps = len(rows)
    first_of_two = steps - 2
    ja = jnp.where(late_even, 2, 0)
    jb = jnp.where(even, 0, 2)
    start = [1, 0, 1, 3, 0, 1, 0]
    number = [own, 2, 2, own - 2, 2, own - 1, 2]
    stride = [1, own + 1, 1, 1, own + 1, 1, own]
    le = [(2,), (0, 2), (1,), (1,), (1,), (1,), (1,)]
    lo_ = [(1,), (0, 1), (2, 3), (2, 3), (2, 3), (1,), (1,)]
    ee = [(), (0,), (), (), (), (), ()]
    eo = [(1,), (0, 1), (), (), (), (1,), (1,)]

    def by_class(i, of):
        table = [pick(i, [of(entry) for entry in c]) for c in (le, lo_, ee, eo)]
        return jnp.where(late, jnp.where(even, table[0], table[1]), jnp.where(even, table[2], table[3]))

    def operand(layer, r, b, d):
        pieces = []
        for a in range(3):
            for k in range(3):
                both = []
                for part_ in range(2):
                    cols = []
                    for h in range(2):
                        c = 2 * b + h - k * d
                        if a == 0:
                            cols.append(ab[layer, r, c, part_])
                        elif a == 2:
                            cols.append(ab[layer, r + 1, c, part_])
                        else:
                            cols += [ab[layer, r, c, part_, :, step:], ab[layer, r + 1, c, part_, :, :step]]
                    both.append(jnp.concatenate(cols, axis=1))
                pieces += [both[0], both[1], both[0]]
        return jnp.concatenate(pieces, axis=0)

    def straddle(layer, j, r):
        cols = []
        for h in range(2):
            cols += [af[layer, j, r, :, (2 * h + 1) * step:(2 * h + 2) * step], af[layer, j, r + 1, :, 2 * h * step:(2 * h + 1) * step]]
        return jnp.concatenate(cols, axis=1)

    def compute(layer, d, units):
        right = jnp.concatenate([operand(layer, r, 3 - j, d) for r, j in units], axis=1)
        total = jnp.dot(taps[layer], right, preferred_element_type=F32)
        pre = total + jnp.concatenate([tall[layer]] * (total.shape[1] // out_ch), axis=1)
        g = jnp.tanh(pre[:ch]) * (0.5 * jnp.tanh(0.5 * pre[ch:]) + 0.5)
        hi, lo = split(g)
        base = jnp.concatenate([straddle(layer, j, r) for r, j in units], axis=1)
        return base + jnp.dot(mix[layer], jnp.concatenate([hi, lo, hi], axis=0), preferred_element_type=F32)

    def body(i, carry):
        for n in range(steps):
            @pl.when(i == n)
            def _(n=n):
                event(n)

        first, each, pace = pick(i, start), pick(i, number), pick(i, stride)
        j0 = by_class(i, lambda e: e[0] if e else 0)
        j1 = by_class(i, lambda e: e[1] if len(e) > 1 else 0)
        blocks = by_class(i, len)
        layer = (i >= first_of_two).astype(jnp.int32)

        def take(n, carry):
            second = n >= each
            q = first + pace * jnp.where(second, n - each, n)
            ingest(layer, jnp.where(second, j1, j0), q)
            return carry

        lax.fori_loop(0, each * blocks, take, 0)

        units = []
        for lane in range(2):
            r = pick(i, [pair[lane][1] for pair in rows])
            kind = pick(i, ["ABC".index(pair[lane][0]) for pair in rows])
            if any(pair[lane][0] == "B" and pair[0][0] == "A" for pair in rows):
                r = jnp.where((kind == 1) & jnp.logical_not(late), own, r)
            j = jnp.where(kind == 0, ja, jnp.where(kind == 1, jnp.where(late, jb, 0), 0))
            units.append((r, j, kind))

        @pl.when(late | (i < 3) | (i >= first_of_two))
        def _():
            value = compute(layer, layer + 1, [(r, j) for r, j, _ in units])

            @pl.when(layer == 0)
            def _():
                for n, (r, j, kind) in enumerate(units):
                    v = value[:, n * 2 * length:(n + 1) * 2 * length]
                    row = F * fib + 2 * r - 1
                    ok = [(row >= 0) & (row < nf * fib), (row + 1 >= 0) & (row + 1 < nf * fib)]
                    v = jnp.concatenate([jnp.where(ok[p % 2], v[:, p * step:(p + 1) * step], 0.0) for p in range(4)], axis=1)
                    af[1, j, r] = v
                    hi, lo = split(v)
                    for h in range(2):
                        ab[1, r, 2 * (3 - j) + h, 0] = hi[:, h * 2 * step:(h + 1) * 2 * step]
                        ab[1, r, 2 * (3 - j) + h, 1] = lo[:, h * 2 * step:(h + 1) * 2 * step]

                for r, j, kind in units:
                    @pl.when((late & (kind == 1)) | ((T == 0) & (kind == 0)))
                    def _(r=r, j=j):
                        share(j, r).start()

            @pl.when(layer == 1)
            def _():
                for n, (r, j, kind) in enumerate(units):
                    for p in range(4):
                        h, e = p // 2, p % 2
                        at = n * 2 * length + p * step
                        out_ref[pl.ds(h * fib + 2 * r + e, ch, stride=fib * 2), :] = value[:, at:at + step]
        return carry

    lax.fori_loop(0, steps, body, 0)

    @pl.when(onward & even)
    def _():
        cross(arrive[-1]).wait_send()

    @pl.when(onward & isodd)
    def _():
        for q in arrive:
            cross(q).wait_send()

    for j, ss, rr, ok in ((0, h0s, h0r, None), (2, h2s, h2r, late)):
        @pl.when(up if ok is None else up & ok)
        def _(j=j, ss=ss, rr=rr):
            halo_up(j, ss, rr).wait_send()

        @pl.when(down if ok is None else down & ok)
        def _(j=j, ss=ss, rr=rr):
            halo_down(j, ss, rr).wait_send()

    for q in range(wide):
        @pl.when(even | late)
        def _(q=q):
            part(0, q).wait_send()

        @pl.when(late_even)
        def _(q=q):
            part3(q).wait_send()

    @pl.when(even | late)
    def _():
        for r in range(mid):
            share(0, r).wait_send()

    if far:
        for i, e, ok, _ok in thirds_list:
            @pl.when(send3 if ok is None else send3 & ok)
            def _(i=i, e=e):
                third(i, e).wait_send()


def spread_kernel(
    nt, nf, fib,
    x_hbm, w1_hbm, b1_hbm, r1_hbm, w2_hbm, b2_hbm, r2_hbm, out_ref,
    xv, w1, b1, r1, w2, b2, r2, taps, mix, tall, pk, af, sf, ab, mf, mb, fs, fr, held,
    in_sem, w_sem, xs, xr, hs, hr, gs, gr, us, ur, vs, vr,
):
    T = lax.axis_index("tm")
    F = lax.axis_index("fibre")
    odd = lax.rem(T, 2)
    partner = T + 1 - 2 * odd
    peers = [partner, lax.rem(T + 2, nt), lax.rem(partner + 2, nt)]
    chip = T - odd
    other = lax.rem(chip + 2, nt)
    ch = pk.shape[2]
    own = fib // 2
    out_ch = 2 * ch
    step = DILATION_ONE
    group = step // nt
    up, down = F + 1 < nf, F > 0
    lane = lax.broadcasted_iota(jnp.int32, (ch, step), 1)
    early_half = lane < 2 * group
    first_fibre = lax.rem(lane, 2 * group) < group

    def dev(t, f):
        return {"tm": t, "fibre": f}

    barrier = pltpu.get_barrier_semaphore()
    for p in peers:
        pl.semaphore_signal(barrier, inc=1, device_id=dev(p, F), device_id_type=pl.DeviceIdType.MESH)
    count = jnp.int32(len(peers))
    for e, ok in ((1, up), (-1, down)):
        @pl.when(ok)
        def _(e=e):
            pl.semaphore_signal(barrier, inc=1, device_id=dev(T, F + e), device_id_type=pl.DeviceIdType.MESH)
        count = count + ok.astype(jnp.int32)

    load = pltpu.make_async_copy(x_hbm, xv, in_sem.at[0])
    load.start()
    weights = [
        pltpu.make_async_copy(a, b, w_sem.at[i])
        for i, (a, b) in enumerate(
            [(w1_hbm, w1), (b1_hbm, b1), (r1_hbm, r1), (w2_hbm, w2), (b2_hbm, b2), (r2_hbm, r2)]
        )
    ]
    for c in weights:
        c.start()

    def swap(parts):
        a, b, c, d = parts
        half = 2 * group
        a, c = jnp.where(early_half, a, pltpu.roll(c, half, 1)), jnp.where(early_half, pltpu.roll(a, half, 1), c)
        b, d = jnp.where(early_half, b, pltpu.roll(d, half, 1)), jnp.where(early_half, pltpu.roll(b, half, 1), d)
        back = step - group
        a, b = jnp.where(first_fibre, a, pltpu.roll(b, group, 1)), jnp.where(first_fibre, pltpu.roll(a, back, 1), b)
        c, d = jnp.where(first_fibre, c, pltpu.roll(d, group, 1)), jnp.where(first_fibre, pltpu.roll(c, back, 1), d)
        return a, b, c, d

    load.wait()

    def pack(q):
        parts = [xv[pl.ds(h * fib + 2 * q + e, ch, stride=fib * 2), :] for h in range(2) for e in range(2)]
        for t, value in enumerate(swap(parts)):
            pk[t, q] = value

            @pl.when(T == t)
            def _(value=value):
                af[q + 1, t] = value

    pack(0)
    pl.semaphore_wait(barrier, count)

    def remote(src, dst, ssem, rsem, t, f):
        return pltpu.make_async_remote_copy(
            src_ref=src, dst_ref=dst, send_sem=ssem, recv_sem=rsem,
            device_id=dev(t, f), device_id_type=pl.DeviceIdType.MESH,
        )

    def signal_out(k, q):
        n = k * own + q - 1
        return remote(pk.at[peers[k], q - 1], af.at[q, T], xs.at[n], xr.at[n], peers[k], F)

    def signal_in(k, q):
        n = k * own + q - 1
        return remote(pk.at[peers[k], q - 1], af.at[q, peers[k]], xs.at[n], xr.at[n], peers[k], F)

    def halo_up(n):
        blocks = pl.ds((chip, other)[n], 2)
        return remote(af.at[own, blocks], af.at[0, blocks], hs.at[2 * n], hr.at[2 * n], T, F + 1)

    def halo_down(n):
        blocks = pl.ds((chip, other)[n], 2)
        return remote(af.at[1, blocks], af.at[own + 1, blocks], hs.at[2 * n + 1], hr.at[2 * n + 1], T, F - 1)

    def edge_up(k):
        return remote(pk.at[peers[k], own - 1], held.at[k - 1], us.at[k - 1], ur.at[k - 1], T, F + 1)

    def relay_out(k):
        return remote(held.at[k - 1], af.at[0, T], vs.at[k - 1], vr.at[k - 1], peers[k], F)

    def relay_in(k):
        return remote(held.at[k - 1], af.at[0, peers[k]], vs.at[k - 1], vr.at[k - 1], peers[k], F)

    def feature_out(k, p):
        n = k * own + p
        return remote(fs.at[p, peers[k]], fr.at[p, T], gs.at[n], gr.at[n], peers[k], F)

    def feature_in(k, p):
        n = k * own + p
        return remote(fs.at[p, peers[k]], fr.at[p, peers[k]], gs.at[n], gr.at[n], peers[k], F)

    def begin(i, carry):
        q = i + 1

        @pl.when(i > 0)
        def _():
            pack(i)

        @pl.when(jnp.logical_not(down) | (i < own - 1))
        def _():
            toward(0, q)

        @pl.when(jnp.logical_not(down))
        def _():
            toward(1, q)
        signal_out(0, q).start()
        return carry

    def toward(core, q):
        for parity in range(2):
            @pl.when(odd == parity)
            def _(parity=parity):
                signal_out(1 if parity == core else 2, q).start()

    lax.fori_loop(0, own, begin, 0)

    @pl.when(down)
    def _():
        for q in range(1, own):
            toward(1, q)
        toward(0, own)
        toward(1, own)

    @pl.when(up)
    def _():
        for k in (1, 2):
            edge_up(k).start()

    no_rows = jnp.zeros((nt, ch, step), F32)

    @pl.when(jnp.logical_not(down))
    def _():
        af[0] = no_rows

    @pl.when(jnp.logical_not(up))
    def _():
        af[own + 1] = no_rows

    for q in range(own + 2):
        for kind in range(2):
            ab[kind, 0, q, :, :, :step] = jnp.zeros((2, ch, step), BF)
            if q <= own:
                mb[kind, q, :, :, :2 * step] = jnp.zeros((2, ch, 2 * step), BF)

    for q in (1, own):
        signal_in(0, q).wait_recv()

    @pl.when(up)
    def _():
        halo_up(0).start()

    @pl.when(down)
    def _():
        halo_down(0).start()

    for c in weights:
        c.wait()

    def prepare(layer, w, r, bias):
        for a in range(3):
            for k in range(3):
                hi, lo = split(w[a, k].T)
                for i, piece in enumerate((hi, hi, lo)):
                    taps[layer, :, pl.ds((9 * a + 3 * k + i) * ch, ch)] = piece
        hi, lo = split(r[...])
        for i, piece in enumerate((hi, hi, lo)):
            mix[layer, :, pl.ds(i * ch, ch)] = piece
        tall[layer] = jnp.broadcast_to(bias[...], (out_ch, out_ch)).T

    prepare(0, w1, r1, b1)
    prepare(1, w2, r2, b2)

    def keep(ref, kind, q, values, lead, shifted, later=None):
        for t, value in enumerate(values):
            at = pl.ds((t + lead) * step, step)
            hi, lo = split(value)
            if shifted:
                turned = pltpu.roll(value, 2 * group, 1)
                before = jnp.where(early_half, jnp.zeros_like(turned) if later is None else later, turned)
                later = turned
                ref[kind, 0, q, 0, :, at], ref[kind, 0, q, 1, :, at] = hi, lo
                hi, lo = split(before)
                ref[kind, 1, q, 0, :, at], ref[kind, 1, q, 1, :, at] = hi, lo
            else:
                ref[kind, q, 0, :, at], ref[kind, q, 1, :, at] = hi, lo

    def pair(q, first, n):
        later = pltpu.roll(af[q, first - 1], 2 * group, 1) if first else None
        keep(ab, 0, q, [af[q, t] for t in range(first, first + n)], first + 1, True, later)

    def between(left, right):
        return jnp.where(first_fibre, pltpu.roll(left, step - group, 1), pltpu.roll(right, group, 1))

    def across(r, first, n):
        values = [between(af[r, t], af[r + 1, t]) for t in range(first, first + n)]
        for t in range(n):
            sf[r, :, pl.ds((first + t) * step, step)] = values[t]
        later = pltpu.roll(between(af[r, first - 1], af[r + 1, first - 1]), 2 * group, 1) if first else None
        keep(ab, 1, r, values, first + 1, True, later)

    def first_operand(r, first, n):
        pieces = []
        for kind, q in ((0, r), (1, r), (0, r + 1)):
            for early, back in ((0, 0), (1, 0), (0, 1)):
                lanes = slice((first + 1 - back) * step, (first + 1 - back + n) * step)
                hi, lo = ab[kind, early, q, 0, :, lanes], ab[kind, early, q, 1, :, lanes]
                pieces += [hi, lo, hi]
        return jnp.concatenate(pieces, axis=0)

    def second_operand(p, first, n):
        pieces = []
        for kind, q in ((0, p), (1, p), (0, p + 1)):
            for k in range(3):
                lanes = pl.ds(pl.multiple_of((2 - k + first) * step, step), n * step)
                hi, lo = mb[kind, q, 0, :, lanes], mb[kind, q, 1, :, lanes]
                pieces += [hi, lo, hi]
        return jnp.concatenate(pieces, axis=0)

    def layer_of(layer, right, base):
        total = jnp.dot(taps[layer], right, preferred_element_type=F32)
        pre = total + jnp.concatenate([tall[layer]] * (total.shape[1] // out_ch), axis=1)
        g = jnp.tanh(pre[:ch]) * (0.5 * jnp.tanh(0.5 * pre[ch:]) + 0.5)
        hi, lo = split(g)
        return base + jnp.dot(mix[layer], jnp.concatenate([hi, lo, hi], axis=0), preferred_element_type=F32)

    def middle(rows, first, n):
        value = layer_of(
            0,
            jnp.concatenate([first_operand(r, first, n) for r in rows], axis=1),
            jnp.concatenate([sf[r, :, first * step:(first + n) * step] for r in rows], axis=1),
        )
        for i, r in enumerate(rows):
            row = F * fib + 2 * r - 1
            ok = [((f >= 0) & (f < nf * fib)).astype(jnp.int32) for f in (row, row + 1)]
            inside = jnp.where(first_fibre, ok[0], ok[1]) == 1
            parts = [jnp.where(inside, value[:, t * step:(t + 1) * step], 0.0) for t in range(i * n, (i + 1) * n)]
            for t in range(n):
                mf[r, first + t] = parts[t]
            keep(mb, 0, r, parts, first + 2, False)

    def join(p, first, n):
        values = [between(mf[p, t], mf[p + 1, t]) for t in range(first, first + n)]
        keep(mb, 1, p, values, first + 2, False)
        for t in range(n):
            sf[p, :, pl.ds((first + t) * step, step)] = values[t]

    def blocks_of(p, first, n):
        return sf[p, :, pl.ds(pl.multiple_of(first * step, step), n * step)]

    def away(p, first):
        value = layer_of(1, second_operand(p, first, 2), blocks_of(p, first, 2))
        for t in range(2):
            fs[p, first + t] = value[:, t * step:(t + 1) * step]

    def home(ps):
        def half(n, carry):
            t = jnp.where(n == 0, partner, T)
            value = layer_of(
                1,
                jnp.concatenate([second_operand(p, t, 1) for p in ps], axis=1),
                jnp.concatenate([blocks_of(p, t, 1) for p in ps], axis=1),
            )
            parts = [value[:, i * step:(i + 1) * step] for i in range(len(ps))]

            @pl.when(n == 0)
            def _():
                for part, p in zip(parts, ps):
                    fs[p, partner] = part
                    feature_out(0, p).start()

            @pl.when(n == 1)
            def _():
                for part, p in zip(parts, ps):
                    fr[p, T] = part
            return carry

        lax.fori_loop(0, 2, half, 0)

    pairs = list(range(1, own + 2)) + [0]
    rows = [0] + list(range(1, own + 1)) + [0]
    outs = [0, 0] + list(range(1, own)) + [0]
    pairs_first = [1, 0] + list(range(2, own + 2))
    rows_first = [0, 0] + list(range(1, own + 1))
    outs_first = [0, 0] + list(range(own))

    def body(i, carry):
        q, r, p = (
            jnp.where(down, pick(i, usual), pick(i, first))
            for usual, first in ((pairs, pairs_first), (rows, rows_first), (outs, outs_first))
        )

        @pl.when((q >= 1) & (q <= own))
        def _():
            for k in (1, 2):
                signal_in(k, q).wait_recv()

        @pl.when((q == 1) & down)
        def _():
            halo_down(1).start()

        @pl.when((q == 2) & down)
        def _():
            for k in (1, 2):
                edge_up(k).wait_recv()
                relay_out(k).start()

        @pl.when((q == own + 1) & up)
        def _():
            for n in range(2):
                halo_down(n).wait_recv()

        @pl.when((q == 0) & down)
        def _():
            halo_up(0).wait_recv()
            for k in (1, 2):
                relay_in(k).wait_recv()

        inner_pair = (q >= 1) & (q <= own) & (chip == 0)
        inner_row = (r >= 1) & (r <= own - 1) & (chip == 0)

        @pl.when(inner_pair)
        def _():
            pair(q, 2, 2)

        @pl.when(jnp.logical_not(inner_pair))
        def _():
            pair(q, 0, nt)

        @pl.when((i >= 1) & inner_row)
        def _():
            across(r, 2, 2)
            middle([r], 2, 2)

        for where, blocks in ((jnp.logical_not(inner_row) & (chip == 0), nt), (chip == 2, 2)):
            @pl.when((i >= 1) & where)
            def _(blocks=blocks):
                across(r, 0, nt)
                middle([r], 0, blocks)

        for where, blocks, theirs in ((0, nt, 2), (2, 2, 0)):
            @pl.when((i >= 2) & (chip == where))
            def _(blocks=blocks, theirs=theirs):
                join(p, 0, blocks)
                away(p, theirs)

        @pl.when((i >= 2) & outer)
        def _():
            for k in (2, 1):
                feature_out(k, p).start()

        @pl.when((i >= 2) & jnp.logical_not(outer))
        def _():
            for k in (1, 2):
                feature_out(k, p).start()
        return carry

    outer = (T == 0) | (T == nt - 1)
    for q in range(2, own):
        signal_in(0, q).wait_recv()

    @pl.when(chip == 0)
    def _():
        def pairs_of_chip(n, carry):
            pair(n + 1, 0, 2)
            return carry

        def rows_of_chip(n, carry):
            across(n + 1, 0, 2)
            return carry

        lax.fori_loop(0, own, pairs_of_chip, 0)
        lax.fori_loop(0, own - 1, rows_of_chip, 0)
        middle(list(range(1, own)), 0, 2)

    lax.fori_loop(0, own + 2, body, 0)

    @pl.when(chip == 2)
    def _():
        middle(list(range(own + 1)), 2, 2)
        for p in range(own):
            join(p, 2, 2)

    home(list(range(own)))

    def finish(i, carry):
        p = jnp.where(down, lax.rem(i + 1, own), i)
        for k in range(3):
            feature_in(k, p).wait_recv()
        for n, value in enumerate(swap([fr[p, t] for t in range(nt)])):
            out_ref[pl.ds(n // 2 * fib + 2 * p + n % 2, ch, stride=fib * 2), :] = value
        return carry

    lax.fori_loop(0, own, finish, 0)

    for k in range(3):
        for q in range(1, own + 1):
            signal_out(k, q).wait_send()
            feature_out(k, q - 1).wait_send()
    @pl.when(up)
    def _():
        halo_up(0).wait_send()
        for k in (1, 2):
            edge_up(k).wait_send()

    @pl.when(down)
    def _():
        for n in range(2):
            halo_down(n).wait_send()
        for k in (1, 2):
            relay_out(k).wait_send()


def solution(mesh):
    nt, nf = mesh.shape["tm"], mesh.shape["fibre"]
    placed = (P(None, "fibre", "tm"), P(), P(), P(), P(), P(), P())

    def body(signal, w1, b1, r1, w2, b2, r2):
        ch, fib, length = signal.shape
        assert length == DILATION_TWO == 2 * DILATION_ONE and nt % 2 == 0 and fib == FIB_DEV
        x = signal.reshape(ch, fib, length // 128, 128).transpose(0, 2, 1, 3).reshape(-1, 128)
        out_ch = w1.shape[2]
        own = fib // 2
        w1, w2 = jnp.transpose(w1, (0, 1, 3, 2)), jnp.transpose(w2, (0, 1, 3, 2))
        b1 = b1.reshape(1, out_ch)
        b2 = b2.reshape(1, out_ch)
        dma = lambda n: pltpu.SemaphoreType.DMA((n,))
        inputs = [
            pltpu.VMEM(x.shape, F32),
            pltpu.VMEM(w1.shape, F32), pltpu.VMEM(b1.shape, F32), pltpu.VMEM(r1.shape, F32),
            pltpu.VMEM(w2.shape, F32), pltpu.VMEM(b2.shape, F32), pltpu.VMEM(r2.shape, F32),
            pltpu.VMEM((2, out_ch, 27 * ch), BF), pltpu.VMEM((2, ch, 3 * ch), BF),
            pltpu.VMEM((2, out_ch, out_ch), F32),
        ]
        step = DILATION_ONE
        if nt == 4:
            form = spread_kernel
            scratch = inputs + [
                pltpu.VMEM((nt, own, ch, step), F32), pltpu.VMEM((own + 2, nt, ch, step), F32),
                pltpu.VMEM((own + 1, ch, nt * step), F32),
                pltpu.VMEM((2, 2, own + 2, 2, ch, (nt + 1) * step), BF),
                pltpu.VMEM((own + 1, nt, ch, step), F32),
                pltpu.VMEM((2, own + 1, 2, ch, (nt + 2) * step), BF),
                pltpu.VMEM((own, nt, ch, step), F32), pltpu.VMEM((own, nt, ch, step), F32),
                pltpu.VMEM((2, ch, step), F32),
                dma(1), dma(6), dma(3 * own), dma(3 * own), dma(4), dma(4), dma(3 * own), dma(3 * own),
                dma(2), dma(2), dma(2), dma(2),
            ]
        else:
            form = kernel
            scratch = [
                pltpu.VMEM((2, 4, own + 2, ch, 2 * length), F32),
                pltpu.VMEM((2, own + 2, 4 * length // step, 2, ch, 2 * step), BF),
            ] + inputs + [
                dma(1), dma(6), dma(2), dma(2), dma(2), dma(2), dma(own + 2), dma(own + 2),
                dma(own + 2), dma(own + 2), dma(own + 2), dma(own + 2),
                dma(own + 1), dma(own + 1), dma(3), dma(3),
                pltpu.SemaphoreType.REGULAR,
            ]
        out = pl.pallas_call(
            lambda *refs: form(nt, nf, fib, *refs),
            name="gated_layers",
            out_shape=pltpu.VMEM(x.shape, F32),
            in_specs=[pl.BlockSpec(memory_space=pl.ANY)] * 7,
            out_specs=pl.BlockSpec(memory_space=pltpu.VMEM),
            scratch_shapes=scratch,
            compiler_params=pltpu.CompilerParams(
                collective_id=0, has_side_effects=True, vmem_limit_bytes=60 * 1024 * 1024
            ),
        )(x, w1, b1, r1, w2, b2, r2)
        out = out.reshape(ch, length // 128, fib, 128).transpose(0, 2, 1, 3)
        return out.reshape(ch, fib, length)

    return jax.shard_map(body, mesh=mesh, in_specs=placed, out_specs=P(None, "fibre", "tm"), check_vma=False)
```

```python
import jax
import jax.numpy as jnp
from jax import lax
from jax.experimental import pallas as pl
from jax.experimental.pallas import tpu as pltpu
from jax.sharding import PartitionSpec as P

DILATION_ONE = 128
DILATION_TWO = 256
FIB_DEV = 8
BF = jnp.bfloat16
F32 = jnp.float32


def split(value):
    hi = value.astype(BF)
    return hi, (value - hi.astype(F32)).astype(BF)


def pick(i, values):
    out = jnp.int32(values[-1])
    for n in range(len(values) - 2, -1, -1):
        out = jnp.where(i == n, jnp.int32(values[n]), out)
    return out


def kernel(
    nt, nf, fib,
    x_hbm, w1_hbm, b1_hbm, r1_hbm, w2_hbm, b2_hbm, r2_hbm, out_ref,
    af, ab, xv, w1, b1, r1, w2, b2, r2, taps, mix, tall,
    in_sem, w_sem, h0s, h0r, h2s, h2r, xs, xr, ps, pr, ts, tr, ms, mr, es, er, go,
):
    s, m = af.at[0], af.at[1]
    T = lax.axis_index("tm")
    F = lax.axis_index("fibre")
    odd = lax.rem(T, 2)
    even = odd == 0
    isodd = odd == 1
    late = T >= 2
    partner = T + 1 - 2 * odd
    ch, length = af.shape[3], af.shape[4] // 2
    own = fib // 2
    wide = own + 2
    mid = own + 1
    out_ch = 2 * ch
    step = DILATION_ONE
    far = nt > 4
    up, down = F + 1 < nf, F > 0
    onward = T + 2 < nt
    inner = list(range(1, own + 1))
    arrive = [1, own] + list(range(2, own))
    edges = [0, own + 1]

    def dev(t, f):
        return {"tm": t, "fibre": f}

    load = pltpu.make_async_copy(x_hbm, xv, in_sem.at[0])
    load.start()
    weights = [
        pltpu.make_async_copy(a, b, w_sem.at[i])
        for i, (a, b) in enumerate(
            [(w1_hbm, w1), (b1_hbm, b1), (r1_hbm, r1), (w2_hbm, w2), (b2_hbm, b2), (r2_hbm, r2)]
        )
    ]
    for c in weights:
        c.start()

    barrier = pltpu.get_barrier_semaphore()
    friends = [(partner, F, None), (T, F + 1, up), (T, F - 1, down), (T + 2, F, onward), (T - 2, F, late)]
    if far:
        send3 = isodd & (T + 3 < nt)
        recv3 = even & (T >= 4)
        for e, ok in ((0, None), (1, up), (-1, down)):
            for d, okt in ((3, send3), (-3, recv3)):
                friends.append((T + d, F + e, okt if ok is None else okt & ok))
    count = jnp.int32(0)
    for t, f, ok in friends:
        if ok is None:
            pl.semaphore_signal(barrier, inc=1, device_id=dev(t, f), device_id_type=pl.DeviceIdType.MESH)
            count = count + 1
        else:
            @pl.when(ok)
            def _(t=t, f=f):
                pl.semaphore_signal(barrier, inc=1, device_id=dev(t, f), device_id_type=pl.DeviceIdType.MESH)
            count = count + ok.astype(jnp.int32)

    load.wait()
    for f in range(fib):
        for h in range(2):
            value = xv[pl.ds(h * fib + f, ch, stride=fib * 2), :]
            lanes = pl.ds((f % 2) * step, step)
            af[0, 0, 1 + f // 2, :, pl.ds((2 * h + f % 2) * step, step)] = value
            hi, lo = split(value)
            ab[0, 1 + f // 2, 6 + h, 0, :, lanes] = hi
            ab[0, 1 + f // 2, 6 + h, 1, :, lanes] = lo
    pl.semaphore_wait(barrier, count)

    def remote(src, dst, ssem, rsem, t, f):
        return pltpu.make_async_remote_copy(
            src_ref=src, dst_ref=dst, send_sem=ssem, recv_sem=rsem,
            device_id=dev(t, f), device_id_type=pl.DeviceIdType.MESH,
        )

    def halo_up(j, ss, rr):
        return remote(s.at[j, own], s.at[j, 0], ss.at[0], rr.at[0], T, F + 1)

    def halo_down(j, ss, rr):
        return remote(s.at[j, 1], s.at[j, own + 1], ss.at[1], rr.at[1], T, F - 1)

    def cross(q):
        return remote(s.at[0, q], s.at[2, q], xs.at[q], xr.at[q], T + 2, F)

    def part(src, q):
        return remote(s.at[src, q], s.at[1, q], ps.at[q], pr.at[q], partner, F)

    def part3(q):
        return remote(s.at[2, q], s.at[3, q], ts.at[q], tr.at[q], partner, F)

    def share(src, r):
        return remote(m.at[src, r], m.at[1, r], ms.at[r], mr.at[r], partner, F)

    @pl.when(onward & even)
    def _():
        for q in arrive:
            cross(q).start()

    @pl.when(up)
    def _():
        halo_up(0, h0s, h0r).start()

    @pl.when(down)
    def _():
        halo_down(0, h0s, h0r).start()

    @pl.when(even)
    def _():
        for q in arrive:
            part(0, q).start()

    if far:
        def third(i, e):
            if e == 0:
                src, dst = s.at[0, pl.ds(1, own)], s.at[3, pl.ds(1, own)]
            elif e == 1:
                src, dst = s.at[0, own], s.at[3, 0]
            else:
                src, dst = s.at[0, 1], s.at[3, own + 1]
            return remote(src, dst, es.at[i], er.at[i], T + 3, F + e)

        thirds_list = [(0, 0, None, None), (1, 1, up, down), (2, -1, down, up)]
        for i, e, ok, _ok in thirds_list:
            @pl.when(send3 if ok is None else send3 & ok)
            def _(i=i, e=e):
                third(i, e).start()

    zero = jnp.zeros(af.shape[3:], F32)

    def zero_halo(j):
        @pl.when(jnp.logical_not(down))
        def _():
            af[0, j, 0] = zero

        @pl.when(jnp.logical_not(up))
        def _():
            af[0, j, own + 1] = zero

    zero_halo(0)

    def no_chunks(layer, first, n):
        for q in range(wide if layer == 0 else mid):
            ab[layer, q, pl.ds(first, n)] = jnp.zeros((n,) + ab.shape[3:], BF)

    @pl.when(T == 0)
    def _():
        no_chunks(0, 4, 2)
        no_chunks(1, 4, 2)

    @pl.when(T < 2)
    def _():
        no_chunks(1, 2, 2)

    @pl.when(T == 2)
    def _():
        no_chunks(0, 0, 2)

    @pl.when(late)
    def _():
        zero_halo(2)

    if far:
        @pl.when(recv3)
        def _():
            zero_halo(3)

    for c in weights:
        c.wait()

    def prepare(layer, w, r, bias):
        for a in range(3):
            for k in range(3):
                hi, lo = split(w[a, k].T)
                for i, piece in enumerate((hi, hi, lo)):
                    taps[layer, :, pl.ds((9 * a + 3 * k + i) * ch, ch)] = piece
        hi, lo = split(r[...])
        for i, piece in enumerate((hi, hi, lo)):
            mix[layer, :, pl.ds(i * ch, ch)] = piece
        tall[layer] = jnp.broadcast_to(bias[...], (out_ch, out_ch)).T

    prepare(0, w1, r1, b1)
    prepare(1, w2, r2, b2)

    def ingest(layer, j, q):
        hi, lo = split(af[layer, j, q])
        for h in range(2):
            ab[layer, q, 2 * (3 - j) + h, 0] = hi[:, h * 2 * step:(h + 1) * 2 * step]
            ab[layer, q, 2 * (3 - j) + h, 1] = lo[:, h * 2 * step:(h + 1) * 2 * step]

    @pl.when(onward & even)
    def _():
        for q in arrive[:-1]:
            cross(q).wait_send()
        pl.semaphore_signal(go, inc=1, device_id=dev(partner, F), device_id_type=pl.DeviceIdType.MESH)

    @pl.when(onward & isodd)
    def _():
        pl.semaphore_wait(go, 1)
        for q in arrive:
            cross(q).start()

    if far:
        @pl.when(recv3)
        def _():
            for i, e, _ok, ok in thirds_list:
                if ok is None:
                    third(i, e).wait_recv()
                else:
                    @pl.when(ok)
                    def _(i=i, e=e):
                        third(i, e).wait_recv()

            def old(q, carry):
                ingest(0, 3, q)
                return carry

            lax.fori_loop(0, wide, old, 0)

    late_even, late_odd = late & even, late & isodd

    def halos_in(j, ss, rr):
        @pl.when(down)
        def _():
            halo_up(j, ss, rr).wait_recv()

        @pl.when(up)
        def _():
            halo_down(j, ss, rr).wait_recv()

    def crossed(q):
        cross(q).wait_recv()

        @pl.when(even)
        def _():
            part3(q).start()

        @pl.when(isodd)
        def _():
            part(2, q).start()

        if q == 1:
            @pl.when(down)
            def _():
                halo_down(2, h2s, h2r).start()

        if q == own:
            @pl.when(up)
            def _():
                halo_up(2, h2s, h2r).start()

    def event(i):
        if i == 0:
            @pl.when(late_even)
            def _():
                for q in arrive:
                    crossed(q)

            @pl.when(isodd)
            def _():
                for q in arrive:
                    part(0, q).wait_recv()
        if i == 1:
            @pl.when(late_odd)
            def _():
                crossed(arrive[0])

            halos_in(0, h0s, h0r)

            @pl.when(even)
            def _():
                for q in edges:
                    part(0, q).start()

            @pl.when(isodd)
            def _():
                for q in edges:
                    part(0, q).wait_recv()

            @pl.when(late_even)
            def _():
                halos_in(2, h2s, h2r)
                for q in edges:
                    part3(q).start()
        if i in (2, 3):
            now = arrive[:-1] if i == 2 else arrive[-1:]

            @pl.when(late_even)
            def _():
                for q in now:
                    part(0, q).wait_recv()

            @pl.when(late_odd)
            def _():
                for q in now:
                    if q != arrive[0]:
                        crossed(q)
                for q in now:
                    part3(q).wait_recv()
        if i == 4:
            @pl.when(late_even)
            def _():
                for q in edges:
                    part(0, q).wait_recv()

            @pl.when(late_odd)
            def _():
                halos_in(2, h2s, h2r)
                for q in edges:
                    part(2, q).start()
                for q in edges:
                    part3(q).wait_recv()
        if i == 5:
            @pl.when(T >= 1)
            def _():
                for r in range(1, own):
                    share(0, r).wait_recv()
        if i == 6:
            @pl.when(T >= 1)
            def _():
                for r in (0, own):
                    share(0, r).wait_recv()

    rows = [
        (("A", 1), ("A", 2)), (("A", 3), ("A", 0)), (("A", own), ("B", 1)), (("B", 2), ("B", 3)), (("B", 0), ("B", own)),
        (("C", 1), ("C", 2)), (("C", 0), ("C", own - 1)),
    ]
    steps = len(rows)
    first_of_two = steps - 2
    ja = jnp.where(late_even, 2, 0)
    jb = jnp.where(even, 0, 2)
    start = [1, 0, 1, 3, 0, 1, 0]
    number = [own, 2, 2, own - 2, 2, own - 1, 2]
    stride = [1, own + 1, 1, 1, own + 1, 1, own]
    le = [(2,), (0, 2), (1,), (1,), (1,), (1,), (1,)]
    lo_ = [(1,), (0, 1), (2, 3), (2, 3), (2, 3), (1,), (1,)]
    ee = [(), (0,), (), (), (), (), ()]
    eo = [(1,), (0, 1), (), (), (), (1,), (1,)]

    def by_class(i, of):
        table = [pick(i, [of(entry) for entry in c]) for c in (le, lo_, ee, eo)]
        return jnp.where(late, jnp.where(even, table[0], table[1]), jnp.where(even, table[2], table[3]))

    def operand(layer, r, b, d):
        pieces = []
        for a in range(3):
            for k in range(3):
                both = []
                for part_ in range(2):
                    cols = []
                    for h in range(2):
                        c = 2 * b + h - k * d
                        if a == 0:
                            cols.append(ab[layer, r, c, part_])
                        elif a == 2:
                            cols.append(ab[layer, r + 1, c, part_])
                        else:
                            cols += [ab[layer, r, c, part_, :, step:], ab[layer, r + 1, c, part_, :, :step]]
                    both.append(jnp.concatenate(cols, axis=1))
                pieces += [both[0], both[1], both[0]]
        return jnp.concatenate(pieces, axis=0)

    def straddle(layer, j, r):
        cols = []
        for h in range(2):
            cols += [af[layer, j, r, :, (2 * h + 1) * step:(2 * h + 2) * step], af[layer, j, r + 1, :, 2 * h * step:(2 * h + 1) * step]]
        return jnp.concatenate(cols, axis=1)

    def compute(layer, d, units):
        right = jnp.concatenate([operand(layer, r, 3 - j, d) for r, j in units], axis=1)
        total = jnp.dot(taps[layer], right, preferred_element_type=F32)
        pre = total + jnp.concatenate([tall[layer]] * (total.shape[1] // out_ch), axis=1)
        g = jnp.tanh(pre[:ch]) * (0.5 * jnp.tanh(0.5 * pre[ch:]) + 0.5)
        hi, lo = split(g)
        base = jnp.concatenate([straddle(layer, j, r) for r, j in units], axis=1)
        return base + jnp.dot(mix[layer], jnp.concatenate([hi, lo, hi], axis=0), preferred_element_type=F32)

    def body(i, carry):
        for n in range(steps):
            @pl.when(i == n)
            def _(n=n):
                event(n)

        first, each, pace = pick(i, start), pick(i, number), pick(i, stride)
        j0 = by_class(i, lambda e: e[0] if e else 0)
        j1 = by_class(i, lambda e: e[1] if len(e) > 1 else 0)
        blocks = by_class(i, len)
        layer = (i >= first_of_two).astype(jnp.int32)

        def take(n, carry):
            second = n >= each
            q = first + pace * jnp.where(second, n - each, n)
            ingest(layer, jnp.where(second, j1, j0), q)
            return carry

        lax.fori_loop(0, each * blocks, take, 0)

        units = []
        for lane in range(2):
            r = pick(i, [pair[lane][1] for pair in rows])
            kind = pick(i, ["ABC".index(pair[lane][0]) for pair in rows])
            if any(pair[lane][0] == "B" and pair[0][0] == "A" for pair in rows):
                r = jnp.where((kind == 1) & jnp.logical_not(late), own, r)
            j = jnp.where(kind == 0, ja, jnp.where(kind == 1, jnp.where(late, jb, 0), 0))
            units.append((r, j, kind))

        @pl.when(late | (i < 3) | (i >= first_of_two))
        def _():
            value = compute(layer, layer + 1, [(r, j) for r, j, _ in units])

            @pl.when(layer == 0)
            def _():
                for n, (r, j, kind) in enumerate(units):
                    v = value[:, n * 2 * length:(n + 1) * 2 * length]
                    row = F * fib + 2 * r - 1
                    ok = [(row >= 0) & (row < nf * fib), (row + 1 >= 0) & (row + 1 < nf * fib)]
                    v = jnp.concatenate([jnp.where(ok[p % 2], v[:, p * step:(p + 1) * step], 0.0) for p in range(4)], axis=1)
                    af[1, j, r] = v
                    hi, lo = split(v)
                    for h in range(2):
                        ab[1, r, 2 * (3 - j) + h, 0] = hi[:, h * 2 * step:(h + 1) * 2 * step]
                        ab[1, r, 2 * (3 - j) + h, 1] = lo[:, h * 2 * step:(h + 1) * 2 * step]

                for r, j, kind in units:
                    @pl.when((late & (kind == 1)) | ((T == 0) & (kind == 0)))
                    def _(r=r, j=j):
                        share(j, r).start()

            @pl.when(layer == 1)
            def _():
                for n, (r, j, kind) in enumerate(units):
                    for p in range(4):
                        h, e = p // 2, p % 2
                        at = n * 2 * length + p * step
                        out_ref[pl.ds(h * fib + 2 * r + e, ch, stride=fib * 2), :] = value[:, at:at + step]
        return carry

    lax.fori_loop(0, steps, body, 0)

    @pl.when(onward & even)
    def _():
        cross(arrive[-1]).wait_send()

    @pl.when(onward & isodd)
    def _():
        for q in arrive:
            cross(q).wait_send()

    for j, ss, rr, ok in ((0, h0s, h0r, None), (2, h2s, h2r, late)):
        @pl.when(up if ok is None else up & ok)
        def _(j=j, ss=ss, rr=rr):
            halo_up(j, ss, rr).wait_send()

        @pl.when(down if ok is None else down & ok)
        def _(j=j, ss=ss, rr=rr):
            halo_down(j, ss, rr).wait_send()

    for q in range(wide):
        @pl.when(even | late)
        def _(q=q):
            part(0, q).wait_send()

        @pl.when(late_even)
        def _(q=q):
            part3(q).wait_send()

    @pl.when(even | late)
    def _():
        for r in range(mid):
            share(0, r).wait_send()

    if far:
        for i, e, ok, _ok in thirds_list:
            @pl.when(send3 if ok is None else send3 & ok)
            def _(i=i, e=e):
                third(i, e).wait_send()


def spread_kernel(
    nt, nf, fib,
    x_hbm, w1_hbm, b1_hbm, r1_hbm, w2_hbm, b2_hbm, r2_hbm, out_ref,
    xv, w1, b1, r1, w2, b2, r2, taps, mix, tall, pk, af, sf, ab, mf, mb, fs, fr, held,
    in_sem, w_sem, xs, xr, hs, hr, gs, gr, us, ur, vs, vr,
):
    T = lax.axis_index("tm")
    F = lax.axis_index("fibre")
    odd = lax.rem(T, 2)
    partner = T + 1 - 2 * odd
    peers = [partner, lax.rem(T + 2, nt), lax.rem(partner + 2, nt)]
    chip = T - odd
    other = lax.rem(chip + 2, nt)
    ch = pk.shape[2]
    own = fib // 2
    out_ch = 2 * ch
    step = DILATION_ONE
    group = step // nt
    up, down = F + 1 < nf, F > 0
    lane = lax.broadcasted_iota(jnp.int32, (ch, step), 1)
    early_half = lane < 2 * group
    first_fibre = lax.rem(lane, 2 * group) < group

    def dev(t, f):
        return {"tm": t, "fibre": f}

    barrier = pltpu.get_barrier_semaphore()
    for p in peers:
        pl.semaphore_signal(barrier, inc=1, device_id=dev(p, F), device_id_type=pl.DeviceIdType.MESH)
    count = jnp.int32(len(peers))
    for e, ok in ((1, up), (-1, down)):
        @pl.when(ok)
        def _(e=e):
            pl.semaphore_signal(barrier, inc=1, device_id=dev(T, F + e), device_id_type=pl.DeviceIdType.MESH)
        count = count + ok.astype(jnp.int32)

    load = pltpu.make_async_copy(x_hbm, xv, in_sem.at[0])
    load.start()
    weights = [
        pltpu.make_async_copy(a, b, w_sem.at[i])
        for i, (a, b) in enumerate(
            [(w1_hbm, w1), (b1_hbm, b1), (r1_hbm, r1), (w2_hbm, w2), (b2_hbm, b2), (r2_hbm, r2)]
        )
    ]
    for c in weights:
        c.start()

    def swap(parts):
        a, b, c, d = parts
        half = 2 * group
        a, c = jnp.where(early_half, a, pltpu.roll(c, half, 1)), jnp.where(early_half, pltpu.roll(a, half, 1), c)
        b, d = jnp.where(early_half, b, pltpu.roll(d, half, 1)), jnp.where(early_half, pltpu.roll(b, half, 1), d)
        back = step - group
        a, b = jnp.where(first_fibre, a, pltpu.roll(b, group, 1)), jnp.where(first_fibre, pltpu.roll(a, back, 1), b)
        c, d = jnp.where(first_fibre, c, pltpu.roll(d, group, 1)), jnp.where(first_fibre, pltpu.roll(c, back, 1), d)
        return a, b, c, d

    load.wait()

    def pack(q):
        parts = [xv[pl.ds(h * fib + 2 * q + e, ch, stride=fib * 2), :] for h in range(2) for e in range(2)]
        for t, value in enumerate(swap(parts)):
            pk[t, q] = value

            @pl.when(T == t)
            def _(value=value):
                af[q + 1, t] = value

    pack(0)
    pl.semaphore_wait(barrier, count)

    def remote(src, dst, ssem, rsem, t, f):
        return pltpu.make_async_remote_copy(
            src_ref=src, dst_ref=dst, send_sem=ssem, recv_sem=rsem,
            device_id=dev(t, f), device_id_type=pl.DeviceIdType.MESH,
        )

    def signal_out(k, q):
        n = k * own + q - 1
        return remote(pk.at[peers[k], q - 1], af.at[q, T], xs.at[n], xr.at[n], peers[k], F)

    def signal_in(k, q):
        n = k * own + q - 1
        return remote(pk.at[peers[k], q - 1], af.at[q, peers[k]], xs.at[n], xr.at[n], peers[k], F)

    def halo_up(n):
        blocks = pl.ds((chip, other)[n], 2)
        return remote(af.at[own, blocks], af.at[0, blocks], hs.at[2 * n], hr.at[2 * n], T, F + 1)

    def halo_down(n):
        blocks = pl.ds((chip, other)[n], 2)
        return remote(af.at[1, blocks], af.at[own + 1, blocks], hs.at[2 * n + 1], hr.at[2 * n + 1], T, F - 1)

    def edge_up(k):
        return remote(pk.at[peers[k], own - 1], held.at[k - 1], us.at[k - 1], ur.at[k - 1], T, F + 1)

    def relay_out(k):
        return remote(held.at[k - 1], af.at[0, T], vs.at[k - 1], vr.at[k - 1], peers[k], F)

    def relay_in(k):
        return remote(held.at[k - 1], af.at[0, peers[k]], vs.at[k - 1], vr.at[k - 1], peers[k], F)

    def feature_out(k, p):
        n = k * own + p
        return remote(fs.at[p, peers[k]], fr.at[p, T], gs.at[n], gr.at[n], peers[k], F)

    def feature_in(k, p):
        n = k * own + p
        return remote(fs.at[p, peers[k]], fr.at[p, peers[k]], gs.at[n], gr.at[n], peers[k], F)

    def begin(i, carry):
        q = i + 1

        @pl.when(i > 0)
        def _():
            pack(i)

        @pl.when(jnp.logical_not(down) | (i < own - 1))
        def _():
            toward(0, q)

        @pl.when(jnp.logical_not(down))
        def _():
            toward(1, q)
        signal_out(0, q).start()
        return carry

    def toward(core, q):
        for parity in range(2):
            @pl.when(odd == parity)
            def _(parity=parity):
                signal_out(1 if parity == core else 2, q).start()

    lax.fori_loop(0, own, begin, 0)

    @pl.when(down)
    def _():
        for q in range(1, own):
            toward(1, q)
        toward(0, own)
        toward(1, own)

    @pl.when(up)
    def _():
        for k in (1, 2):
            edge_up(k).start()

    no_rows = jnp.zeros((nt, ch, step), F32)

    @pl.when(jnp.logical_not(down))
    def _():
        af[0] = no_rows

    @pl.when(jnp.logical_not(up))
    def _():
        af[own + 1] = no_rows

    for q in range(own + 2):
        for kind in range(2):
            ab[kind, 0, q, :, :, :step] = jnp.zeros((2, ch, step), BF)
            if q <= own:
                mb[kind, q, :, :, :2 * step] = jnp.zeros((2, ch, 2 * step), BF)

    for q in (1, own):
        signal_in(0, q).wait_recv()

    @pl.when(up)
    def _():
        halo_up(0).start()

    @pl.when(down)
    def _():
        halo_down(0).start()

    for c in weights:
        c.wait()

    def prepare(layer, w, r, bias):
        for a in range(3):
            for k in range(3):
                hi, lo = split(w[a, k].T)
                for i, piece in enumerate((hi, hi, lo)):
                    taps[layer, :, pl.ds((9 * a + 3 * k + i) * ch, ch)] = piece
        hi, lo = split(r[...])
        for i, piece in enumerate((hi, hi, lo)):
            mix[layer, :, pl.ds(i * ch, ch)] = piece
        tall[layer] = jnp.broadcast_to(bias[...], (out_ch, out_ch)).T

    prepare(0, w1, r1, b1)
    prepare(1, w2, r2, b2)

    def keep(ref, kind, q, values, lead, shifted, later=None):
        for t, value in enumerate(values):
            at = pl.ds((t + lead) * step, step)
            hi, lo = split(value)
            if shifted:
                turned = pltpu.roll(value, 2 * group, 1)
                before = jnp.where(early_half, jnp.zeros_like(turned) if later is None else later, turned)
                later = turned
                ref[kind, 0, q, 0, :, at], ref[kind, 0, q, 1, :, at] = hi, lo
                hi, lo = split(before)
                ref[kind, 1, q, 0, :, at], ref[kind, 1, q, 1, :, at] = hi, lo
            else:
                ref[kind, q, 0, :, at], ref[kind, q, 1, :, at] = hi, lo

    def pair(q, first, n):
        later = pltpu.roll(af[q, first - 1], 2 * group, 1) if first else None
        keep(ab, 0, q, [af[q, t] for t in range(first, first + n)], first + 1, True, later)

    def between(left, right):
        return jnp.where(first_fibre, pltpu.roll(left, step - group, 1), pltpu.roll(right, group, 1))

    def across(r, first, n):
        values = [between(af[r, t], af[r + 1, t]) for t in range(first, first + n)]
        for t in range(n):
            sf[r, :, pl.ds((first + t) * step, step)] = values[t]
        later = pltpu.roll(between(af[r, first - 1], af[r + 1, first - 1]), 2 * group, 1) if first else None
        keep(ab, 1, r, values, first + 1, True, later)

    def first_operand(r, first, n):
        pieces = []
        for kind, q in ((0, r), (1, r), (0, r + 1)):
            for early, back in ((0, 0), (1, 0), (0, 1)):
                lanes = slice((first + 1 - back) * step, (first + 1 - back + n) * step)
                hi, lo = ab[kind, early, q, 0, :, lanes], ab[kind, early, q, 1, :, lanes]
                pieces += [hi, lo, hi]
        return jnp.concatenate(pieces, axis=0)

    def second_operand(p, first, n):
        pieces = []
        for kind, q in ((0, p), (1, p), (0, p + 1)):
            for k in range(3):
                lanes = pl.ds(pl.multiple_of((2 - k + first) * step, step), n * step)
                hi, lo = mb[kind, q, 0, :, lanes], mb[kind, q, 1, :, lanes]
                pieces += [hi, lo, hi]
        return jnp.concatenate(pieces, axis=0)

    def layer_of(layer, right, base):
        total = jnp.dot(taps[layer], right, preferred_element_type=F32)
        pre = total + jnp.concatenate([tall[layer]] * (total.shape[1] // out_ch), axis=1)
        g = jnp.tanh(pre[:ch]) * (0.5 * jnp.tanh(0.5 * pre[ch:]) + 0.5)
        hi, lo = split(g)
        return base + jnp.dot(mix[layer], jnp.concatenate([hi, lo, hi], axis=0), preferred_element_type=F32)

    def middle(rows, first, n):
        value = layer_of(
            0,
            jnp.concatenate([first_operand(r, first, n) for r in rows], axis=1),
            jnp.concatenate([sf[r, :, first * step:(first + n) * step] for r in rows], axis=1),
        )
        for i, r in enumerate(rows):
            row = F * fib + 2 * r - 1
            ok = [((f >= 0) & (f < nf * fib)).astype(jnp.int32) for f in (row, row + 1)]
            inside = jnp.where(first_fibre, ok[0], ok[1]) == 1
            parts = [jnp.where(inside, value[:, t * step:(t + 1) * step], 0.0) for t in range(i * n, (i + 1) * n)]
            for t in range(n):
                mf[r, first + t] = parts[t]
            keep(mb, 0, r, parts, first + 2, False)

    def join(p, first, n):
        values = [between(mf[p, t], mf[p + 1, t]) for t in range(first, first + n)]
        keep(mb, 1, p, values, first + 2, False)
        for t in range(n):
            sf[p, :, pl.ds((first + t) * step, step)] = values[t]

    def blocks_of(p, first, n):
        return sf[p, :, pl.ds(pl.multiple_of(first * step, step), n * step)]

    def away(p, first):
        value = layer_of(1, second_operand(p, first, 2), blocks_of(p, first, 2))
        for t in range(2):
            fs[p, first + t] = value[:, t * step:(t + 1) * step]

    def home(ps):
        def half(n, carry):
            t = jnp.where(n == 0, partner, T)
            value = layer_of(
                1,
                jnp.concatenate([second_operand(p, t, 1) for p in ps], axis=1),
                jnp.concatenate([blocks_of(p, t, 1) for p in ps], axis=1),
            )
            parts = [value[:, i * step:(i + 1) * step] for i in range(len(ps))]

            @pl.when(n == 0)
            def _():
                for part, p in zip(parts, ps):
                    fs[p, partner] = part
                    feature_out(0, p).start()

            @pl.when(n == 1)
            def _():
                for part, p in zip(parts, ps):
                    fr[p, T] = part
            return carry

        lax.fori_loop(0, 2, half, 0)

    pairs = list(range(1, own + 2)) + [0]
    rows = [0] + list(range(1, own + 1)) + [0]
    outs = [0, 0] + list(range(1, own)) + [0]
    pairs_first = [1, 0] + list(range(2, own + 2))
    rows_first = [0, 0] + list(range(1, own + 1))
    outs_first = [0, 0] + list(range(own))

    def body(i, carry):
        q, r, p = (
            jnp.where(down, pick(i, usual), pick(i, first))
            for usual, first in ((pairs, pairs_first), (rows, rows_first), (outs, outs_first))
        )

        @pl.when((q >= 1) & (q <= own))
        def _():
            for k in (1, 2):
                signal_in(k, q).wait_recv()

        @pl.when((q == 1) & down)
        def _():
            halo_down(1).start()

        @pl.when((q == 3) & down)
        def _():
            for k in (1, 2):
                edge_up(k).wait_recv()
                relay_out(k).start()

        @pl.when((q == own + 1) & up)
        def _():
            for n in range(2):
                halo_down(n).wait_recv()

        @pl.when((q == 0) & down)
        def _():
            halo_up(0).wait_recv()
            for k in (1, 2):
                relay_in(k).wait_recv()

        inner_pair = (q >= 1) & (q <= own) & (chip == 0)
        inner_row = (r >= 1) & (r <= own - 1) & (chip == 0)

        @pl.when(inner_pair)
        def _():
            pair(q, 2, 2)

        @pl.when(jnp.logical_not(inner_pair))
        def _():
            pair(q, 0, nt)

        @pl.when((i >= 1) & inner_row)
        def _():
            across(r, 2, 2)
            middle([r], 2, 2)

        for where, blocks in ((jnp.logical_not(inner_row) & (chip == 0), nt), (chip == 2, 2)):
            @pl.when((i >= 1) & where)
            def _(blocks=blocks):
                across(r, 0, nt)
                middle([r], 0, blocks)

        for where, blocks, theirs in ((0, nt, 2), (2, 2, 0)):
            @pl.when((i >= 2) & (chip == where))
            def _(blocks=blocks, theirs=theirs):
                join(p, 0, blocks)
                away(p, theirs)

        @pl.when((i >= 2) & outer)
        def _():
            for k in (2, 1):
                feature_out(k, p).start()

        @pl.when((i >= 2) & jnp.logical_not(outer))
        def _():
            for k in (1, 2):
                feature_out(k, p).start()
        return carry

    outer = (T == 0) | (T == nt - 1)
    for q in range(2, own):
        signal_in(0, q).wait_recv()

    @pl.when(chip == 0)
    def _():
        def pairs_of_chip(n, carry):
            pair(n + 1, 0, 2)
            return carry

        def rows_of_chip(n, carry):
            across(n + 1, 0, 2)
            return carry

        lax.fori_loop(0, own, pairs_of_chip, 0)
        lax.fori_loop(0, own - 1, rows_of_chip, 0)
        middle(list(range(1, own)), 0, 2)

    lax.fori_loop(0, own + 2, body, 0)

    @pl.when(chip == 2)
    def _():
        middle(list(range(own + 1)), 2, 2)
        for p in range(own):
            join(p, 2, 2)

    home(list(range(own)))

    def finish(i, carry):
        p = jnp.where(down, lax.rem(i + 1, own), i)
        for k in range(3):
            feature_in(k, p).wait_recv()
        for n, value in enumerate(swap([fr[p, t] for t in range(nt)])):
            out_ref[pl.ds(n // 2 * fib + 2 * p + n % 2, ch, stride=fib * 2), :] = value
        return carry

    lax.fori_loop(0, own, finish, 0)

    for k in range(3):
        for q in range(1, own + 1):
            signal_out(k, q).wait_send()
            feature_out(k, q - 1).wait_send()
    @pl.when(up)
    def _():
        halo_up(0).wait_send()
        for k in (1, 2):
            edge_up(k).wait_send()

    @pl.when(down)
    def _():
        for n in range(2):
            halo_down(n).wait_send()
        for k in (1, 2):
            relay_out(k).wait_send()


def solution(mesh):
    nt, nf = mesh.shape["tm"], mesh.shape["fibre"]
    placed = (P(None, "fibre", "tm"), P(), P(), P(), P(), P(), P())

    def body(signal, w1, b1, r1, w2, b2, r2):
        ch, fib, length = signal.shape
        assert length == DILATION_TWO == 2 * DILATION_ONE and nt % 2 == 0 and fib == FIB_DEV
        x = signal.reshape(ch, fib, length // 128, 128).transpose(0, 2, 1, 3).reshape(-1, 128)
        out_ch = w1.shape[2]
        own = fib // 2
        w1, w2 = jnp.transpose(w1, (0, 1, 3, 2)), jnp.transpose(w2, (0, 1, 3, 2))
        b1 = b1.reshape(1, out_ch)
        b2 = b2.reshape(1, out_ch)
        dma = lambda n: pltpu.SemaphoreType.DMA((n,))
        inputs = [
            pltpu.VMEM(x.shape, F32),
            pltpu.VMEM(w1.shape, F32), pltpu.VMEM(b1.shape, F32), pltpu.VMEM(r1.shape, F32),
            pltpu.VMEM(w2.shape, F32), pltpu.VMEM(b2.shape, F32), pltpu.VMEM(r2.shape, F32),
            pltpu.VMEM((2, out_ch, 27 * ch), BF), pltpu.VMEM((2, ch, 3 * ch), BF),
            pltpu.VMEM((2, out_ch, out_ch), F32),
        ]
        step = DILATION_ONE
        if nt == 4:
            form = spread_kernel
            scratch = inputs + [
                pltpu.VMEM((nt, own, ch, step), F32), pltpu.VMEM((own + 2, nt, ch, step), F32),
                pltpu.VMEM((own + 1, ch, nt * step), F32),
                pltpu.VMEM((2, 2, own + 2, 2, ch, (nt + 1) * step), BF),
                pltpu.VMEM((own + 1, nt, ch, step), F32),
                pltpu.VMEM((2, own + 1, 2, ch, (nt + 2) * step), BF),
                pltpu.VMEM((own, nt, ch, step), F32), pltpu.VMEM((own, nt, ch, step), F32),
                pltpu.VMEM((2, ch, step), F32),
                dma(1), dma(6), dma(3 * own), dma(3 * own), dma(4), dma(4), dma(3 * own), dma(3 * own),
                dma(2), dma(2), dma(2), dma(2),
            ]
        else:
            form = kernel
            scratch = [
                pltpu.VMEM((2, 4, own + 2, ch, 2 * length), F32),
                pltpu.VMEM((2, own + 2, 4 * length // step, 2, ch, 2 * step), BF),
            ] + inputs + [
                dma(1), dma(6), dma(2), dma(2), dma(2), dma(2), dma(own + 2), dma(own + 2),
                dma(own + 2), dma(own + 2), dma(own + 2), dma(own + 2),
                dma(own + 1), dma(own + 1), dma(3), dma(3),
                pltpu.SemaphoreType.REGULAR,
            ]
        out = pl.pallas_call(
            lambda *refs: form(nt, nf, fib, *refs),
            name="gated_layers",
            out_shape=pltpu.VMEM(x.shape, F32),
            in_specs=[pl.BlockSpec(memory_space=pl.ANY)] * 7,
            out_specs=pl.BlockSpec(memory_space=pltpu.VMEM),
            scratch_shapes=scratch,
            compiler_params=pltpu.CompilerParams(
                collective_id=0, has_side_effects=True, vmem_limit_bytes=60 * 1024 * 1024
            ),
        )(x, w1, b1, r1, w2, b2, r2)
        out = out.reshape(ch, length // 128, fib, 128).transpose(0, 2, 1, 3)
        return out.reshape(ch, fib, length)

    return jax.shard_map(body, mesh=mesh, in_specs=placed, out_specs=P(None, "fibre", "tm"), check_vma=False)
```
